32 devices in a mesh: context: 4 (over z), dp: 4 (over y, x), tensor: 2 (over core).
Axes of the slice: x: 2, y: 2, z: 4, core: 2. Of those that a mesh axis runs over, the one named last changes fastest.
Arguments:
- ssm_input: bfloat16 [4096, 4096], P(('dp', 'context'), 'tensor'), parts along dimension 0, may hold values from -6 to 6
- input_map: bfloat16 [4096, 128], P(('dp', 'context')), parts along dimension 0, may hold values from -0.119628906 to 0.119628906
- output_map: bfloat16 [4096, 128], P(('dp', 'context')), parts along dimension 0, may hold values from -6 to 6
- step_size: float32 [64, 4096], P('tensor', ('dp', 'context')), parts along dimension 1, may hold values from 0.25 to 1
- log_decay: float32 [64, 4096], P('tensor', ('dp', 'context')), parts along dimension 1, may hold values from -1.6 to 0
- skip_gain: float32 [64], P('tensor'), may hold values from 0.5 to 1.5
- norm_gain: float32 [4096], P('tensor'), may hold values from 0.5 to 1.5
- query_weight: bfloat16 [4096, 4096], P('tensor'), may hold values from -0.09375 to 0.09375
- key_states: bfloat16 [4096, 1024], P(('dp', 'context'), 'tensor'), parts along dimension 0, may hold values from -140 to 140
- value_states: bfloat16 [4096, 1024], P(('dp', 'context'), 'tensor'), parts along dimension 0, may hold values from -6 to 6
- block_mask: int32 [32, 8], P('dp'), parts along dimension 0, may hold values 0 or 1
Outputs:
- mixer_out: bfloat16 [4096, 4096], P(('dp', 'context'), 'tensor'), parts along dimension 0
- attended: bfloat16 [4096, 4096], P(('dp', 'context'), 'tensor'), parts along dimension 0
The draws below stay inside these ranges and needn't reach their ends.
There are 4 independent parts, one for each index of `dp`. The reference program is written for one: setup_inputs(seed, part) draws one part's arguments, and reference() takes and returns one part's arrays. A program takes and returns all parts, laid end to end along the dimension named above; an argument that names none is the same for every part. Nothing has to cross between parts.
All inputs are finite; a program needn't handle non-finite values.
Results may differ from the reference program's by a relative error of at most 0.0045.
The reference program's roundings to bfloat16 on the way count: a program that leaves them out, or rounds other values in their place, can miss the bound.
Values may be sent and summed in bfloat16 or wider, within the bound.
A program may use at most 128 MiB of HBM per device.

```python
import math
import jax
import jax.numpy as jnp
from jax import lax

TOK_DEV = 256
SSM_HEADS = 64
HEAD_P = 64
STATE = 128
SPAN = 64
Q_HEADS = 32
KV_HEADS = 8
HEAD_DIM = 128
BLOCK = 128
SEQUENCE_TOKENS = 1024
INNER = 4096
NBLK = 8


def draw_log_decay(key, part):
    stream = jax.random.fold_in(key, 11)
    k_pick, k_slow, k_fast, k_device, k_token, key_positions, key_penalty = jax.random.split(stream, 7)
    share = 0.5
    slow_pick = jax.random.uniform(k_pick, (SSM_HEADS,)) < share
    slow_rate = jnp.exp(jax.random.uniform(k_slow, (SSM_HEADS,), minval=math.log(0.02), maxval=math.log(0.5))) / SEQUENCE_TOKENS
    fast_rate = jnp.exp(jax.random.uniform(k_fast, (SSM_HEADS,), minval=math.log(0.02), maxval=math.log(0.05)))
    head_decay_rate = jnp.where(slow_pick, slow_rate, fast_rate)
    device_factor = jnp.exp(jax.random.uniform(k_device, (SEQUENCE_TOKENS // TOK_DEV,), minval=math.log(0.5), maxval=math.log(2.0)))
    token_multiplier = jnp.exp(jax.random.uniform(k_token, (SSM_HEADS, SEQUENCE_TOKENS), minval=math.log(0.5), maxval=math.log(2.0)))
    dispersion_factor = jnp.repeat(device_factor, TOK_DEV)
    surge_positions = jax.random.randint(key_positions, (2,), 0, SEQUENCE_TOKENS)
    surge_penalty = jax.random.uniform(key_penalty, (2,), minval=0.2, maxval=0.5)
    match_lookup = jnp.arange(SEQUENCE_TOKENS)[:, None] == surge_positions[None, :]
    surge_magnitude = jnp.sum(jnp.where(match_lookup, -jnp.log(1.0 - surge_penalty)[None, :], 0.0), axis=1)
    return -(head_decay_rate[:, None] * dispersion_factor[None, :] * token_multiplier) - surge_magnitude[None, :]


def draw_key_states(key, part):
    stream = jax.random.fold_in(key, 23)
    k_base = jax.random.fold_in(stream, 0)
    shape = (SEQUENCE_TOKENS, KV_HEADS * HEAD_DIM)
    return jnp.clip(jax.random.normal(k_base, shape), -4.0, 4.0).astype(jnp.bfloat16)


def with_ends(result, own_key, smallest, high):
    spot = [jax.random.randint(jax.random.fold_in(own_key, axis), (), 0, length) for axis, length in enumerate(result.shape)]
    main_axis = result.shape.index(max(result.shape))
    next_to = spot[:main_axis] + [(spot[main_axis] + 1) % result.shape[main_axis]] + spot[main_axis + 1:]
    return result.at[tuple(spot)].set(smallest).at[tuple(next_to)].set(high)


def steps_of(stream_key, dims, shards, smallest, largest):
    def one(axis_at, shards_of):
        draws = jax.random.uniform(jax.random.fold_in(jax.random.fold_in(stream_key, 6), axis_at), (shards_of,), jnp.float32, smallest / len(shards), largest / len(shards))
        return jnp.repeat(jnp.exp(draws), dims[axis_at] // shards_of).reshape((-1,) + (1,) * (len(dims) - axis_at - 1))

    factor_of = one(*shards[0])
    for cut in shards[1:]:
        factor_of = factor_of * one(*cut)
    return factor_of


def centred(own_key, dims, spread, limit, cuts=(), held_as=jnp.bfloat16):
    entries = jax.random.normal(own_key, dims, jnp.float32) * spread
    if len(cuts) > 0:
        entries = steps_of(own_key, dims, cuts, -0.22, 0.18) * entries
    return jnp.clip(entries, min=-limit, max=limit).astype(held_as)


def setup_inputs(seed: int = 0, part: int = 0) -> dict:
    keys = jax.random.split(jax.random.key(seed), 12)
    part_keys = jax.random.split(jax.random.fold_in(keys[11], part), 12)
    ssm_input = centred(part_keys[0], (SEQUENCE_TOKENS, INNER), 1.0, 6.0, ((0, 4), (1, 2)))
    input_map = centred(part_keys[1], (SEQUENCE_TOKENS, STATE), 0.02, 0.119628906, ((0, 4),))
    output_map = centred(part_keys[2], (SEQUENCE_TOKENS, STATE), 1.0, 6.0, ((0, 4),))
    step_size = jnp.clip(jnp.exp(math.log(1.0) - 1.3862944 * jax.random.uniform(part_keys[3], (SSM_HEADS, SEQUENCE_TOKENS), jnp.float32) ** steps_of(part_keys[3], (SSM_HEADS, SEQUENCE_TOKENS), ((0, 2), (1, 4)), -0.2, 0.2)), 0.25, 1.0)
    log_decay = draw_log_decay(jax.random.fold_in(jax.random.fold_in(keys[11], part), 71), part)
    skip_gain = jnp.clip(0.5 + 1.0 * jax.random.uniform(keys[5], (SSM_HEADS,), jnp.float32) ** steps_of(keys[5], (SSM_HEADS,), ((0, 2),), -0.2, 0.2), 0.5, 1.5)
    norm_gain = jnp.clip(0.5 + 1.0 * jax.random.uniform(keys[6], (INNER,), jnp.float32) ** steps_of(keys[6], (INNER,), ((0, 2),), -0.2, 0.2), 0.5, 1.5)
    query_weight = centred(keys[7], (INNER, Q_HEADS * HEAD_DIM), INNER ** -0.5, 0.09375, ((0, 2),))
    key_states = draw_key_states(jax.random.fold_in(jax.random.fold_in(keys[11], part), 71), part)
    value_states = centred(part_keys[9], (SEQUENCE_TOKENS, KV_HEADS * HEAD_DIM), 1.0, 6.0, ((0, 4), (1, 2)))
    block_mask = with_ends((jax.random.randint(part_keys[10], (NBLK, NBLK), 0, 2) < 1).astype(jnp.int32), jax.random.fold_in(part_keys[10], 1), 0, 1)
    return {"ssm_input": ssm_input, "input_map": input_map, "output_map": output_map, "step_size": step_size, "log_decay": log_decay, "skip_gain": skip_gain, "norm_gain": norm_gain, "query_weight": query_weight, "key_states": key_states, "value_states": value_states, "block_mask": block_mask}


HIGHEST = lax.Precision.HIGHEST
NEGATIVE = -1e+30

def span_pass(carried, pieces):
    inputs, in_narrow, out_narrow, step_sizes, decays = pieces
    in_wide = in_narrow.astype(jnp.float32)
    out_wide = out_narrow.astype(jnp.float32)
    running = jnp.cumsum(decays, axis=1)
    length = decays.shape[1]
    row_index = lax.broadcasted_iota(jnp.int32, (length, length), 0)
    col_index = lax.broadcasted_iota(jnp.int32, (length, length), 1)
    causal = (row_index >= col_index)[None]
    spread_log = running[:, :, None] - running[:, None, :]
    retain = jnp.where(causal, jnp.exp(jnp.where(causal, spread_log, 0.0)), 0.0)
    intersection = jnp.dot(out_narrow, in_narrow.T, preferred_element_type=jnp.float32)
    weights = intersection[None] * retain * step_sizes[:, None, :]
    y_intra = jnp.einsum('hij,jhp->ihp', weights, inputs, precision=HIGHEST)
    y_inter = jnp.einsum('in,hpn->ihp', out_wide, carried, precision=HIGHEST) * jnp.exp(running).T[:, :, None]
    to_end = jnp.exp(running[:, -1:] - running) * step_sizes
    injected = jnp.einsum('hj,jhp,jn->hpn', to_end, inputs, in_wide, precision=HIGHEST)
    carried = jnp.exp(running[:, -1])[:, None, None] * carried + injected
    return (carried, y_intra + y_inter)

def reference(ssm_input, input_map, output_map, step_size, log_decay, skip_gain, norm_gain, query_weight, key_states, value_states, block_mask):
    length = ssm_input.shape[0]
    span_count = length // SPAN
    inputs = ssm_input.astype(jnp.float32).reshape(length, SSM_HEADS, HEAD_P)
    pieces = (inputs.reshape(span_count, SPAN, SSM_HEADS, HEAD_P), input_map.reshape(span_count, SPAN, STATE), output_map.reshape(span_count, SPAN, STATE), step_size.reshape(SSM_HEADS, span_count, SPAN).transpose(1, 0, 2), log_decay.reshape(SSM_HEADS, span_count, SPAN).transpose(1, 0, 2))
    start_state = jnp.zeros((SSM_HEADS, HEAD_P, STATE), jnp.float32)
    final_state, outputs = lax.scan(span_pass, start_state, pieces)
    scan_out = outputs.reshape(length, SSM_HEADS, HEAD_P) + skip_gain[None, :, None] * inputs
    squares = lax.optimization_barrier(jnp.mean(scan_out * scan_out, axis=-1, keepdims=True))
    normed = scan_out * lax.rsqrt(squares + 1e-05) * norm_gain.reshape(SSM_HEADS, HEAD_P)
    mixer_out = normed.reshape(length, INNER).astype(jnp.bfloat16)
    query = jnp.dot(mixer_out, query_weight, preferred_element_type=jnp.float32).astype(jnp.bfloat16)
    positions = jnp.arange(length, dtype=jnp.int32)
    block_of = positions // BLOCK
    table = block_mask[block_of][:, block_of]
    allowed = (positions[None, :] <= positions[:, None]) & ((table == 1) | (block_of[:, None] == block_of[None, :]))
    group_size = Q_HEADS // KV_HEADS
    score_scale = HEAD_DIM ** (-0.5)

    def one_head(head_index):
        kv_index = head_index // group_size
        q_head = lax.dynamic_slice_in_dim(query, head_index * HEAD_DIM, HEAD_DIM, 1)
        k_head = lax.dynamic_slice_in_dim(key_states, kv_index * HEAD_DIM, HEAD_DIM, 1)
        v_head = lax.dynamic_slice_in_dim(value_states, kv_index * HEAD_DIM, HEAD_DIM, 1)
        scores = jnp.dot(q_head, k_head.T, preferred_element_type=jnp.float32) * score_scale
        scores = jnp.where(allowed, scores, NEGATIVE)
        row_top = lax.optimization_barrier(jnp.max(scores, axis=1, keepdims=True))
        expo_terms = jnp.where(allowed, jnp.exp(scores - row_top), 0.0)
        denominator = lax.optimization_barrier(jnp.sum(expo_terms, axis=1, keepdims=True))
        summed = jnp.dot(expo_terms.astype(jnp.bfloat16), v_head, preferred_element_type=jnp.float32)
        return (summed / denominator).astype(jnp.bfloat16)
    head_outputs = lax.map(one_head, jnp.arange(Q_HEADS, dtype=jnp.int32))
    attended = head_outputs.transpose(1, 0, 2).reshape(length, Q_HEADS * HEAD_DIM)
    return (mixer_out, attended)
```

```python
import functools

import jax
import jax.numpy as jnp
from jax import lax
from jax.experimental import pallas as pl
from jax.experimental.pallas import tpu as pltpu
from jax.sharding import PartitionSpec as P

HEAD_P = 64
STATE = 128
HEAD_DIM = 128
BLOCK = 128
CHUNK = 256
NEGATIVE = -1e30
LOG2E = 1.4426950408889634
LEVELS = 524287.0
MESH = pl.DeviceIdType.MESH
F32 = jnp.float32
BF16 = jnp.bfloat16
NT = (((1,), (1,)), ((), ()))


def split(wide):
    high = wide.astype(BF16)
    rest = wide - high.astype(F32)
    middle = rest.astype(BF16)
    return high, middle, (rest - middle.astype(F32)).astype(BF16)


def dot(a, b):
    return jnp.dot(a, b, preferred_element_type=F32)


def dot_left(wide, narrow):
    high, middle, low = split(wide)
    return dot(high, narrow) + (dot(middle, narrow) + dot(low, narrow))


def dot_right(narrow, wide):
    high, middle, low = split(wide)
    return dot(narrow, high) + (dot(narrow, middle) + dot(narrow, low))


def encode(wide):
    largest = jnp.maximum(jnp.max(jnp.abs(wide), axis=0, keepdims=True), 1e-30)
    whole = jnp.round(wide * (LEVELS / largest)).astype(jnp.int32)
    quarter = wide.shape[0] // 4
    low = whole & 15
    packed = low[:quarter]
    for i in range(1, 4):
        packed = packed | (low[i * quarter : (i + 1) * quarter] << (4 * i))
    return (whole >> 4).astype(jnp.int16), (packed - 32768).astype(jnp.int16), largest * (1.0 / LEVELS)


def decode(high, packed, scale):
    packed = packed.astype(jnp.int32) + 32768
    low = jnp.concatenate([(packed >> (4 * i)) & 15 for i in range(4)], axis=0)
    return (high.astype(jnp.int32) * 16 + low).astype(F32) * scale


def kernel(
    n,
    mask_ref,
    skip_ref,
    x_hbm,
    b_hbm,
    c_hbm,
    dt_hbm,
    ld_hbm,
    gain_hbm,
    w_ref,
    k_hbm,
    v_hbm,
    mixer_hbm,
    attended_hbm,
    mixer_ref,
    attended_ref,
    x_ref,
    b_ref,
    c_ref,
    dt_ref,
    ld_ref,
    gain_ref,
    kv,
    w_own,
    w_other,
    bt,
    gram,
    rows_run,
    cols_run,
    rows_adj,
    code,
    code_in,
    scale,
    scale_in,
    mixed_other,
    q_acc,
    q_all,
    bias,
    weights,
    top,
    total,
    acc,
    ld_sem,
    own_sem,
    kv_send,
    kv_recv,
    st_send,
    st_recv,
    sc_send,
    sc_recv,
    mx_send,
    mx_recv,
    wt_send,
    wt_recv,
    wt_own,
    mx_out,
    at_out,
):
    me = lax.axis_index("context")
    core = lax.axis_index("tensor")
    other = 1 - core
    length = x_ref.shape[0]
    half = length // 2
    chunks = x_ref.shape[1] // CHUNK
    per = CHUNK // HEAD_P
    pairs = CHUNK // 128
    q_cols = w_own.shape[2]
    has_left = me > 0
    has_right = me < n - 1
    middle = has_left & has_right
    heads = q_cols // HEAD_DIM
    groups = kv.shape[2]
    members = heads // groups
    blocks = length // BLOCK

    barrier = pltpu.get_barrier_semaphore()
    pl.semaphore_signal(barrier, inc=1, device_id={"tensor": other}, device_id_type=MESH)

    @pl.when(has_left)
    def _():
        pl.semaphore_signal(barrier, inc=1, device_id={"context": me - 1}, device_id_type=MESH)

    @pl.when(has_right)
    def _():
        pl.semaphore_signal(barrier, inc=1, device_id={"context": me + 1}, device_id_type=MESH)

    loads = [
        pltpu.make_async_copy(src, dst, ld_sem.at[i])
        for i, (src, dst) in enumerate(
            (
                (ld_hbm, ld_ref),
                (dt_hbm, dt_ref),
                (b_hbm, b_ref),
                (c_hbm, c_ref),
                (x_hbm, x_ref),
                (gain_hbm, gain_ref),
            )
        )
    ]
    for load in loads:
        load.start()

    hbm = (k_hbm, v_hbm)

    def fixed_lanes(g):
        return pl.ds(g * HEAD_DIM, HEAD_DIM)

    def own_load(which, g):
        return pltpu.make_async_copy(hbm[which].at[:, fixed_lanes(g)], kv.at[which, 0, g], own_sem.at[which, g])

    for which in range(2):
        for g in range(groups):
            own_load(which, g).start()

    peers = 1 + has_left.astype(jnp.int32) + has_right.astype(jnp.int32)
    pl.semaphore_wait(barrier, peers)

    def pass_own(which, g):
        return pltpu.make_async_remote_copy(
            src_ref=hbm[which].at[:, fixed_lanes(g)],
            dst_ref=kv.at[which, 1, g],
            send_sem=kv_send.at[which, 0, g],
            recv_sem=kv_recv.at[which, 1, g],
            device_id={"context": me + 1},
            device_id_type=MESH,
        )

    def pass_on(which, slot, g):
        return pltpu.make_async_remote_copy(
            src_ref=kv.at[which, slot, g],
            dst_ref=kv.at[which, slot + 1, g],
            send_sem=kv_send.at[which, slot, g],
            recv_sem=kv_recv.at[which, slot + 1, g],
            device_id={"context": me + 1},
            device_id_type=MESH,
        )

    def arrive(which, slot, g):
        pltpu.make_async_remote_copy(
            src_ref=kv.at[which, slot - 1, g],
            dst_ref=kv.at[which, slot, g],
            send_sem=kv_send.at[which, slot - 1, g],
            recv_sem=kv_recv.at[which, slot, g],
            device_id={"context": me - 1},
            device_id_type=MESH,
        ).wait_recv()

    def forward(which, slot, g):
        arrive(which, slot, g)
        pass_on(which, slot, g).start()

    def state_copies(j):
        return [
            pltpu.make_async_remote_copy(
                src_ref=src.at[j],
                dst_ref=dst.at[j],
                send_sem=send.at[j],
                recv_sem=recv.at[j],
                device_id={"context": me + 1},
                device_id_type=MESH,
            )
            for src, dst, send, recv in ((scale, scale_in, sc_send, sc_recv), (code, code_in, st_send, st_recv))
        ]

    def lanes_of(j):
        return pl.ds(pl.multiple_of(j * CHUNK, CHUNK), CHUNK)

    def mixed_copy(j):
        return pltpu.make_async_remote_copy(
            src_ref=mixer_ref.at[:, lanes_of(j)],
            dst_ref=mixed_other.at[j],
            send_sem=mx_send.at[j],
            recv_sem=mx_recv.at[j],
            device_id={"tensor": other},
            device_id_type=MESH,
        )

    def mixed_out(j):
        return pltpu.make_async_copy(mixer_ref.at[:, lanes_of(j)], mixer_hbm.at[:, lanes_of(j)], mx_out.at[j])

    def attended_out(g):
        lanes = pl.ds(pl.multiple_of(g * members * HEAD_DIM, HEAD_DIM), members * HEAD_DIM)
        return pltpu.make_async_copy(attended_ref.at[:, lanes], attended_hbm.at[:, lanes], at_out.at[g])

    def weight_out(j):
        return pltpu.make_async_remote_copy(
            src_ref=w_ref.at[lanes_of(j), pl.ds(pl.multiple_of(other * q_cols, CHUNK), q_cols)],
            dst_ref=w_other.at[j],
            send_sem=wt_send.at[j],
            recv_sem=wt_recv.at[j],
            device_id={"tensor": other},
            device_id_type=MESH,
        )

    def weight_in(j):
        return pltpu.make_async_copy(
            w_ref.at[lanes_of(j), pl.ds(pl.multiple_of(core * q_cols, CHUNK), q_cols)],
            w_own.at[j],
            wt_own.at[j],
        )

    @pl.when(has_right)
    def _():
        for g in range(groups):

            @pl.when(has_left | (g < groups // 2))
            def _(g=g):
                pass_own(0, g).start()

    @pl.loop(0, chunks)
    def _(j):
        weight_in(j).start()
        weight_out(j).start()

    row = lax.broadcasted_iota(jnp.int32, (length, length), 0)
    col = lax.broadcasted_iota(jnp.int32, (length, length), 1)
    same = (row // BLOCK) == (col // BLOCK)
    loads[0].wait()
    loads[1].wait()
    up_to = jnp.where((row <= col) & ((row // half) == (col // half)), 1.0, 0.0).astype(BF16)
    run = dot_left(ld_ref[...], up_to) * LOG2E
    ends = jnp.concatenate(
        [
            jnp.broadcast_to(run[:, half - 1 : half], (run.shape[0], half)),
            jnp.broadcast_to(run[:, length - 1 : length], (run.shape[0], half)),
        ],
        axis=1,
    )
    steps = dt_ref[...]
    grow = jnp.exp2(run)
    inject = jnp.exp2(ends - run) * steps
    adjusted = run - jnp.log(steps) * LOG2E
    for j in range(chunks):
        part = slice(j * per, (j + 1) * per)
        rows_run[j, 0:per, :] = run[part]
        rows_run[j, per : 2 * per, :] = grow[part]
        rows_run[j, 2 * per : 3 * per, :] = inject[part]
        rows_run[j, 3 * per : 4 * per, :] = inject[part]
        rows_adj[j] = adjusted[part]
    for j in range(chunks):
        cols_run[j] = jnp.transpose(rows_run[j])
    loads[2].wait()
    loads[3].wait()
    bt[...] = jnp.transpose(b_ref[...].astype(F32)).astype(BF16)
    for s in range(2):
        part = slice(s * half, (s + 1) * half)
        gram[s] = jnp.where(
            row[:half, :half] >= col[:half, :half],
            lax.dot_general(c_ref[part, :], b_ref[part, :], NT, preferred_element_type=F32),
            0.0,
        )
    first = lax.broadcasted_iota(jnp.int32, (1, 128), 1) < HEAD_P
    loads[4].wait()
    loads[5].wait()

    def spread(table, at):
        return jnp.concatenate(
            [
                jnp.where(first, table[:, at + 2 * p : at + 2 * p + 1], table[:, at + 2 * p + 1 : at + 2 * p + 2])
                for p in range(pairs)
            ],
            axis=1,
        )

    def own_part(j, s):
        return jnp.concatenate([top[pairs * j + p, s * half : (s + 1) * half, :] for p in range(pairs)], axis=1)

    def send_state(j, entering):
        keep = spread(cols_run[j, length - 1 : length, :], per)
        high, packed, unit = encode(keep * entering + own_part(j, 1))
        code[j, 0:STATE, :] = high
        code[j, STATE : STATE + STATE // 4, :] = packed
        scale[j] = unit
        for copy in state_copies(j):
            copy.start()

    @pl.loop(0, chunks)
    def _(j):
        weighted = x_ref[:, lanes_of(j)].astype(F32) * spread(cols_run[j], 2 * per)

        def keep_part(s):
            part = dot_right(bt[:, s * half : (s + 1) * half], weighted[s * half : (s + 1) * half])
            for p in range(pairs):
                top[pairs * j + p, s * half : (s + 1) * half, :] = part[:, p * 128 : (p + 1) * 128]

        keep_part(0)

        @pl.when(has_right)
        def _():
            keep_part(1)

        @pl.when(~has_left & has_right)
        def _():
            send_state(j, own_part(j, 0))

    @pl.when(~has_left & has_right)
    def _():
        for g in range(groups // 2, groups):
            pass_own(0, g).start()
        for g in range(groups):
            pass_own(1, g).start()

    def inside(j):
        runs = cols_run[j]
        adj = rows_adj[j]
        for p in range(pairs):
            lanes = pl.ds(pl.multiple_of(j * CHUNK + p * 128, 128), 128)
            for s in range(2):
                part = slice(s * half, (s + 1) * half)
                x_own = x_ref[part, lanes]
                x_wide = x_own.astype(F32)
                pieces = []
                for m in range(2):
                    a = 2 * p + m
                    weight = gram[s] * jnp.exp2(jnp.minimum(runs[part, a : a + 1] - adj[a : a + 1, part], 0.0))
                    pieces.append(split(weight))
                both = jnp.concatenate(
                    [
                        jnp.where(first, x_wide, 0.0).astype(BF16),
                        jnp.where(first, 0.0, x_wide).astype(BF16),
                    ],
                    axis=0,
                )
                high, mid, low = (jnp.concatenate([pieces[0][i], pieces[1][i]], axis=1) for i in range(3))
                gain = jnp.where(first, skip_ref[j * per + 2 * p], skip_ref[j * per + 2 * p + 1])
                acc[pairs * j + p, part, :] = (dot(high, both) + (dot(mid, both) + dot(low, both))) + gain * x_wide

    for slot in range(n):

        @pl.when(slot <= me)
        def _(slot=slot):
            for i in range(blocks):
                for m in range(blocks):
                    seen = mask_ref[me * blocks + i, (me - slot) * blocks + m] == 1
                    bias[slot, i * BLOCK : (i + 1) * BLOCK, m * BLOCK : (m + 1) * BLOCK] = jnp.full(
                        (BLOCK, BLOCK), jnp.where(seen, 0.0, NEGATIVE), F32
                    )

    bias[0] = jnp.where(row >= col, jnp.where(same, 0.0, bias[0]), NEGATIVE)
    q_acc[...] = jnp.zeros_like(q_acc)
    total[...] = jnp.zeros_like(total)

    @pl.when((me >= 2) & has_right)
    def _():
        for g in range(groups):
            forward(0, 1, g)

    ahead = jnp.where(has_right, jnp.minimum(me, 2), chunks)

    @pl.loop(0, ahead)
    def _(j):
        inside(j)

    def add_query(j):
        for t in range(0, q_cols, 512):
            q_acc[:, t : t + 512] += dot(mixer_ref[:, lanes_of(j)], w_own[j, :, t : t + 512])

    def add_other(j):
        mixed_copy(j).wait_recv()
        weight_out(j).wait_recv()
        for t in range(0, q_cols, 512):
            q_acc[:, t : t + 512] += dot(mixed_other[j], w_other[j, :, t : t + 512])

    @pl.when(~has_left)
    def _():
        code_in[...] = jnp.zeros_like(code_in)
        scale_in[...] = jnp.zeros_like(scale_in)

    second = me == 1
    later = (me >= 2) & has_right

    @pl.loop(0, chunks)
    def _(j):
        @pl.when(has_left)
        def _():
            for copy in state_copies(j):
                copy.wait_recv()

        arrived = decode(code_in[j, 0:STATE, :], code_in[j, STATE : STATE + STATE // 4, :], scale_in[j])
        entering = spread(cols_run[j, half - 1 : half, :], per) * arrived + own_part(j, 0)

        @pl.when(middle)
        def _():
            send_state(j, entering)

        for g in range(groups):
            for role, at in ((second, (1, 2, chunks - 2, chunks - 1)[g]), (later, (2, 3, chunks - 1, chunks)[g])):

                @pl.when(role & (j == at))
                def _(g=g, role=role):
                    if role is second:
                        forward(0, 1, g)
                    else:

                        @pl.when(me >= 2)
                        def _():
                            forward(0, 2, g)

            @pl.when(second & has_right & (j == (0, 3, 4, 5)[g]))
            def _(g=g):
                pass_own(1, g).start()

        @pl.when(j >= ahead)
        def _():
            inside(j)

        runs = cols_run[j]
        for s in range(2):
            part = slice(s * half, (s + 1) * half)
            carried = dot_right(c_ref[part, :], arrived if s == 0 else entering)
            grown = spread(runs[part], per)
            for p in range(pairs):
                lanes = slice(p * 128, (p + 1) * 128)
                out_lanes = pl.ds(pl.multiple_of(j * CHUNK + p * 128, 128), 128)
                y = acc[pairs * j + p, part, :] + carried[:, lanes] * grown[:, lanes]
                squares = y * y
                left = jnp.sum(jnp.where(first, squares, 0.0), axis=1, keepdims=True)
                right = jnp.sum(jnp.where(first, 0.0, squares), axis=1, keepdims=True)
                mean = jnp.where(first, left, right) * (1.0 / HEAD_P)
                mixer_ref[part, out_lanes] = (y * lax.rsqrt(mean + 1e-05) * gain_ref[:, out_lanes]).astype(BF16)
        mixed_copy(j).start()
        mixed_out(j).start()
        weight_in(j).wait()
        add_query(j)

        @pl.when(j >= 1)
        def _():
            add_other(j - 1)

    @pl.when(later)
    def _():
        forward(0, 2, groups - 1)

        @pl.loop(3, n)
        def _(slot):
            @pl.when(slot <= me)
            def _():
                for g in range(groups):
                    forward(0, slot, g)

        for g in range(groups):
            pass_own(1, g).start()
        for g in range(groups):
            forward(1, 1, g)

    @pl.when(second & has_right)
    def _():
        for g in range(groups):
            forward(1, 1, g)

    add_other(chunks - 1)
    for h in range(heads):
        q_all[h] = q_acc[:, h * HEAD_DIM : (h + 1) * HEAD_DIM].astype(BF16)
    for which in range(2):
        for g in range(groups):
            own_load(which, g).wait()
    unit = HEAD_DIM ** (-0.5) * LOG2E

    def head_lanes(h):
        return pl.ds(pl.multiple_of(h * HEAD_DIM, HEAD_DIM), HEAD_DIM)

    def scores_of(slot, h, keys):
        return lax.dot_general(q_all[h], keys, NT, preferred_element_type=F32) + bias[slot]

    @pl.loop(0, n)
    def _(slot):
        @pl.when(slot <= me)
        def _():
            @pl.loop(0, groups)
            def _(g):
                @pl.when(~has_right & (slot >= 1))
                def _():
                    arrive(0, slot, g)

                keys = kv[0, slot, g]
                for member in range(members):
                    h = g * members + member
                    scores = scores_of(slot, h, keys)
                    best = jnp.where(slot == 0, NEGATIVE, top[h])
                    for t in range(0, length, 128):
                        best = jnp.maximum(best, scores[:, t : t + 128])
                    top[h] = best

    @pl.when(later)
    def _():
        @pl.loop(2, n)
        def _(slot):
            @pl.when(slot <= me)
            def _():
                for g in range(groups):
                    forward(1, slot, g)

    @pl.loop(0, heads)
    def _(h):
        top[h] = jnp.broadcast_to(jnp.max(top[h], axis=1, keepdims=True), top.shape[1:])

    @pl.loop(0, n)
    def _(slot):
        @pl.when(slot <= me)
        def _():
            @pl.loop(0, groups)
            def _(g):
                keys = kv[0, slot, g]
                for member in range(members):
                    h = g * members + member
                    scores = scores_of(slot, h, keys)
                    best = top[h]
                    summed = total[h]
                    for t in range(0, length, 128):
                        part = jnp.exp2((scores[:, t : t + 128] - best) * unit)
                        summed = summed + part
                        weights[h, :, t : t + 128] = part.astype(BF16)
                    total[h] = summed

            @pl.loop(0, groups)
            def _(g):
                @pl.when(~has_right & (slot >= 1))
                def _():
                    arrive(1, slot, g)

                values = kv[1, slot, g]
                for member in range(members):
                    h = g * members + member
                    sum_ = jnp.where(slot == 0, 0.0, acc[h]) + dot(weights[h], values)
                    acc[h] = sum_

                    @pl.when(slot == me)
                    def _(h=h, sum_=sum_):
                        attended_ref[:, head_lanes(h)] = (
                            sum_ / jnp.sum(total[h], axis=1, keepdims=True)
                        ).astype(BF16)

                @pl.when(slot == me)
                def _():
                    attended_out(g).start()

    @pl.loop(0, groups)
    def _(g):
        attended_out(g).wait()

    @pl.loop(0, chunks)
    def _(j):
        mixed_copy(j).wait_send()
        mixed_out(j).wait()
        weight_out(j).wait_send()

        @pl.when(has_right)
        def _():
            for copy in state_copies(j):
                copy.wait_send()

    @pl.loop(0, n)
    def _(slot):
        @pl.when((slot <= me) & has_right)
        def _():
            for which in range(2):
                for g in range(groups):
                    pass_on(which, slot, g).wait_send()


def hand_on(mixer_ref, attended_ref, mixer_out, attended_out, sems):
    parts = sems.shape[1]
    rows = mixer_ref.shape[0] // parts
    copies = [
        pltpu.make_async_copy(src.at[pl.ds(i * rows, rows)], dst.at[pl.ds(i * rows, rows)], sems.at[k, i])
        for k, (src, dst) in enumerate(((mixer_ref, mixer_out), (attended_ref, attended_out)))
        for i in range(parts)
    ]
    for copy in copies:
        copy.start()
    for copy in copies:
        copy.wait()


def on_device(
    ssm_input,
    input_map,
    output_map,
    step_size,
    log_decay,
    skip_gain,
    norm_gain,
    query_weight,
    key_states,
    value_states,
    block_mask,
):
    n = lax.axis_size("context")
    length, channels = ssm_input.shape
    q_cols = query_weight.shape[1] // lax.axis_size("tensor")
    chunks = channels // CHUNK
    heads = q_cols // HEAD_DIM
    per = CHUNK // HEAD_P
    groups = key_states.shape[1] // HEAD_DIM
    smem = pl.BlockSpec(memory_space=pltpu.SMEM)
    hbm = pl.BlockSpec(memory_space=pltpu.HBM)
    far = pl.BlockSpec(memory_space=pl.ANY)
    dma = pltpu.SemaphoreType.DMA
    outs = (
        jax.ShapeDtypeStruct((length, channels), BF16),
        jax.ShapeDtypeStruct((length, q_cols), BF16),
    )
    coded = STATE + STATE // 4
    results = pl.pallas_call(
        functools.partial(kernel, n),
        out_shape=outs,
        in_specs=[smem, smem] + [hbm] * 9,
        out_specs=(hbm, hbm),
        scratch_shapes=[
            pltpu.VMEM((length, channels), BF16),
            pltpu.VMEM((length, q_cols), BF16),
            pltpu.VMEM((length, channels), BF16),
            pltpu.VMEM((length, STATE), BF16),
            pltpu.VMEM((length, STATE), BF16),
            pltpu.VMEM(step_size.shape, F32),
            pltpu.VMEM(log_decay.shape, F32),
            pltpu.VMEM((1, channels), F32),
            pltpu.VMEM((2, n, groups, length, HEAD_DIM), BF16),
            pltpu.VMEM((chunks, CHUNK, q_cols), BF16),
            pltpu.VMEM((chunks, CHUNK, q_cols), BF16),
            pltpu.VMEM((STATE, length), BF16),
            pltpu.VMEM((2, length // 2, length // 2), F32),
            pltpu.VMEM((chunks, 4 * per, length), F32),
            pltpu.VMEM((chunks, length, 4 * per), F32),
            pltpu.VMEM((chunks, per, length), F32),
            pltpu.VMEM((chunks, coded, CHUNK), jnp.int16),
            pltpu.VMEM((chunks, coded, CHUNK), jnp.int16),
            pltpu.VMEM((chunks, 1, CHUNK), F32),
            pltpu.VMEM((chunks, 1, CHUNK), F32),
            pltpu.VMEM((chunks, length, CHUNK), BF16),
            pltpu.VMEM((length, q_cols), F32),
            pltpu.VMEM((heads, length, HEAD_DIM), BF16),
            pltpu.VMEM((n, length, length), F32),
            pltpu.VMEM((heads, length, length), BF16),
            pltpu.VMEM((heads, length, HEAD_DIM), F32),
            pltpu.VMEM((heads, length, HEAD_DIM), F32),
            pltpu.VMEM((heads, length, HEAD_DIM), F32),
            dma((6,)),
            dma((2, groups)),
            dma((2, n, groups)),
            dma((2, n + 1, groups)),
        ]
        + [dma((chunks,))] * 10
        + [dma((groups,))],
        compiler_params=pltpu.CompilerParams(
            collective_id=0, has_side_effects=True, vmem_limit_bytes=56 * 1024 * 1024
        ),
        name="mixer_attention",
    )(
        block_mask,
        skip_gain,
        ssm_input,
        input_map,
        output_map,
        step_size,
        log_decay,
        norm_gain.reshape(1, channels),
        query_weight,
        key_states,
        value_states,
    )
    return pl.pallas_call(
        hand_on,
        out_shape=outs,
        in_specs=[far, far],
        out_specs=[far, far],
        scratch_shapes=[dma((2, 4))],
        name="hand_on",
    )(*results)


def solution(mesh):
    return jax.shard_map(
        on_device,
        mesh=mesh,
        in_specs=(
            P(("dp", "context"), "tensor"),
            P(("dp", "context"), None),
            P(("dp", "context"), None),
            P("tensor", ("dp", "context")),
            P("tensor", ("dp", "context")),
            P("tensor"),
            P("tensor"),
            P("tensor", None),
            P(("dp", "context"), "tensor"),
            P(("dp", "context"), "tensor"),
            P("dp", None),
        ),
        out_specs=(P(("dp", "context"), "tensor"), P(("dp", "context"), "tensor")),
        check_vma=False,
    )
```

```python
import functools

import jax
import jax.numpy as jnp
from jax import lax
from jax.experimental import pallas as pl
from jax.experimental.pallas import tpu as pltpu
from jax.sharding import PartitionSpec as P

HEAD_P = 64
STATE = 128
HEAD_DIM = 128
BLOCK = 128
CHUNK = 256
NEGATIVE = -1e30
LOG2E = 1.4426950408889634
LEVELS = 524287.0
MESH = pl.DeviceIdType.MESH
F32 = jnp.float32
BF16 = jnp.bfloat16
NT = (((1,), (1,)), ((), ()))


def split(wide):
    high = wide.astype(BF16)
    rest = wide - high.astype(F32)
    middle = rest.astype(BF16)
    return high, middle, (rest - middle.astype(F32)).astype(BF16)


def dot(a, b):
    return jnp.dot(a, b, preferred_element_type=F32)


def dot_left(wide, narrow):
    high, middle, low = split(wide)
    return dot(high, narrow) + (dot(middle, narrow) + dot(low, narrow))


def dot_right(narrow, wide):
    high, middle, low = split(wide)
    return dot(narrow, high) + (dot(narrow, middle) + dot(narrow, low))


def encode(wide):
    largest = jnp.maximum(jnp.max(jnp.abs(wide), axis=0, keepdims=True), 1e-30)
    whole = jnp.round(wide * (LEVELS / largest)).astype(jnp.int32)
    quarter = wide.shape[0] // 4
    low = whole & 15
    packed = low[:quarter]
    for i in range(1, 4):
        packed = packed | (low[i * quarter : (i + 1) * quarter] << (4 * i))
    return (whole >> 4).astype(jnp.int16), (packed - 32768).astype(jnp.int16), largest * (1.0 / LEVELS)


def decode(high, packed, scale):
    packed = packed.astype(jnp.int32) + 32768
    low = jnp.concatenate([(packed >> (4 * i)) & 15 for i in range(4)], axis=0)
    return (high.astype(jnp.int32) * 16 + low).astype(F32) * scale


def kernel(
    n,
    mask_ref,
    skip_ref,
    x_hbm,
    b_hbm,
    c_hbm,
    dt_hbm,
    ld_hbm,
    gain_hbm,
    w_ref,
    k_hbm,
    v_hbm,
    mixer_hbm,
    attended_hbm,
    mixer_ref,
    attended_ref,
    x_ref,
    b_ref,
    c_ref,
    dt_ref,
    ld_ref,
    gain_ref,
    kv,
    w_own,
    w_other,
    bt,
    gram,
    rows_run,
    cols_run,
    rows_adj,
    code,
    code_in,
    scale,
    scale_in,
    mixed_other,
    q_acc,
    q_all,
    bias,
    weights,
    top,
    total,
    acc,
    own,
    ld_sem,
    own_sem,
    kv_send,
    kv_recv,
    st_send,
    st_recv,
    sc_send,
    sc_recv,
    mx_send,
    mx_recv,
    wt_send,
    wt_recv,
    wt_own,
    mx_out,
    at_out,
):
    me = lax.axis_index("context")
    core = lax.axis_index("tensor")
    other = 1 - core
    length = x_ref.shape[0]
    half = length // 2
    chunks = x_ref.shape[1] // CHUNK
    per = CHUNK // HEAD_P
    pairs = CHUNK // 128
    q_cols = w_own.shape[2]
    has_left = me > 0
    has_right = me < n - 1
    middle = has_left & has_right
    heads = q_cols // HEAD_DIM
    groups = kv.shape[2]
    members = heads // groups
    blocks = length // BLOCK

    barrier = pltpu.get_barrier_semaphore()
    pl.semaphore_signal(barrier, inc=1, device_id={"tensor": other}, device_id_type=MESH)

    @pl.when(has_left)
    def _():
        pl.semaphore_signal(barrier, inc=1, device_id={"context": me - 1}, device_id_type=MESH)

    @pl.when(has_right)
    def _():
        pl.semaphore_signal(barrier, inc=1, device_id={"context": me + 1}, device_id_type=MESH)

    loads = [
        pltpu.make_async_copy(src, dst, ld_sem.at[i])
        for i, (src, dst) in enumerate(
            (
                (ld_hbm, ld_ref),
                (dt_hbm, dt_ref),
                (b_hbm, b_ref),
                (c_hbm, c_ref),
                (x_hbm, x_ref),
                (gain_hbm, gain_ref),
            )
        )
    ]
    for load in loads:
        load.start()

    hbm = (k_hbm, v_hbm)

    def fixed_lanes(g):
        return pl.ds(g * HEAD_DIM, HEAD_DIM)

    def own_load(which, g):
        return pltpu.make_async_copy(hbm[which].at[:, fixed_lanes(g)], kv.at[which, 0, g], own_sem.at[which, g])

    for which in range(2):
        for g in range(groups):
            own_load(which, g).start()

    peers = 1 + has_left.astype(jnp.int32) + has_right.astype(jnp.int32)
    pl.semaphore_wait(barrier, peers)

    def pass_own(which, g):
        return pltpu.make_async_remote_copy(
            src_ref=hbm[which].at[:, fixed_lanes(g)],
            dst_ref=kv.at[which, 1, g],
            send_sem=kv_send.at[which, 0, g],
            recv_sem=kv_recv.at[which, 1, g],
            device_id={"context": me + 1},
            device_id_type=MESH,
        )

    def pass_on(which, slot, g):
        return pltpu.make_async_remote_copy(
            src_ref=kv.at[which, slot, g],
            dst_ref=kv.at[which, slot + 1, g],
            send_sem=kv_send.at[which, slot, g],
            recv_sem=kv_recv.at[which, slot + 1, g],
            device_id={"context": me + 1},
            device_id_type=MESH,
        )

    def arrive(which, slot, g):
        pltpu.make_async_remote_copy(
            src_ref=kv.at[which, slot - 1, g],
            dst_ref=kv.at[which, slot, g],
            send_sem=kv_send.at[which, slot - 1, g],
            recv_sem=kv_recv.at[which, slot, g],
            device_id={"context": me - 1},
            device_id_type=MESH,
        ).wait_recv()

    def forward(which, slot, g):
        arrive(which, slot, g)
        pass_on(which, slot, g).start()

    def state_copies(j):
        return [
            pltpu.make_async_remote_copy(
                src_ref=src.at[j],
                dst_ref=dst.at[j],
                send_sem=send.at[j],
                recv_sem=recv.at[j],
                device_id={"context": me + 1},
                device_id_type=MESH,
            )
            for src, dst, send, recv in ((scale, scale_in, sc_send, sc_recv), (code, code_in, st_send, st_recv))
        ]

    def lanes_of(j):
        return pl.ds(pl.multiple_of(j * CHUNK, CHUNK), CHUNK)

    def mixed_copy(j):
        return pltpu.make_async_remote_copy(
            src_ref=mixer_ref.at[:, lanes_of(j)],
            dst_ref=mixed_other.at[j],
            send_sem=mx_send.at[j],
            recv_sem=mx_recv.at[j],
            device_id={"tensor": other},
            device_id_type=MESH,
        )

    def mixed_out(j):
        return pltpu.make_async_copy(mixer_ref.at[:, lanes_of(j)], mixer_hbm.at[:, lanes_of(j)], mx_out.at[j])

    def attended_out(g):
        lanes = pl.ds(pl.multiple_of(g * members * HEAD_DIM, HEAD_DIM), members * HEAD_DIM)
        return pltpu.make_async_copy(attended_ref.at[:, lanes], attended_hbm.at[:, lanes], at_out.at[g])

    def weight_out(j):
        return pltpu.make_async_remote_copy(
            src_ref=w_ref.at[lanes_of(j), pl.ds(pl.multiple_of(other * q_cols, CHUNK), q_cols)],
            dst_ref=w_other.at[j],
            send_sem=wt_send.at[j],
            recv_sem=wt_recv.at[j],
            device_id={"tensor": other},
            device_id_type=MESH,
        )

    def weight_in(j):
        return pltpu.make_async_copy(
            w_ref.at[lanes_of(j), pl.ds(pl.multiple_of(core * q_cols, CHUNK), q_cols)],
            w_own.at[j],
            wt_own.at[j],
        )

    @pl.when(has_right)
    def _():
        for g in range(groups):

            @pl.when(has_left | (g < groups // 2))
            def _(g=g):
                pass_own(0, g).start()

    @pl.loop(0, chunks)
    def _(j):
        weight_in(j).start()
        weight_out(j).start()

    row = lax.broadcasted_iota(jnp.int32, (length, length), 0)
    col = lax.broadcasted_iota(jnp.int32, (length, length), 1)
    same = (row // BLOCK) == (col // BLOCK)
    loads[0].wait()
    loads[1].wait()
    up_to = jnp.where((row <= col) & ((row // half) == (col // half)), 1.0, 0.0).astype(BF16)
    run = dot_left(ld_ref[...], up_to) * LOG2E
    ends = jnp.concatenate(
        [
            jnp.broadcast_to(run[:, half - 1 : half], (run.shape[0], half)),
            jnp.broadcast_to(run[:, length - 1 : length], (run.shape[0], half)),
        ],
        axis=1,
    )
    steps = dt_ref[...]
    grow = jnp.exp2(run)
    inject = jnp.exp2(ends - run) * steps
    adjusted = run - jnp.log(steps) * LOG2E
    for j in range(chunks):
        part = slice(j * per, (j + 1) * per)
        rows_run[j, 0:per, :] = run[part]
        rows_run[j, per : 2 * per, :] = grow[part]
        rows_run[j, 2 * per : 3 * per, :] = inject[part]
        rows_run[j, 3 * per : 4 * per, :] = inject[part]
        rows_adj[j] = adjusted[part]
    for j in range(chunks):
        cols_run[j] = jnp.transpose(rows_run[j])
    loads[2].wait()
    loads[3].wait()
    bt[...] = jnp.transpose(b_ref[...].astype(F32)).astype(BF16)
    for s in range(2):
        part = slice(s * half, (s + 1) * half)
        gram[s] = jnp.where(
            row[:half, :half] >= col[:half, :half],
            lax.dot_general(c_ref[part, :], b_ref[part, :], NT, preferred_element_type=F32),
            0.0,
        )
    first = lax.broadcasted_iota(jnp.int32, (1, 128), 1) < HEAD_P
    loads[4].wait()
    loads[5].wait()

    def spread(table, at):
        return jnp.concatenate(
            [
                jnp.where(first, table[:, at + 2 * p : at + 2 * p + 1], table[:, at + 2 * p + 1 : at + 2 * p + 2])
                for p in range(pairs)
            ],
            axis=1,
        )

    def own_part(j, s):
        return own[2 * j + s]

    def send_state(j, entering):
        keep = spread(cols_run[j, length - 1 : length, :], per)
        high, packed, unit = encode(keep * entering + own_part(j, 1))
        code[j, 0:STATE, :] = high
        code[j, STATE : STATE + STATE // 4, :] = packed
        scale[j] = unit
        for copy in state_copies(j):
            copy.start()

    @pl.loop(0, chunks)
    def _(j):
        weighted = x_ref[:, lanes_of(j)].astype(F32) * spread(cols_run[j], 2 * per)

        def keep_part(s):
            own[2 * j + s] = dot_right(bt[:, s * half : (s + 1) * half], weighted[s * half : (s + 1) * half])

        keep_part(0)

        @pl.when(has_right)
        def _():
            keep_part(1)

        @pl.when(~has_left & has_right)
        def _():
            send_state(j, own_part(j, 0))

    @pl.when(~has_left & has_right)
    def _():
        for g in range(groups // 2, groups):
            pass_own(0, g).start()
        for g in range(groups):
            pass_own(1, g).start()

    def inside(j):
        runs = cols_run[j]
        adj = rows_adj[j]
        for p in range(pairs):
            lanes = pl.ds(pl.multiple_of(j * CHUNK + p * 128, 128), 128)
            for s in range(2):
                part = slice(s * half, (s + 1) * half)
                x_own = x_ref[part, lanes]
                x_wide = x_own.astype(F32)
                pieces = []
                for m in range(2):
                    a = 2 * p + m
                    weight = gram[s] * jnp.exp2(jnp.minimum(runs[part, a : a + 1] - adj[a : a + 1, part], 0.0))
                    pieces.append(split(weight))
                both = jnp.concatenate(
                    [
                        jnp.where(first, x_wide, 0.0).astype(BF16),
                        jnp.where(first, 0.0, x_wide).astype(BF16),
                    ],
                    axis=0,
                )
                high, mid, low = (jnp.concatenate([pieces[0][i], pieces[1][i]], axis=1) for i in range(3))
                gain = jnp.where(first, skip_ref[j * per + 2 * p], skip_ref[j * per + 2 * p + 1])
                acc[2 * j + s, :, p * 128 : (p + 1) * 128] = (dot(high, both) + (dot(mid, both) + dot(low, both))) + gain * x_wide

    for slot in range(n):

        @pl.when(slot <= me)
        def _(slot=slot):
            for i in range(blocks):
                for m in range(blocks):
                    seen = mask_ref[me * blocks + i, (me - slot) * blocks + m] == 1
                    bias[slot, m * BLOCK : (m + 1) * BLOCK, i * BLOCK : (i + 1) * BLOCK] = jnp.full(
                        (BLOCK, BLOCK), jnp.where(seen, 0.0, NEGATIVE), F32
                    )

    bias[0] = jnp.where(row <= col, jnp.where(same, 0.0, bias[0]), NEGATIVE)
    q_acc[...] = jnp.zeros_like(q_acc)
    total[...] = jnp.zeros_like(total)
    top[...] = jnp.full_like(top, NEGATIVE)

    @pl.when((me >= 2) & has_right)
    def _():
        for g in range(groups):
            forward(0, 1, g)

    ahead = jnp.where(has_right, jnp.minimum(me, 2), chunks)

    @pl.loop(0, ahead)
    def _(j):
        inside(j)

    def add_query(j):
        for t in range(0, q_cols, 512):
            q_acc[:, t : t + 512] += dot(mixer_ref[:, lanes_of(j)], w_own[j, :, t : t + 512])

    def add_other(j):
        mixed_copy(j).wait_recv()
        weight_out(j).wait_recv()
        for t in range(0, q_cols, 512):
            q_acc[:, t : t + 512] += dot(mixed_other[j], w_other[j, :, t : t + 512])

    @pl.when(~has_left)
    def _():
        code_in[...] = jnp.zeros_like(code_in)
        scale_in[...] = jnp.zeros_like(scale_in)

    second = me == 1
    later = (me >= 2) & has_right

    @pl.loop(0, chunks)
    def _(j):
        @pl.when(has_left)
        def _():
            for copy in state_copies(j):
                copy.wait_recv()

        arrived = decode(code_in[j, 0:STATE, :], code_in[j, STATE : STATE + STATE // 4, :], scale_in[j])
        entering = spread(cols_run[j, half - 1 : half, :], per) * arrived + own_part(j, 0)

        @pl.when(middle)
        def _():
            send_state(j, entering)

        for g in range(groups):
            for role, at in ((second, (1, 2, chunks - 2, chunks - 1)[g]), (later, (2, 3, chunks - 1, chunks)[g])):

                @pl.when(role & (j == at))
                def _(g=g, role=role):
                    if role is second:
                        forward(0, 1, g)
                    else:

                        @pl.when(me >= 2)
                        def _():
                            forward(0, 2, g)

            @pl.when(second & has_right & (j == (0, 3, 4, 5)[g]))
            def _(g=g):
                pass_own(1, g).start()

        @pl.when(j >= ahead)
        def _():
            inside(j)

        runs = cols_run[j]
        for s in range(2):
            part = slice(s * half, (s + 1) * half)
            carried = dot_right(c_ref[part, :], arrived if s == 0 else entering)
            grown = spread(runs[part], per)
            for p in range(pairs):
                lanes = slice(p * 128, (p + 1) * 128)
                out_lanes = pl.ds(pl.multiple_of(j * CHUNK + p * 128, 128), 128)
                y = acc[2 * j + s, :, lanes] + carried[:, lanes] * grown[:, lanes]
                squares = y * y
                left = jnp.sum(jnp.where(first, squares, 0.0), axis=1, keepdims=True)
                right = jnp.sum(jnp.where(first, 0.0, squares), axis=1, keepdims=True)
                mean = jnp.where(first, left, right) * (1.0 / HEAD_P)
                mixer_ref[part, out_lanes] = (y * lax.rsqrt(mean + 1e-05) * gain_ref[:, out_lanes]).astype(BF16)
        mixed_copy(j).start()
        mixed_out(j).start()
        weight_in(j).wait()
        add_query(j)

        @pl.when(j >= 1)
        def _():
            add_other(j - 1)

    @pl.when(later)
    def _():
        forward(0, 2, groups - 1)

        @pl.loop(3, n)
        def _(slot):
            @pl.when(slot <= me)
            def _():
                for g in range(groups):
                    forward(0, slot, g)

        for g in range(groups):
            pass_own(1, g).start()
        for g in range(groups):
            forward(1, 1, g)

    @pl.when(second & has_right)
    def _():
        for g in range(groups):
            forward(1, 1, g)

    add_other(chunks - 1)
    for h in range(heads):
        q_all[h] = q_acc[:, h * HEAD_DIM : (h + 1) * HEAD_DIM].astype(BF16)
    for which in range(2):
        for g in range(groups):
            own_load(which, g).wait()
    unit = HEAD_DIM ** (-0.5) * LOG2E

    def head_lanes(h):
        return pl.ds(pl.multiple_of(h * HEAD_DIM, HEAD_DIM), HEAD_DIM)

    def scores_of(slot, h, keys):
        return lax.dot_general(keys, q_all[h], NT, preferred_element_type=F32) + bias[slot]

    def by_eight(table):
        return table.reshape(length // 8, 8, length)

    @pl.loop(0, n)
    def _(slot):
        @pl.when(slot <= me)
        def _():
            @pl.loop(0, groups)
            def _(g):
                @pl.when(~has_right & (slot >= 1))
                def _():
                    arrive(0, slot, g)

                keys = kv[0, slot, g]
                for member in range(members):
                    h = g * members + member
                    top[h] = jnp.maximum(top[h], jnp.max(by_eight(scores_of(slot, h, keys)), axis=0))

    @pl.when(later)
    def _():
        @pl.loop(2, n)
        def _(slot):
            @pl.when(slot <= me)
            def _():
                for g in range(groups):
                    forward(1, slot, g)

    for h in range(heads):
        top[h] = jnp.broadcast_to(jnp.max(top[h], axis=0, keepdims=True), top.shape[1:])

    def weigh(slot, g):
        keys = kv[0, slot, g]
        for member in range(members):
            h = g * members + member
            part = jnp.exp2((by_eight(scores_of(slot, h, keys)) - top[h]) * unit)
            total[h] += jnp.sum(part, axis=0)
            weights[slot % 2, h] = part.reshape(length, length).astype(BF16)

    def attend(slot, g):
        values = jnp.transpose(kv[1, slot, g].astype(F32)).astype(BF16)
        for member in range(members):
            h = g * members + member
            acc[h] = jnp.where(slot == 0, 0.0, acc[h]) + dot(values, weights[slot % 2, h])

    def arrive_values(slot, g):
        @pl.when(~has_right & (slot >= 1))
        def _():
            arrive(1, slot, g)

    @pl.loop(0, groups)
    def _(g):
        weigh(0, g)

    @pl.loop(1, n)
    def _(slot):
        @pl.when(slot <= me)
        def _():
            @pl.loop(0, groups)
            def _(g):
                arrive_values(slot - 1, g)
                weigh(slot, g)
                attend(slot - 1, g)

    @pl.loop(0, groups)
    def _(g):
        arrive_values(me, g)
        attend(me, g)
        for member in range(members):
            h = g * members + member
            out = acc[h] / jnp.sum(total[h], axis=0, keepdims=True)
            attended_ref[:, head_lanes(h)] = jnp.transpose(out).astype(BF16)
        attended_out(g).start()

    @pl.loop(0, groups)
    def _(g):
        attended_out(g).wait()

    @pl.loop(0, chunks)
    def _(j):
        mixed_copy(j).wait_send()
        mixed_out(j).wait()
        weight_out(j).wait_send()

        @pl.when(has_right)
        def _():
            for copy in state_copies(j):
                copy.wait_send()

    @pl.loop(0, n)
    def _(slot):
        @pl.when((slot <= me) & has_right)
        def _():
            for which in range(2):
                for g in range(groups):
                    pass_on(which, slot, g).wait_send()


def hand_on(mixer_ref, attended_ref, mixer_out, attended_out, held, loads, stores):
    parts = held.shape[1]
    rows = held.shape[2]
    refs = ((mixer_ref, mixer_out), (attended_ref, attended_out))

    def load(k, i):
        return pltpu.make_async_copy(refs[k][0].at[pl.ds(i * rows, rows)], held.at[k, i], loads.at[k, i])

    def store(k, i):
        return pltpu.make_async_copy(held.at[k, i], refs[k][1].at[pl.ds(i * rows, rows)], stores.at[k, i])

    every = [(k, i) for k in range(2) for i in range(parts)]
    for at in every:
        load(*at).start()
    for at in every:
        load(*at).wait()
        store(*at).start()
    for at in every:
        store(*at).wait()


def on_device(
    ssm_input,
    input_map,
    output_map,
    step_size,
    log_decay,
    skip_gain,
    norm_gain,
    query_weight,
    key_states,
    value_states,
    block_mask,
):
    n = lax.axis_size("context")
    length, channels = ssm_input.shape
    q_cols = query_weight.shape[1] // lax.axis_size("tensor")
    chunks = channels // CHUNK
    heads = q_cols // HEAD_DIM
    per = CHUNK // HEAD_P
    groups = key_states.shape[1] // HEAD_DIM
    smem = pl.BlockSpec(memory_space=pltpu.SMEM)
    hbm = pl.BlockSpec(memory_space=pltpu.HBM)
    far = pl.BlockSpec(memory_space=pl.ANY)
    dma = pltpu.SemaphoreType.DMA
    outs = (
        jax.ShapeDtypeStruct((length, channels), BF16),
        jax.ShapeDtypeStruct((length, q_cols), BF16),
    )
    coded = STATE + STATE // 4
    results = pl.pallas_call(
        functools.partial(kernel, n),
        out_shape=outs,
        in_specs=[smem, smem] + [hbm] * 9,
        out_specs=(hbm, hbm),
        scratch_shapes=[
            pltpu.VMEM((length, channels), BF16),
            pltpu.VMEM((length, q_cols), BF16),
            pltpu.VMEM((length, channels), BF16),
            pltpu.VMEM((length, STATE), BF16),
            pltpu.VMEM((length, STATE), BF16),
            pltpu.VMEM(step_size.shape, F32),
            pltpu.VMEM(log_decay.shape, F32),
            pltpu.VMEM((1, channels), F32),
            pltpu.VMEM((2, n, groups, length, HEAD_DIM), BF16),
            pltpu.VMEM((chunks, CHUNK, q_cols), BF16),
            pltpu.VMEM((chunks, CHUNK, q_cols), BF16),
            pltpu.VMEM((STATE, length), BF16),
            pltpu.VMEM((2, length // 2, length // 2), F32),
            pltpu.VMEM((chunks, 4 * per, length), F32),
            pltpu.VMEM((chunks, length, 4 * per), F32),
            pltpu.VMEM((chunks, per, length), F32),
            pltpu.VMEM((chunks, coded, CHUNK), jnp.int16),
            pltpu.VMEM((chunks, coded, CHUNK), jnp.int16),
            pltpu.VMEM((chunks, 1, CHUNK), F32),
            pltpu.VMEM((chunks, 1, CHUNK), F32),
            pltpu.VMEM((chunks, length, CHUNK), BF16),
            pltpu.VMEM((length, q_cols), F32),
            pltpu.VMEM((heads, length, HEAD_DIM), BF16),
            pltpu.VMEM((n, length, length), F32),
            pltpu.VMEM((2, heads, length, length), BF16),
            pltpu.VMEM((heads, 8, length), F32),
            pltpu.VMEM((heads, 8, length), F32),
            pltpu.VMEM((max(heads, 2 * chunks), HEAD_DIM, length), F32),
            pltpu.VMEM((2 * chunks, STATE, CHUNK), F32),
            dma((6,)),
            dma((2, groups)),
            dma((2, n, groups)),
            dma((2, n + 1, groups)),
        ]
        + [dma((chunks,))] * 10
        + [dma((groups,))],
        compiler_params=pltpu.CompilerParams(
            collective_id=0, has_side_effects=True, vmem_limit_bytes=56 * 1024 * 1024
        ),
        name="mixer_attention",
    )(
        block_mask,
        skip_gain,
        ssm_input,
        input_map,
        output_map,
        step_size,
        log_decay,
        norm_gain.reshape(1, channels),
        query_weight,
        key_states,
        value_states,
    )
    return pl.pallas_call(
        hand_on,
        out_shape=outs,
        in_specs=[far, far],
        out_specs=[far, far],
        scratch_shapes=[pltpu.VMEM((2, 4, length // 4, channels), BF16), dma((2, 4)), dma((2, 4))],
        name="hand_on",
    )(*results)


def solution(mesh):
    return jax.shard_map(
        on_device,
        mesh=mesh,
        in_specs=(
            P(("dp", "context"), "tensor"),
            P(("dp", "context"), None),
            P(("dp", "context"), None),
            P("tensor", ("dp", "context")),
            P("tensor", ("dp", "context")),
            P("tensor"),
            P("tensor"),
            P("tensor", None),
            P(("dp", "context"), "tensor"),
            P(("dp", "context"), "tensor"),
            P("dp", None),
        ),
        out_specs=(P(("dp", "context"), "tensor"), P(("dp", "context"), "tensor")),
        check_vma=False,
    )
```

```python
import functools

import jax
import jax.numpy as jnp
from jax import lax
from jax.experimental import pallas as pl
from jax.experimental.pallas import tpu as pltpu
from jax.sharding import PartitionSpec as P

HEAD_P = 64
STATE = 128
HEAD_DIM = 128
BLOCK = 128
CHUNK = 256
NEGATIVE = -1e30
LOG2E = 1.4426950408889634
LEVELS = 524287.0
MESH = pl.DeviceIdType.MESH
F32 = jnp.float32
BF16 = jnp.bfloat16
NT = (((1,), (1,)), ((), ()))


def split(wide):
    high = wide.astype(BF16)
    rest = wide - high.astype(F32)
    middle = rest.astype(BF16)
    return high, middle, (rest - middle.astype(F32)).astype(BF16)


def dot(a, b):
    return jnp.dot(a, b, preferred_element_type=F32)


def dot_left(wide, narrow):
    high, middle, low = split(wide)
    return dot(high, narrow) + (dot(middle, narrow) + dot(low, narrow))


def dot_right(narrow, wide):
    high, middle, low = split(wide)
    return dot(narrow, high) + (dot(narrow, middle) + dot(narrow, low))


def encode(wide):
    largest = jnp.maximum(jnp.max(jnp.abs(wide), axis=0, keepdims=True), 1e-30)
    whole = jnp.round(wide * (LEVELS / largest)).astype(jnp.int32)
    quarter = wide.shape[0] // 4
    low = whole & 15
    packed = low[:quarter]
    for i in range(1, 4):
        packed = packed | (low[i * quarter : (i + 1) * quarter] << (4 * i))
    return (whole >> 4).astype(jnp.int16), (packed - 32768).astype(jnp.int16), largest * (1.0 / LEVELS)


def decode(high, packed, scale):
    packed = packed.astype(jnp.int32) + 32768
    low = jnp.concatenate([(packed >> (4 * i)) & 15 for i in range(4)], axis=0)
    return (high.astype(jnp.int32) * 16 + low).astype(F32) * scale


def kernel(
    n,
    mask_ref,
    skip_ref,
    x_hbm,
    b_hbm,
    c_hbm,
    dt_hbm,
    ld_hbm,
    gain_hbm,
    w_ref,
    k_hbm,
    v_hbm,
    mixer_hbm,
    attended_hbm,
    mixer_ref,
    attended_ref,
    x_ref,
    b_ref,
    c_ref,
    dt_ref,
    ld_ref,
    gain_ref,
    kv,
    w_own,
    w_other,
    bt,
    gram,
    rows_run,
    cols_run,
    rows_adj,
    code,
    code_in,
    scale,
    scale_in,
    mixed_other,
    q_acc,
    q_all,
    bias,
    weights,
    top,
    total,
    acc,
    own,
    ld_sem,
    own_sem,
    kv_send,
    kv_recv,
    st_send,
    st_recv,
    sc_send,
    sc_recv,
    mx_send,
    mx_recv,
    wt_send,
    wt_recv,
    wt_own,
    mx_out,
    at_out,
):
    me = lax.axis_index("context")
    core = lax.axis_index("tensor")
    other = 1 - core
    length = x_ref.shape[0]
    half = length // 2
    chunks = x_ref.shape[1] // CHUNK
    per = CHUNK // HEAD_P
    pairs = CHUNK // 128
    q_cols = w_own.shape[2]
    has_left = me > 0
    has_right = me < n - 1
    middle = has_left & has_right
    heads = q_cols // HEAD_DIM
    groups = kv.shape[2]
    members = heads // groups
    blocks = length // BLOCK

    barrier = pltpu.get_barrier_semaphore()
    pl.semaphore_signal(barrier, inc=1, device_id={"tensor": other}, device_id_type=MESH)

    @pl.when(has_left)
    def _():
        pl.semaphore_signal(barrier, inc=1, device_id={"context": me - 1}, device_id_type=MESH)

    @pl.when(has_right)
    def _():
        pl.semaphore_signal(barrier, inc=1, device_id={"context": me + 1}, device_id_type=MESH)

    loads = [
        pltpu.make_async_copy(src, dst, ld_sem.at[i])
        for i, (src, dst) in enumerate(
            (
                (ld_hbm, ld_ref),
                (dt_hbm, dt_ref),
                (b_hbm, b_ref),
                (c_hbm, c_ref),
                (x_hbm, x_ref),
                (gain_hbm, gain_ref),
            )
        )
    ]
    for load in loads:
        load.start()

    hbm = (k_hbm, v_hbm)

    def fixed_lanes(g):
        return pl.ds(g * HEAD_DIM, HEAD_DIM)

    def own_load(which, g):
        return pltpu.make_async_copy(hbm[which].at[:, fixed_lanes(g)], kv.at[which, 0, g], own_sem.at[which, g])

    for which in range(2):
        for g in range(groups):
            own_load(which, g).start()

    peers = 1 + has_left.astype(jnp.int32) + has_right.astype(jnp.int32)

    @pl.when(has_left)
    def _():
        pl.semaphore_wait(barrier, peers)

    def pass_own(which, g):
        return pltpu.make_async_remote_copy(
            src_ref=hbm[which].at[:, fixed_lanes(g)],
            dst_ref=kv.at[which, 1, g],
            send_sem=kv_send.at[which, 0, g],
            recv_sem=kv_recv.at[which, 1, g],
            device_id={"context": me + 1},
            device_id_type=MESH,
        )

    def pass_on(which, slot, g):
        return pltpu.make_async_remote_copy(
            src_ref=kv.at[which, slot, g],
            dst_ref=kv.at[which, slot + 1, g],
            send_sem=kv_send.at[which, slot, g],
            recv_sem=kv_recv.at[which, slot + 1, g],
            device_id={"context": me + 1},
            device_id_type=MESH,
        )

    def arrive(which, slot, g):
        pltpu.make_async_remote_copy(
            src_ref=kv.at[which, slot - 1, g],
            dst_ref=kv.at[which, slot, g],
            send_sem=kv_send.at[which, slot - 1, g],
            recv_sem=kv_recv.at[which, slot, g],
            device_id={"context": me - 1},
            device_id_type=MESH,
        ).wait_recv()

    def forward(which, slot, g):
        arrive(which, slot, g)
        pass_on(which, slot, g).start()

    def state_copies(j):
        return [
            pltpu.make_async_remote_copy(
                src_ref=src.at[j],
                dst_ref=dst.at[j],
                send_sem=send.at[j],
                recv_sem=recv.at[j],
                device_id={"context": me + 1},
                device_id_type=MESH,
            )
            for src, dst, send, recv in ((scale, scale_in, sc_send, sc_recv), (code, code_in, st_send, st_recv))
        ]

    def lanes_of(j):
        return pl.ds(pl.multiple_of(j * CHUNK, CHUNK), CHUNK)

    def mixed_copy(j):
        return pltpu.make_async_remote_copy(
            src_ref=mixer_ref.at[:, lanes_of(j)],
            dst_ref=mixed_other.at[j],
            send_sem=mx_send.at[j],
            recv_sem=mx_recv.at[j],
            device_id={"tensor": other},
            device_id_type=MESH,
        )

    def mixed_out(j):
        return pltpu.make_async_copy(mixer_ref.at[:, lanes_of(j)], mixer_hbm.at[:, lanes_of(j)], mx_out.at[j])

    def attended_out(g):
        lanes = pl.ds(pl.multiple_of(g * members * HEAD_DIM, HEAD_DIM), members * HEAD_DIM)
        return pltpu.make_async_copy(attended_ref.at[:, lanes], attended_hbm.at[:, lanes], at_out.at[g])

    def weight_out(j):
        return pltpu.make_async_remote_copy(
            src_ref=w_ref.at[lanes_of(j), pl.ds(pl.multiple_of(other * q_cols, CHUNK), q_cols)],
            dst_ref=w_other.at[j],
            send_sem=wt_send.at[j],
            recv_sem=wt_recv.at[j],
            device_id={"tensor": other},
            device_id_type=MESH,
        )

    def weight_in(j):
        return pltpu.make_async_copy(
            w_ref.at[lanes_of(j), pl.ds(pl.multiple_of(core * q_cols, CHUNK), q_cols)],
            w_own.at[j],
            wt_own.at[j],
        )

    def start_weights():
        @pl.loop(0, chunks)
        def _(j):
            weight_in(j).start()
            weight_out(j).start()

    @pl.when(has_left)
    def _():
        @pl.when(has_right)
        def _():
            for g in range(groups):
                pass_own(0, g).start()

        start_weights()

    row = lax.broadcasted_iota(jnp.int32, (length, length), 0)
    col = lax.broadcasted_iota(jnp.int32, (length, length), 1)
    same = (row // BLOCK) == (col // BLOCK)
    loads[0].wait()
    loads[1].wait()
    up_to = jnp.where((row <= col) & ((row // half) == (col // half)), 1.0, 0.0).astype(BF16)
    run = dot_left(ld_ref[...], up_to) * LOG2E
    ends = jnp.concatenate(
        [
            jnp.broadcast_to(run[:, half - 1 : half], (run.shape[0], half)),
            jnp.broadcast_to(run[:, length - 1 : length], (run.shape[0], half)),
        ],
        axis=1,
    )
    steps = dt_ref[...]
    grow = jnp.exp2(run)
    inject = jnp.exp2(ends - run) * steps
    adjusted = run - jnp.log(steps) * LOG2E
    for j in range(chunks):
        part = slice(j * per, (j + 1) * per)
        rows_run[j, 0:per, :] = run[part]
        rows_run[j, per : 2 * per, :] = grow[part]
        rows_run[j, 2 * per : 3 * per, :] = inject[part]
        rows_run[j, 3 * per : 4 * per, :] = inject[part]
        rows_adj[j] = adjusted[part]
    for j in range(chunks):
        cols_run[j] = jnp.transpose(rows_run[j])
    loads[2].wait()
    loads[3].wait()
    bt[...] = jnp.transpose(b_ref[...].astype(F32)).astype(BF16)
    for s in range(2):
        part = slice(s * half, (s + 1) * half)
        gram[s] = jnp.where(
            row[:half, :half] >= col[:half, :half],
            lax.dot_general(c_ref[part, :], b_ref[part, :], NT, preferred_element_type=F32),
            0.0,
        )
    first = lax.broadcasted_iota(jnp.int32, (1, 128), 1) < HEAD_P
    loads[4].wait()
    loads[5].wait()
    second = (me == 1) & has_right
    later = (me >= 2) & has_right
    stride = chunks // groups

    @pl.when(~has_left)
    def _():
        pl.semaphore_wait(barrier, peers)
        start_weights()

    def spread(table, at):
        return jnp.concatenate(
            [
                jnp.where(first, table[:, at + 2 * p : at + 2 * p + 1], table[:, at + 2 * p + 1 : at + 2 * p + 2])
                for p in range(pairs)
            ],
            axis=1,
        )

    def own_part(j, s):
        return own[2 * j + s]

    def send_state(j, entering):
        keep = spread(cols_run[j, length - 1 : length, :], per)
        high, packed, unit = encode(keep * entering + own_part(j, 1))
        code[j, 0:STATE, :] = high
        code[j, STATE : STATE + STATE // 4, :] = packed
        scale[j] = unit
        for copy in state_copies(j):
            copy.start()

    @pl.loop(0, chunks)
    def _(j):
        weighted = x_ref[:, lanes_of(j)].astype(F32) * spread(cols_run[j], 2 * per)

        def keep_part(s):
            own[2 * j + s] = dot_right(bt[:, s * half : (s + 1) * half], weighted[s * half : (s + 1) * half])

        keep_part(0)

        @pl.when(has_right)
        def _():
            keep_part(1)

        @pl.when(~has_left & has_right)
        def _():
            send_state(j, own_part(j, 0))

        for g in range(groups):

            @pl.when(later & (j == g * stride))
            def _(g=g):
                forward(0, 1, g)

    @pl.when(~has_left & has_right)
    def _():
        for g in range(groups):
            pass_own(0, g).start()
            pass_own(1, g).start()

    def inside(j):
        runs = cols_run[j]
        adj = rows_adj[j]
        for p in range(pairs):
            lanes = pl.ds(pl.multiple_of(j * CHUNK + p * 128, 128), 128)
            for s in range(2):
                part = slice(s * half, (s + 1) * half)
                x_own = x_ref[part, lanes]
                x_wide = x_own.astype(F32)
                pieces = []
                for m in range(2):
                    a = 2 * p + m
                    weight = gram[s] * jnp.exp2(jnp.minimum(runs[part, a : a + 1] - adj[a : a + 1, part], 0.0))
                    pieces.append(split(weight))
                both = jnp.concatenate(
                    [
                        jnp.where(first, x_wide, 0.0).astype(BF16),
                        jnp.where(first, 0.0, x_wide).astype(BF16),
                    ],
                    axis=0,
                )
                high, mid, low = (jnp.concatenate([pieces[0][i], pieces[1][i]], axis=1) for i in range(3))
                gain = jnp.where(first, skip_ref[j * per + 2 * p], skip_ref[j * per + 2 * p + 1])
                acc[2 * j + s, :, p * 128 : (p + 1) * 128] = (dot(high, both) + (dot(mid, both) + dot(low, both))) + gain * x_wide

    for slot in range(n):

        @pl.when(slot <= me)
        def _(slot=slot):
            for i in range(blocks):
                for m in range(blocks):
                    seen = mask_ref[me * blocks + i, (me - slot) * blocks + m] == 1
                    bias[slot, m * BLOCK : (m + 1) * BLOCK, i * BLOCK : (i + 1) * BLOCK] = jnp.full(
                        (BLOCK, BLOCK), jnp.where(seen, 0.0, NEGATIVE), F32
                    )

    bias[0] = jnp.where(row <= col, jnp.where(same, 0.0, bias[0]), NEGATIVE)
    q_acc[...] = jnp.zeros_like(q_acc)
    total[...] = jnp.zeros_like(total)
    top[...] = jnp.full_like(top, NEGATIVE)

    ahead = jnp.where(me >= 2, chunks, 0)

    @pl.loop(0, ahead)
    def _(j):
        inside(j)

    def add_query(j):
        for t in range(0, q_cols, 512):
            q_acc[:, t : t + 512] += dot(mixer_ref[:, lanes_of(j)], w_own[j, :, t : t + 512])

    def add_other(j):
        mixed_copy(j).wait_recv()
        weight_out(j).wait_recv()
        for t in range(0, q_cols, 512):
            q_acc[:, t : t + 512] += dot(mixed_other[j], w_other[j, :, t : t + 512])

    @pl.when(~has_left)
    def _():
        code_in[...] = jnp.zeros_like(code_in)
        scale_in[...] = jnp.zeros_like(scale_in)

    lag = jnp.where(second, chunks, 0)

    def states_at(j):
        arrived = decode(code_in[j, 0:STATE, :], code_in[j, STATE : STATE + STATE // 4, :], scale_in[j])
        return arrived, spread(cols_run[j, half - 1 : half, :], per) * arrived + own_part(j, 0)

    def relay(j):
        @pl.when(has_left)
        def _():
            for copy in state_copies(j):
                copy.wait_recv()

        @pl.when(middle)
        def _():
            send_state(j, states_at(j)[1])

        @pl.when(later & (j == chunks - 1))
        def _():
            for g in range(groups):
                pass_own(1, g).start()

        @pl.when(j >= ahead)
        def _():
            inside(j)

    def mix(j):
        for g in range(groups):

            @pl.when(second & (j == g * stride))
            def _(g=g):
                forward(0, 1, g)
                pass_own(1, g).start()
                forward(1, 1, g)

        arrived, entering = states_at(j)
        runs = cols_run[j]
        for s in range(2):
            part = slice(s * half, (s + 1) * half)
            carried = dot_right(c_ref[part, :], arrived if s == 0 else entering)
            grown = spread(runs[part], per)
            for p in range(pairs):
                lanes = slice(p * 128, (p + 1) * 128)
                out_lanes = pl.ds(pl.multiple_of(j * CHUNK + p * 128, 128), 128)
                y = acc[2 * j + s, :, lanes] + carried[:, lanes] * grown[:, lanes]
                squares = y * y
                left = jnp.sum(jnp.where(first, squares, 0.0), axis=1, keepdims=True)
                right = jnp.sum(jnp.where(first, 0.0, squares), axis=1, keepdims=True)
                mean = jnp.where(first, left, right) * (1.0 / HEAD_P)
                mixer_ref[part, out_lanes] = (y * lax.rsqrt(mean + 1e-05) * gain_ref[:, out_lanes]).astype(BF16)
        mixed_copy(j).start()
        mixed_out(j).start()
        weight_in(j).wait()
        add_query(j)

        @pl.when(j >= 1)
        def _():
            add_other(j - 1)

    @pl.loop(0, chunks + lag)
    def _(t):
        @pl.when(t < chunks)
        def _():
            relay(t)

        @pl.when(t >= lag)
        def _():
            mix(t - lag)

    add_other(chunks - 1)
    for h in range(heads):
        q_all[h] = q_acc[:, h * HEAD_DIM : (h + 1) * HEAD_DIM].astype(BF16)
    for which in range(2):
        for g in range(groups):
            own_load(which, g).wait()
    unit = HEAD_DIM ** (-0.5) * LOG2E

    def head_lanes(h):
        return pl.ds(pl.multiple_of(h * HEAD_DIM, HEAD_DIM), HEAD_DIM)

    def scores_of(slot, h, keys):
        return lax.dot_general(keys, q_all[h], NT, preferred_element_type=F32) + bias[slot]

    def by_eight(table):
        return table.reshape(length // 8, 8, length)

    def weigh(slot, g):
        keys = kv[0, slot, g]
        for member in range(members):
            h = g * members + member
            part = jnp.exp2((by_eight(scores_of(slot, h, keys)) - top[h]) * unit)
            total[h] += jnp.sum(part, axis=0)
            weights[slot % 2, member] = part.reshape(length, length).astype(BF16)

    def attend(slot, g):
        values = jnp.transpose(kv[1, slot, g].astype(F32)).astype(BF16)
        for member in range(members):
            h = g * members + member
            acc[h] = jnp.where(slot == 0, 0.0, acc[h]) + dot(values, weights[slot % 2, member])

    def arrive_values(slot, g):
        @pl.when(~has_right & (slot >= 1))
        def _():
            arrive(1, slot, g)

    @pl.loop(0, groups)
    def _(g):
        @pl.when(later)
        def _():
            @pl.loop(2, me + 1)
            def _(slot):
                forward(0, slot, g)

            @pl.loop(1, me + 1)
            def _(slot):
                forward(1, slot, g)

        @pl.loop(0, me + 1)
        def _(slot):
            @pl.when(~has_right & (slot >= 1))
            def _():
                arrive(0, slot, g)

            keys = kv[0, slot, g]
            for member in range(members):
                h = g * members + member
                top[h] = jnp.maximum(top[h], jnp.max(by_eight(scores_of(slot, h, keys)), axis=0))

        for member in range(members):
            h = g * members + member
            top[h] = jnp.broadcast_to(jnp.max(top[h], axis=0, keepdims=True), top.shape[1:])
        weigh(0, g)

        @pl.loop(1, me + 1)
        def _(slot):
            arrive_values(slot - 1, g)
            weigh(slot, g)
            attend(slot - 1, g)

        arrive_values(me, g)
        attend(me, g)
        for member in range(members):
            h = g * members + member
            out = acc[h] / jnp.sum(total[h], axis=0, keepdims=True)
            attended_ref[:, head_lanes(h)] = jnp.transpose(out).astype(BF16)
        attended_out(g).start()

    @pl.loop(0, groups)
    def _(g):
        attended_out(g).wait()

    @pl.loop(0, chunks)
    def _(j):
        mixed_copy(j).wait_send()
        mixed_out(j).wait()
        weight_out(j).wait_send()

        @pl.when(has_right)
        def _():
            for copy in state_copies(j):
                copy.wait_send()

    @pl.loop(0, n)
    def _(slot):
        @pl.when((slot <= me) & has_right)
        def _():
            for which in range(2):
                for g in range(groups):
                    pass_on(which, slot, g).wait_send()


def hand_on(mixer_ref, attended_ref, mixer_out, attended_out, held, loads, stores):
    parts = held.shape[1]
    rows = held.shape[2]
    refs = ((mixer_ref, mixer_out), (attended_ref, attended_out))

    def load(k, i):
        return pltpu.make_async_copy(refs[k][0].at[pl.ds(i * rows, rows)], held.at[k, i], loads.at[k, i])

    def store(k, i):
        return pltpu.make_async_copy(held.at[k, i], refs[k][1].at[pl.ds(i * rows, rows)], stores.at[k, i])

    every = [(k, i) for k in range(2) for i in range(parts)]
    for at in every:
        load(*at).start()
    for at in every:
        load(*at).wait()
        store(*at).start()
    for at in every:
        store(*at).wait()


def on_device(
    ssm_input,
    input_map,
    output_map,
    step_size,
    log_decay,
    skip_gain,
    norm_gain,
    query_weight,
    key_states,
    value_states,
    block_mask,
):
    n = lax.axis_size("context")
    length, channels = ssm_input.shape
    q_cols = query_weight.shape[1] // lax.axis_size("tensor")
    chunks = channels // CHUNK
    heads = q_cols // HEAD_DIM
    per = CHUNK // HEAD_P
    groups = key_states.shape[1] // HEAD_DIM
    smem = pl.BlockSpec(memory_space=pltpu.SMEM)
    hbm = pl.BlockSpec(memory_space=pltpu.HBM)
    far = pl.BlockSpec(memory_space=pl.ANY)
    dma = pltpu.SemaphoreType.DMA
    outs = (
        jax.ShapeDtypeStruct((length, channels), BF16),
        jax.ShapeDtypeStruct((length, q_cols), BF16),
    )
    coded = STATE + STATE // 4
    results = pl.pallas_call(
        functools.partial(kernel, n),
        out_shape=outs,
        in_specs=[smem, smem] + [hbm] * 9,
        out_specs=(hbm, hbm),
        scratch_shapes=[
            pltpu.VMEM((length, channels), BF16),
            pltpu.VMEM((length, q_cols), BF16),
            pltpu.VMEM((length, channels), BF16),
            pltpu.VMEM((length, STATE), BF16),
            pltpu.VMEM((length, STATE), BF16),
            pltpu.VMEM(step_size.shape, F32),
            pltpu.VMEM(log_decay.shape, F32),
            pltpu.VMEM((1, channels), F32),
            pltpu.VMEM((2, n, groups, length, HEAD_DIM), BF16),
            pltpu.VMEM((chunks, CHUNK, q_cols), BF16),
            pltpu.VMEM((chunks, CHUNK, q_cols), BF16),
            pltpu.VMEM((STATE, length), BF16),
            pltpu.VMEM((2, length // 2, length // 2), F32),
            pltpu.VMEM((chunks, 4 * per, length), F32),
            pltpu.VMEM((chunks, length, 4 * per), F32),
            pltpu.VMEM((chunks, per, length), F32),
            pltpu.VMEM((chunks, coded, CHUNK), jnp.int16),
            pltpu.VMEM((chunks, coded, CHUNK), jnp.int16),
            pltpu.VMEM((chunks, 1, CHUNK), F32),
            pltpu.VMEM((chunks, 1, CHUNK), F32),
            pltpu.VMEM((chunks, length, CHUNK), BF16),
            pltpu.VMEM((length, q_cols), F32),
            pltpu.VMEM((heads, length, HEAD_DIM), BF16),
            pltpu.VMEM((n, length, length), F32),
            pltpu.VMEM((2, heads // groups, length, length), BF16),
            pltpu.VMEM((heads, 8, length), F32),
            pltpu.VMEM((heads, 8, length), F32),
            pltpu.VMEM((max(heads, 2 * chunks), HEAD_DIM, length), F32),
            pltpu.VMEM((2 * chunks, STATE, CHUNK), F32),
            dma((6,)),
            dma((2, groups)),
            dma((2, n, groups)),
            dma((2, n + 1, groups)),
        ]
        + [dma((chunks,))] * 10
        + [dma((groups,))],
        compiler_params=pltpu.CompilerParams(
            collective_id=0, has_side_effects=True, vmem_limit_bytes=56 * 1024 * 1024
        ),
        name="mixer_attention",
    )(
        block_mask,
        skip_gain,
        ssm_input,
        input_map,
        output_map,
        step_size,
        log_decay,
        norm_gain.reshape(1, channels),
        query_weight,
        key_states,
        value_states,
    )
    return pl.pallas_call(
        hand_on,
        out_shape=outs,
        in_specs=[far, far],
        out_specs=[far, far],
        scratch_shapes=[pltpu.VMEM((2, 4, length // 4, channels), BF16), dma((2, 4)), dma((2, 4))],
        name="hand_on",
    )(*results)


def solution(mesh):
    return jax.shard_map(
        on_device,
        mesh=mesh,
        in_specs=(
            P(("dp", "context"), "tensor"),
            P(("dp", "context"), None),
            P(("dp", "context"), None),
            P("tensor", ("dp", "context")),
            P("tensor", ("dp", "context")),
            P("tensor"),
            P("tensor"),
            P("tensor", None),
            P(("dp", "context"), "tensor"),
            P(("dp", "context"), "tensor"),
            P("dp", None),
        ),
        out_specs=(P(("dp", "context"), "tensor"), P(("dp", "context"), "tensor")),
        check_vma=False,
    )
```

```python
import functools

import jax
import jax.numpy as jnp
from jax import lax
from jax.experimental import pallas as pl
from jax.experimental.pallas import tpu as pltpu
from jax.sharding import PartitionSpec as P

HEAD_P = 64
STATE = 128
HEAD_DIM = 128
BLOCK = 128
CHUNK = 256
NEGATIVE = -1e30
LOG2E = 1.4426950408889634
LEVELS = 524287.0
MESH = pl.DeviceIdType.MESH
F32 = jnp.float32
BF16 = jnp.bfloat16
NT = (((1,), (1,)), ((), ()))


def split(wide):
    high = wide.astype(BF16)
    rest = wide - high.astype(F32)
    middle = rest.astype(BF16)
    return high, middle, (rest - middle.astype(F32)).astype(BF16)


def dot(a, b):
    return jnp.dot(a, b, preferred_element_type=F32)


def dot_left(wide, narrow):
    high, middle, low = split(wide)
    return dot(high, narrow) + (dot(middle, narrow) + dot(low, narrow))


def dot_right(narrow, wide):
    high, middle, low = split(wide)
    return dot(narrow, high) + (dot(narrow, middle) + dot(narrow, low))


def encode(wide):
    largest = jnp.maximum(jnp.max(jnp.abs(wide), axis=0, keepdims=True), 1e-30)
    whole = jnp.round(wide * (LEVELS / largest)).astype(jnp.int32)
    quarter = wide.shape[0] // 4
    low = whole & 15
    packed = low[:quarter]
    for i in range(1, 4):
        packed = packed | (low[i * quarter : (i + 1) * quarter] << (4 * i))
    return (whole >> 4).astype(jnp.int16), (packed - 32768).astype(jnp.int16), largest * (1.0 / LEVELS)


def decode(high, packed, scale):
    packed = packed.astype(jnp.int32) + 32768
    low = jnp.concatenate([(packed >> (4 * i)) & 15 for i in range(4)], axis=0)
    return (high.astype(jnp.int32) * 16 + low).astype(F32) * scale


def kernel(
    n,
    mask_ref,
    skip_ref,
    x_hbm,
    b_hbm,
    c_hbm,
    dt_hbm,
    ld_hbm,
    gain_hbm,
    w_ref,
    k_hbm,
    v_hbm,
    mixer_hbm,
    attended_hbm,
    mixer_ref,
    attended_ref,
    x_ref,
    b_ref,
    c_ref,
    dt_ref,
    ld_ref,
    gain_ref,
    kv,
    w_own,
    w_other,
    bt,
    gram,
    rows_run,
    cols_run,
    rows_adj,
    code,
    code_in,
    scale,
    scale_in,
    mixed_other,
    q_acc,
    q_all,
    bias,
    weights,
    top,
    total,
    acc,
    own,
    ld_sem,
    own_sem,
    kv_send,
    kv_recv,
    st_send,
    st_recv,
    sc_send,
    sc_recv,
    mx_send,
    mx_recv,
    wt_send,
    wt_recv,
    wt_own,
    mx_out,
    at_out,
    answer,
    lk_send,
    lk_recv,
    lq_send,
    lq_recv,
    an_send,
    an_recv,
):
    me = lax.axis_index("context")
    core = lax.axis_index("tensor")
    other = 1 - core
    length = x_ref.shape[0]
    half = length // 2
    chunks = x_ref.shape[1] // CHUNK
    per = CHUNK // HEAD_P
    pairs = CHUNK // 128
    q_cols = w_own.shape[2]
    has_left = me > 0
    has_right = me < n - 1
    helper = me == n - 2
    last = me == n - 1
    middle = has_left & has_right
    heads = q_cols // HEAD_DIM
    groups = kv.shape[2]
    members = heads // groups
    blocks = length // BLOCK

    barrier = pltpu.get_barrier_semaphore()
    pl.semaphore_signal(barrier, inc=1, device_id={"tensor": other}, device_id_type=MESH)

    @pl.when(has_left)
    def _():
        pl.semaphore_signal(barrier, inc=1, device_id={"context": me - 1}, device_id_type=MESH)

    @pl.when(has_right)
    def _():
        pl.semaphore_signal(barrier, inc=1, device_id={"context": me + 1}, device_id_type=MESH)

    loads = [
        pltpu.make_async_copy(src, dst, ld_sem.at[i])
        for i, (src, dst) in enumerate(
            (
                (ld_hbm, ld_ref),
                (dt_hbm, dt_ref),
                (b_hbm, b_ref),
                (c_hbm, c_ref),
                (x_hbm, x_ref),
                (gain_hbm, gain_ref),
            )
        )
    ]
    for load in loads:
        load.start()

    hbm = (k_hbm, v_hbm)

    def fixed_lanes(g):
        return pl.ds(g * HEAD_DIM, HEAD_DIM)

    def own_load(which, g):
        return pltpu.make_async_copy(hbm[which].at[:, fixed_lanes(g)], kv.at[which, 0, g], own_sem.at[which, g])

    for which in range(2):
        for g in range(groups):
            own_load(which, g).start()

    peers = 1 + has_left.astype(jnp.int32) + has_right.astype(jnp.int32)

    @pl.when(has_left)
    def _():
        pl.semaphore_wait(barrier, peers)

    def pass_own(which, g):
        return pltpu.make_async_remote_copy(
            src_ref=hbm[which].at[:, fixed_lanes(g)],
            dst_ref=kv.at[which, 1, g],
            send_sem=kv_send.at[which, 0, g],
            recv_sem=kv_recv.at[which, 1, g],
            device_id={"context": me + 1},
            device_id_type=MESH,
        )

    def pass_on(which, slot, g):
        return pltpu.make_async_remote_copy(
            src_ref=kv.at[which, slot, g],
            dst_ref=kv.at[which, slot + 1, g],
            send_sem=kv_send.at[which, slot, g],
            recv_sem=kv_recv.at[which, slot + 1, g],
            device_id={"context": me + 1},
            device_id_type=MESH,
        )

    def arrive(which, slot, g):
        pltpu.make_async_remote_copy(
            src_ref=kv.at[which, slot - 1, g],
            dst_ref=kv.at[which, slot, g],
            send_sem=kv_send.at[which, slot - 1, g],
            recv_sem=kv_recv.at[which, slot, g],
            device_id={"context": me - 1},
            device_id_type=MESH,
        ).wait_recv()

    lent = groups - 1

    def passes(g):
        return ~helper | (g != lent)

    def forward(which, slot, g):
        arrive(which, slot, g)

        @pl.when(passes(g))
        def _():
            pass_on(which, slot, g).start()

    def lend(which):
        return pltpu.make_async_remote_copy(
            src_ref=hbm[which].at[:, fixed_lanes(lent)],
            dst_ref=kv.at[which, n, lent],
            send_sem=lk_send.at[which],
            recv_sem=lk_recv.at[which],
            device_id={"context": me - 1},
            device_id_type=MESH,
        )

    def lend_query(member):
        return pltpu.make_async_remote_copy(
            src_ref=q_all.at[lent * members + member],
            dst_ref=q_all.at[heads + member],
            send_sem=lq_send.at[member],
            recv_sem=lq_recv.at[member],
            device_id={"context": me - 1},
            device_id_type=MESH,
        )

    def give_back(member):
        return pltpu.make_async_remote_copy(
            src_ref=answer.at[member],
            dst_ref=attended_ref.at[:, fixed_lanes(lent * members + member)],
            send_sem=an_send.at[member],
            recv_sem=an_recv.at[member],
            device_id={"context": me + 1},
            device_id_type=MESH,
        )

    def state_copies(j):
        return [
            pltpu.make_async_remote_copy(
                src_ref=src.at[j],
                dst_ref=dst.at[j],
                send_sem=send.at[j],
                recv_sem=recv.at[j],
                device_id={"context": me + 1},
                device_id_type=MESH,
            )
            for src, dst, send, recv in ((scale, scale_in, sc_send, sc_recv), (code, code_in, st_send, st_recv))
        ]

    def lanes_of(j):
        return pl.ds(pl.multiple_of(j * CHUNK, CHUNK), CHUNK)

    def mixed_copy(j):
        return pltpu.make_async_remote_copy(
            src_ref=mixer_ref.at[:, lanes_of(j)],
            dst_ref=mixed_other.at[j],
            send_sem=mx_send.at[j],
            recv_sem=mx_recv.at[j],
            device_id={"tensor": other},
            device_id_type=MESH,
        )

    def mixed_out(j):
        return pltpu.make_async_copy(mixer_ref.at[:, lanes_of(j)], mixer_hbm.at[:, lanes_of(j)], mx_out.at[j])

    def attended_out(g):
        lanes = pl.ds(pl.multiple_of(g * members * HEAD_DIM, HEAD_DIM), members * HEAD_DIM)
        return pltpu.make_async_copy(attended_ref.at[:, lanes], attended_hbm.at[:, lanes], at_out.at[g])

    def weight_out(j):
        return pltpu.make_async_remote_copy(
            src_ref=w_ref.at[lanes_of(j), pl.ds(pl.multiple_of(other * q_cols, CHUNK), q_cols)],
            dst_ref=w_other.at[j],
            send_sem=wt_send.at[j],
            recv_sem=wt_recv.at[j],
            device_id={"tensor": other},
            device_id_type=MESH,
        )

    def weight_in(j):
        return pltpu.make_async_copy(
            w_ref.at[lanes_of(j), pl.ds(pl.multiple_of(core * q_cols, CHUNK), q_cols)],
            w_own.at[j],
            wt_own.at[j],
        )

    def start_weights():
        @pl.loop(0, chunks)
        def _(j):
            weight_in(j).start()
            weight_out(j).start()

    @pl.when(has_left)
    def _():
        @pl.when(has_right)
        def _():
            for g in range(groups):

                @pl.when(passes(g))
                def _(g=g):
                    pass_own(0, g).start()

        @pl.when(last)
        def _():
            for which in range(2):
                lend(which).start()

        start_weights()

    row = lax.broadcasted_iota(jnp.int32, (length, length), 0)
    col = lax.broadcasted_iota(jnp.int32, (length, length), 1)
    same = (row // BLOCK) == (col // BLOCK)
    loads[0].wait()
    loads[1].wait()
    up_to = jnp.where((row <= col) & ((row // half) == (col // half)), 1.0, 0.0).astype(BF16)
    run = dot_left(ld_ref[...], up_to) * LOG2E
    ends = jnp.concatenate(
        [
            jnp.broadcast_to(run[:, half - 1 : half], (run.shape[0], half)),
            jnp.broadcast_to(run[:, length - 1 : length], (run.shape[0], half)),
        ],
        axis=1,
    )
    steps = dt_ref[...]
    grow = jnp.exp2(run)
    inject = jnp.exp2(ends - run) * steps
    adjusted = run - jnp.log(steps) * LOG2E
    for j in range(chunks):
        part = slice(j * per, (j + 1) * per)
        rows_run[j, 0:per, :] = run[part]
        rows_run[j, per : 2 * per, :] = grow[part]
        rows_run[j, 2 * per : 3 * per, :] = inject[part]
        rows_run[j, 3 * per : 4 * per, :] = inject[part]
        rows_adj[j] = adjusted[part]
    for j in range(chunks):
        cols_run[j] = jnp.transpose(rows_run[j])
    loads[2].wait()
    loads[3].wait()
    bt[...] = jnp.transpose(b_ref[...].astype(F32)).astype(BF16)
    for s in range(2):
        part = slice(s * half, (s + 1) * half)
        gram[s] = jnp.where(
            row[:half, :half] >= col[:half, :half],
            lax.dot_general(c_ref[part, :], b_ref[part, :], NT, preferred_element_type=F32),
            0.0,
        )
    first = lax.broadcasted_iota(jnp.int32, (1, 128), 1) < HEAD_P
    loads[4].wait()
    loads[5].wait()
    second = (me == 1) & has_right
    later = (me >= 2) & has_right
    stride = chunks // groups

    @pl.when(~has_left)
    def _():
        pl.semaphore_wait(barrier, peers)
        start_weights()

    def spread(table, at):
        return jnp.concatenate(
            [
                jnp.where(first, table[:, at + 2 * p : at + 2 * p + 1], table[:, at + 2 * p + 1 : at + 2 * p + 2])
                for p in range(pairs)
            ],
            axis=1,
        )

    def own_part(j, s):
        return own[2 * j + s]

    def send_state(j, entering):
        keep = spread(cols_run[j, length - 1 : length, :], per)
        high, packed, unit = encode(keep * entering + own_part(j, 1))
        code[j, 0:STATE, :] = high
        code[j, STATE : STATE + STATE // 4, :] = packed
        scale[j] = unit
        for copy in state_copies(j):
            copy.start()

    @pl.loop(0, chunks)
    def _(j):
        weighted = x_ref[:, lanes_of(j)].astype(F32) * spread(cols_run[j], 2 * per)

        def keep_part(s):
            own[2 * j + s] = dot_right(bt[:, s * half : (s + 1) * half], weighted[s * half : (s + 1) * half])

        keep_part(0)

        @pl.when(has_right)
        def _():
            keep_part(1)

        @pl.when(~has_left & has_right)
        def _():
            send_state(j, own_part(j, 0))

        for g in range(groups):

            @pl.when(later & (j == g * stride))
            def _(g=g):
                forward(0, 1, g)

    @pl.when(~has_left & has_right)
    def _():
        for g in range(groups):
            pass_own(0, g).start()
            pass_own(1, g).start()

    def inside(j):
        runs = cols_run[j]
        adj = rows_adj[j]
        for p in range(pairs):
            lanes = pl.ds(pl.multiple_of(j * CHUNK + p * 128, 128), 128)
            for s in range(2):
                part = slice(s * half, (s + 1) * half)
                x_own = x_ref[part, lanes]
                x_wide = x_own.astype(F32)
                pieces = []
                for m in range(2):
                    a = 2 * p + m
                    weight = gram[s] * jnp.exp2(jnp.minimum(runs[part, a : a + 1] - adj[a : a + 1, part], 0.0))
                    pieces.append(split(weight))
                both = jnp.concatenate(
                    [
                        jnp.where(first, x_wide, 0.0).astype(BF16),
                        jnp.where(first, 0.0, x_wide).astype(BF16),
                    ],
                    axis=0,
                )
                high, mid, low = (jnp.concatenate([pieces[0][i], pieces[1][i]], axis=1) for i in range(3))
                gain = jnp.where(first, skip_ref[j * per + 2 * p], skip_ref[j * per + 2 * p + 1])
                acc[2 * j + s, :, p * 128 : (p + 1) * 128] = (dot(high, both) + (dot(mid, both) + dot(low, both))) + gain * x_wide

    for slot in range(n):

        @pl.when(slot <= me)
        def _(slot=slot):
            for i in range(blocks):
                for m in range(blocks):
                    seen = mask_ref[me * blocks + i, (me - slot) * blocks + m] == 1
                    bias[slot, m * BLOCK : (m + 1) * BLOCK, i * BLOCK : (i + 1) * BLOCK] = jnp.full(
                        (BLOCK, BLOCK), jnp.where(seen, 0.0, NEGATIVE), F32
                    )

    @pl.when(helper)
    def _():
        for slot in range(n):
            for i in range(blocks):
                for m in range(blocks):
                    seen = mask_ref[(me + 1) * blocks + i, (me + 1 - slot) * blocks + m] == 1
                    bias[n + slot, m * BLOCK : (m + 1) * BLOCK, i * BLOCK : (i + 1) * BLOCK] = jnp.full(
                        (BLOCK, BLOCK), jnp.where(seen, 0.0, NEGATIVE), F32
                    )
        bias[n] = jnp.where(row <= col, jnp.where(same, 0.0, bias[n]), NEGATIVE)

    bias[0] = jnp.where(row <= col, jnp.where(same, 0.0, bias[0]), NEGATIVE)
    q_acc[...] = jnp.zeros_like(q_acc)
    total[...] = jnp.zeros_like(total)
    top[...] = jnp.full_like(top, NEGATIVE)

    ahead = jnp.where(me >= 2, chunks, 0)

    @pl.loop(0, ahead)
    def _(j):
        inside(j)

    def add_query(j):
        for t in range(0, q_cols, 512):
            q_acc[:, t : t + 512] += dot(mixer_ref[:, lanes_of(j)], w_own[j, :, t : t + 512])

    def add_other(j):
        mixed_copy(j).wait_recv()
        weight_out(j).wait_recv()
        for t in range(0, q_cols, 512):
            q_acc[:, t : t + 512] += dot(mixed_other[j], w_other[j, :, t : t + 512])

    @pl.when(~has_left)
    def _():
        code_in[...] = jnp.zeros_like(code_in)
        scale_in[...] = jnp.zeros_like(scale_in)

    lag = jnp.where(second, chunks, 0)

    def states_at(j):
        arrived = decode(code_in[j, 0:STATE, :], code_in[j, STATE : STATE + STATE // 4, :], scale_in[j])
        return arrived, spread(cols_run[j, half - 1 : half, :], per) * arrived + own_part(j, 0)

    def relay(j):
        @pl.when(has_left)
        def _():
            for copy in state_copies(j):
                copy.wait_recv()

        @pl.when(middle)
        def _():
            send_state(j, states_at(j)[1])

        @pl.when(later & (j == chunks - 1))
        def _():
            for g in range(groups):

                @pl.when(passes(g))
                def _(g=g):
                    pass_own(1, g).start()

        @pl.when(j >= ahead)
        def _():
            inside(j)

    def mix(j):
        for g in range(groups):

            @pl.when(second & (j == g * stride))
            def _(g=g):
                forward(0, 1, g)
                pass_own(1, g).start()
                forward(1, 1, g)

        arrived, entering = states_at(j)
        runs = cols_run[j]
        for s in range(2):
            part = slice(s * half, (s + 1) * half)
            carried = dot_right(c_ref[part, :], arrived if s == 0 else entering)
            grown = spread(runs[part], per)
            for p in range(pairs):
                lanes = slice(p * 128, (p + 1) * 128)
                out_lanes = pl.ds(pl.multiple_of(j * CHUNK + p * 128, 128), 128)
                y = acc[2 * j + s, :, lanes] + carried[:, lanes] * grown[:, lanes]
                squares = y * y
                left = jnp.sum(jnp.where(first, squares, 0.0), axis=1, keepdims=True)
                right = jnp.sum(jnp.where(first, 0.0, squares), axis=1, keepdims=True)
                mean = jnp.where(first, left, right) * (1.0 / HEAD_P)
                mixer_ref[part, out_lanes] = (y * lax.rsqrt(mean + 1e-05) * gain_ref[:, out_lanes]).astype(BF16)
        mixed_copy(j).start()
        mixed_out(j).start()
        weight_in(j).wait()
        add_query(j)

        @pl.when(j >= 1)
        def _():
            add_other(j - 1)

    @pl.loop(0, chunks + lag)
    def _(t):
        @pl.when(t < chunks)
        def _():
            relay(t)

        @pl.when(t >= lag)
        def _():
            mix(t - lag)

    add_other(chunks - 1)
    for h in range(heads):
        q_all[h] = q_acc[:, h * HEAD_DIM : (h + 1) * HEAD_DIM].astype(BF16)

    @pl.when(last)
    def _():
        for member in range(members):
            lend_query(member).start()

    for which in range(2):
        for g in range(groups):
            own_load(which, g).wait()
    unit_scale = HEAD_DIM ** (-0.5) * LOG2E

    def head_lanes(h):
        return pl.ds(pl.multiple_of(h * HEAD_DIM, HEAD_DIM), HEAD_DIM)

    def by_eight(table):
        return table.reshape(length // 8, 8, length)

    def arrive_values(slot, g):
        @pl.when(last & (slot >= 1))
        def _():
            arrive(1, slot, g)

    @pl.loop(0, jnp.where(helper, groups + 1, jnp.where(last, groups - 1, groups)))
    def _(unit):
        lending = helper & (unit == lent)
        g = jnp.minimum(unit, groups - 1)
        base = jnp.where(lending, heads, g * members)
        end = jnp.where(lending, me + 1, me)

        def held(slot):
            return jnp.where(lending, jnp.where(slot == 0, n, slot - 1), slot)

        def scores_of(slot, member):
            keys = kv[0, held(slot), g]
            scores = lax.dot_general(keys, q_all[base + member], NT, preferred_element_type=F32)
            return by_eight(scores + bias[jnp.where(lending, n + slot, slot)])

        def weigh(slot):
            for member in range(members):
                h = base + member
                part = jnp.exp2((scores_of(slot, member) - top[h]) * unit_scale)
                total[h] += jnp.sum(part, axis=0)
                weights[slot % 2, member] = part.reshape(length, length).astype(BF16)

        def attend(slot):
            values = jnp.transpose(kv[1, held(slot), g].astype(F32)).astype(BF16)
            for member in range(members):
                h = base + member
                acc[h] = jnp.where(slot == 0, 0.0, acc[h]) + dot(values, weights[slot % 2, member])

        @pl.when(later & (unit < groups))
        def _():
            @pl.loop(2, me + 1)
            def _(slot):
                forward(0, slot, g)

            @pl.loop(1, me + 1)
            def _(slot):
                forward(1, slot, g)

        @pl.when(lending)
        def _():
            for which in range(2):
                lend(which).wait_recv()
            for member in range(members):
                lend_query(member).wait_recv()

        @pl.loop(0, end + 1)
        def _(slot):
            @pl.when(last & (slot >= 1))
            def _():
                arrive(0, slot, g)

            for member in range(members):
                h = base + member
                top[h] = jnp.maximum(top[h], jnp.max(scores_of(slot, member), axis=0))

        for member in range(members):
            h = base + member
            top[h] = jnp.broadcast_to(jnp.max(top[h], axis=0, keepdims=True), top.shape[1:])
        weigh(0)

        @pl.loop(1, end + 1)
        def _(slot):
            arrive_values(slot - 1, g)
            weigh(slot)
            attend(slot - 1)

        arrive_values(end, g)
        attend(end)
        for member in range(members):
            h = base + member
            out = jnp.transpose(acc[h] / jnp.sum(total[h], axis=0, keepdims=True)).astype(BF16)

            @pl.when(lending)
            def _(member=member, out=out):
                answer[member] = out
                give_back(member).start()

            @pl.when(~lending)
            def _(h=h, out=out):
                attended_ref[:, head_lanes(h)] = out

        @pl.when(~lending)
        def _():
            attended_out(g).start()

    @pl.when(last)
    def _():
        for member in range(members):
            give_back(member).wait_recv()
        attended_out(lent).start()
        for which in range(2):
            lend(which).wait_send()
        for member in range(members):
            lend_query(member).wait_send()

    @pl.when(helper)
    def _():
        for member in range(members):
            give_back(member).wait_send()

    @pl.loop(0, groups)
    def _(g):
        attended_out(g).wait()

    @pl.loop(0, chunks)
    def _(j):
        mixed_copy(j).wait_send()
        mixed_out(j).wait()
        weight_out(j).wait_send()

        @pl.when(has_right)
        def _():
            for copy in state_copies(j):
                copy.wait_send()

    @pl.loop(0, n)
    def _(slot):
        @pl.when((slot <= me) & has_right)
        def _():
            for which in range(2):
                for g in range(groups):

                    @pl.when(passes(g))
                    def _(which=which, g=g):
                        pass_on(which, slot, g).wait_send()


def hand_on(mixer_ref, attended_ref, mixer_out, attended_out, held, loads, stores):
    parts = held.shape[1]
    rows = held.shape[2]
    refs = ((mixer_ref, mixer_out), (attended_ref, attended_out))

    def load(k, i):
        return pltpu.make_async_copy(refs[k][0].at[pl.ds(i * rows, rows)], held.at[k, i], loads.at[k, i])

    def store(k, i):
        return pltpu.make_async_copy(held.at[k, i], refs[k][1].at[pl.ds(i * rows, rows)], stores.at[k, i])

    every = [(k, i) for k in range(2) for i in range(parts)]
    for at in every:
        load(*at).start()
    for at in every:
        load(*at).wait()
        store(*at).start()
    for at in every:
        store(*at).wait()


def on_device(
    ssm_input,
    input_map,
    output_map,
    step_size,
    log_decay,
    skip_gain,
    norm_gain,
    query_weight,
    key_states,
    value_states,
    block_mask,
):
    n = lax.axis_size("context")
    length, channels = ssm_input.shape
    q_cols = query_weight.shape[1] // lax.axis_size("tensor")
    chunks = channels // CHUNK
    heads = q_cols // HEAD_DIM
    per = CHUNK // HEAD_P
    groups = key_states.shape[1] // HEAD_DIM
    smem = pl.BlockSpec(memory_space=pltpu.SMEM)
    hbm = pl.BlockSpec(memory_space=pltpu.HBM)
    far = pl.BlockSpec(memory_space=pl.ANY)
    dma = pltpu.SemaphoreType.DMA
    outs = (
        jax.ShapeDtypeStruct((length, channels), BF16),
        jax.ShapeDtypeStruct((length, q_cols), BF16),
    )
    coded = STATE + STATE // 4
    results = pl.pallas_call(
        functools.partial(kernel, n),
        out_shape=outs,
        in_specs=[smem, smem] + [hbm] * 9,
        out_specs=(hbm, hbm),
        scratch_shapes=[
            pltpu.VMEM((length, channels), BF16),
            pltpu.VMEM((length, q_cols), BF16),
            pltpu.VMEM((length, channels), BF16),
            pltpu.VMEM((length, STATE), BF16),
            pltpu.VMEM((length, STATE), BF16),
            pltpu.VMEM(step_size.shape, F32),
            pltpu.VMEM(log_decay.shape, F32),
            pltpu.VMEM((1, channels), F32),
            pltpu.VMEM((2, n + 1, groups, length, HEAD_DIM), BF16),
            pltpu.VMEM((chunks, CHUNK, q_cols), BF16),
            pltpu.VMEM((chunks, CHUNK, q_cols), BF16),
            pltpu.VMEM((STATE, length), BF16),
            pltpu.VMEM((2, length // 2, length // 2), F32),
            pltpu.VMEM((chunks, 4 * per, length), F32),
            pltpu.VMEM((chunks, length, 4 * per), F32),
            pltpu.VMEM((chunks, per, length), F32),
            pltpu.VMEM((chunks, coded, CHUNK), jnp.int16),
            pltpu.VMEM((chunks, coded, CHUNK), jnp.int16),
            pltpu.VMEM((chunks, 1, CHUNK), F32),
            pltpu.VMEM((chunks, 1, CHUNK), F32),
            pltpu.VMEM((chunks, length, CHUNK), BF16),
            pltpu.VMEM((length, q_cols), F32),
            pltpu.VMEM((heads + heads // groups, length, HEAD_DIM), BF16),
            pltpu.VMEM((2 * n, length, length), F32),
            pltpu.VMEM((2, heads // groups, length, length), BF16),
            pltpu.VMEM((heads + heads // groups, 8, length), F32),
            pltpu.VMEM((heads + heads // groups, 8, length), F32),
            pltpu.VMEM((max(heads + heads // groups, 2 * chunks), HEAD_DIM, length), F32),
            pltpu.VMEM((2 * chunks, STATE, CHUNK), F32),
            dma((6,)),
            dma((2, groups)),
            dma((2, n, groups)),
            dma((2, n + 1, groups)),
        ]
        + [dma((chunks,))] * 10
        + [dma((groups,)), pltpu.VMEM((heads // groups, length, HEAD_DIM), BF16), dma((2,)), dma((2,))]
        + [dma((heads // groups,))] * 4,
        compiler_params=pltpu.CompilerParams(
            collective_id=0, has_side_effects=True, vmem_limit_bytes=56 * 1024 * 1024
        ),
        name="mixer_attention",
    )(
        block_mask,
        skip_gain,
        ssm_input,
        input_map,
        output_map,
        step_size,
        log_decay,
        norm_gain.reshape(1, channels),
        query_weight,
        key_states,
        value_states,
    )
    return pl.pallas_call(
        hand_on,
        out_shape=outs,
        in_specs=[far, far],
        out_specs=[far, far],
        scratch_shapes=[pltpu.VMEM((2, 4, length // 4, channels), BF16), dma((2, 4)), dma((2, 4))],
        name="hand_on",
    )(*results)


def solution(mesh):
    return jax.shard_map(
        on_device,
        mesh=mesh,
        in_specs=(
            P(("dp", "context"), "tensor"),
            P(("dp", "context"), None),
            P(("dp", "context"), None),
            P("tensor", ("dp", "context")),
            P("tensor", ("dp", "context")),
            P("tensor"),
            P("tensor"),
            P("tensor", None),
            P(("dp", "context"), "tensor"),
            P(("dp", "context"), "tensor"),
            P("dp", None),
        ),
        out_specs=(P(("dp", "context"), "tensor"), P(("dp", "context"), "tensor")),
        check_vma=False,
    )
```

```python
import functools

import jax
import jax.numpy as jnp
from jax import lax
from jax.experimental import pallas as pl
from jax.experimental.pallas import tpu as pltpu
from jax.sharding import PartitionSpec as P

HEAD_P = 64
STATE = 128
HEAD_DIM = 128
BLOCK = 128
CHUNK = 256
NEGATIVE = -1e30
LOG2E = 1.4426950408889634
LEVELS = 524287.0
MESH = pl.DeviceIdType.MESH
F32 = jnp.float32
BF16 = jnp.bfloat16
NT = (((1,), (1,)), ((), ()))


def split(wide):
    high = wide.astype(BF16)
    rest = wide - high.astype(F32)
    middle = rest.astype(BF16)
    return high, middle, (rest - middle.astype(F32)).astype(BF16)


def dot(a, b):
    return jnp.dot(a, b, preferred_element_type=F32)


def dot_left(wide, narrow):
    high, middle, low = split(wide)
    return dot(high, narrow) + (dot(middle, narrow) + dot(low, narrow))


def dot_right(narrow, wide):
    high, middle, low = split(wide)
    return dot(narrow, high) + (dot(narrow, middle) + dot(narrow, low))


def encode(wide):
    largest = jnp.maximum(jnp.max(jnp.abs(wide), axis=0, keepdims=True), 1e-30)
    whole = jnp.round(wide * (LEVELS / largest)).astype(jnp.int32)
    quarter = wide.shape[0] // 4
    low = whole & 15
    packed = low[:quarter]
    for i in range(1, 4):
        packed = packed | (low[i * quarter : (i + 1) * quarter] << (4 * i))
    return (whole >> 4).astype(jnp.int16), (packed - 32768).astype(jnp.int16), largest * (1.0 / LEVELS)


def decode(high, packed, scale):
    packed = packed.astype(jnp.int32) + 32768
    low = jnp.concatenate([(packed >> (4 * i)) & 15 for i in range(4)], axis=0)
    return (high.astype(jnp.int32) * 16 + low).astype(F32) * scale


def kernel(
    n,
    mask_ref,
    skip_ref,
    x_hbm,
    b_hbm,
    c_hbm,
    dt_hbm,
    ld_hbm,
    gain_hbm,
    w_ref,
    k_hbm,
    v_hbm,
    mixer_hbm,
    attended_hbm,
    mixer_ref,
    attended_ref,
    x_ref,
    b_ref,
    c_ref,
    dt_ref,
    ld_ref,
    gain_ref,
    kv,
    w_own,
    w_other,
    bt,
    gram,
    rows_run,
    cols_run,
    rows_adj,
    code,
    code_in,
    scale,
    scale_in,
    mixed_other,
    q_acc,
    q_all,
    bias,
    rows_bias,
    weights,
    top,
    total,
    acc,
    own,
    ld_sem,
    own_sem,
    kv_send,
    kv_recv,
    st_send,
    st_recv,
    sc_send,
    sc_recv,
    mx_send,
    mx_recv,
    wt_send,
    wt_recv,
    wt_own,
    mx_out,
    at_out,
    answer,
    lk_send,
    lk_recv,
    lq_send,
    lq_recv,
    an_send,
    an_recv,
):
    me = lax.axis_index("context")
    core = lax.axis_index("tensor")
    other = 1 - core
    length = x_ref.shape[0]
    half = length // 2
    chunks = x_ref.shape[1] // CHUNK
    per = CHUNK // HEAD_P
    pairs = CHUNK // 128
    q_cols = w_own.shape[2]
    has_left = me > 0
    has_right = me < n - 1
    helper = me == n - 2
    last = me == n - 1
    middle = has_left & has_right
    heads = q_cols // HEAD_DIM
    groups = kv.shape[2]
    members = heads // groups
    blocks = length // BLOCK

    barrier = pltpu.get_barrier_semaphore()
    pl.semaphore_signal(barrier, inc=1, device_id={"tensor": other}, device_id_type=MESH)

    @pl.when(has_left)
    def _():
        pl.semaphore_signal(barrier, inc=1, device_id={"context": me - 1}, device_id_type=MESH)

    @pl.when(has_right)
    def _():
        pl.semaphore_signal(barrier, inc=1, device_id={"context": me + 1}, device_id_type=MESH)

    loads = [
        pltpu.make_async_copy(src, dst, ld_sem.at[i])
        for i, (src, dst) in enumerate(
            (
                (ld_hbm, ld_ref),
                (dt_hbm, dt_ref),
                (b_hbm, b_ref),
                (c_hbm, c_ref),
                (x_hbm, x_ref),
                (gain_hbm, gain_ref),
            )
        )
    ]
    for load in loads:
        load.start()

    hbm = (k_hbm, v_hbm)

    def fixed_lanes(g):
        return pl.ds(g * HEAD_DIM, HEAD_DIM)

    def own_load(which, g):
        return pltpu.make_async_copy(hbm[which].at[:, fixed_lanes(g)], kv.at[which, 0, g], own_sem.at[which, g])

    for which in range(2):
        for g in range(groups):
            own_load(which, g).start()

    peers = 1 + has_left.astype(jnp.int32) + has_right.astype(jnp.int32)

    @pl.when(has_left)
    def _():
        pl.semaphore_wait(barrier, peers)

    def pass_own(which, g):
        return pltpu.make_async_remote_copy(
            src_ref=hbm[which].at[:, fixed_lanes(g)],
            dst_ref=kv.at[which, 1, g],
            send_sem=kv_send.at[which, 0, g],
            recv_sem=kv_recv.at[which, 1, g],
            device_id={"context": me + 1},
            device_id_type=MESH,
        )

    def pass_on(which, slot, g):
        return pltpu.make_async_remote_copy(
            src_ref=kv.at[which, slot, g],
            dst_ref=kv.at[which, slot + 1, g],
            send_sem=kv_send.at[which, slot, g],
            recv_sem=kv_recv.at[which, slot + 1, g],
            device_id={"context": me + 1},
            device_id_type=MESH,
        )

    def arrive(which, slot, g):
        pltpu.make_async_remote_copy(
            src_ref=kv.at[which, slot - 1, g],
            dst_ref=kv.at[which, slot, g],
            send_sem=kv_send.at[which, slot - 1, g],
            recv_sem=kv_recv.at[which, slot, g],
            device_id={"context": me - 1},
            device_id_type=MESH,
        ).wait_recv()

    lent = groups - 1

    def passes(g):
        return ~helper | (g != lent)

    def forward(which, slot, g):
        arrive(which, slot, g)

        @pl.when(passes(g))
        def _():
            pass_on(which, slot, g).start()

    def lend(which):
        return pltpu.make_async_remote_copy(
            src_ref=hbm[which].at[:, fixed_lanes(lent)],
            dst_ref=kv.at[which, n, lent],
            send_sem=lk_send.at[which],
            recv_sem=lk_recv.at[which],
            device_id={"context": me - 1},
            device_id_type=MESH,
        )

    def lend_query(member):
        return pltpu.make_async_remote_copy(
            src_ref=q_all.at[lent * members + member],
            dst_ref=q_all.at[heads + member],
            send_sem=lq_send.at[member],
            recv_sem=lq_recv.at[member],
            device_id={"context": me - 1},
            device_id_type=MESH,
        )

    def give_back(member):
        return pltpu.make_async_remote_copy(
            src_ref=answer.at[member],
            dst_ref=attended_ref.at[:, fixed_lanes(lent * members + member)],
            send_sem=an_send.at[member],
            recv_sem=an_recv.at[member],
            device_id={"context": me + 1},
            device_id_type=MESH,
        )

    def state_copies(j):
        return [
            pltpu.make_async_remote_copy(
                src_ref=src.at[j],
                dst_ref=dst.at[j],
                send_sem=send.at[j],
                recv_sem=recv.at[j],
                device_id={"context": me + 1},
                device_id_type=MESH,
            )
            for src, dst, send, recv in ((scale, scale_in, sc_send, sc_recv), (code, code_in, st_send, st_recv))
        ]

    def lanes_of(j):
        return pl.ds(pl.multiple_of(j * CHUNK, CHUNK), CHUNK)

    def mixed_copy(j):
        return pltpu.make_async_remote_copy(
            src_ref=mixer_ref.at[:, lanes_of(j)],
            dst_ref=mixed_other.at[j],
            send_sem=mx_send.at[j],
            recv_sem=mx_recv.at[j],
            device_id={"tensor": other},
            device_id_type=MESH,
        )

    def mixed_out(j):
        return pltpu.make_async_copy(mixer_ref.at[:, lanes_of(j)], mixer_hbm.at[:, lanes_of(j)], mx_out.at[j])

    def attended_out(g):
        lanes = pl.ds(pl.multiple_of(g * members * HEAD_DIM, HEAD_DIM), members * HEAD_DIM)
        return pltpu.make_async_copy(attended_ref.at[:, lanes], attended_hbm.at[:, lanes], at_out.at[g])

    def weight_out(j):
        return pltpu.make_async_remote_copy(
            src_ref=w_ref.at[lanes_of(j), pl.ds(pl.multiple_of(other * q_cols, CHUNK), q_cols)],
            dst_ref=w_other.at[j],
            send_sem=wt_send.at[j],
            recv_sem=wt_recv.at[j],
            device_id={"tensor": other},
            device_id_type=MESH,
        )

    def weight_in(j):
        return pltpu.make_async_copy(
            w_ref.at[lanes_of(j), pl.ds(pl.multiple_of(core * q_cols, CHUNK), q_cols)],
            w_own.at[j],
            wt_own.at[j],
        )

    def start_weights():
        @pl.loop(0, chunks)
        def _(j):
            weight_in(j).start()
            weight_out(j).start()

    @pl.when(has_left)
    def _():
        @pl.when(has_right)
        def _():
            for g in range(groups):

                @pl.when(passes(g))
                def _(g=g):
                    pass_own(0, g).start()

        @pl.when(last)
        def _():
            for which in range(2):
                lend(which).start()

        start_weights()

    row = lax.broadcasted_iota(jnp.int32, (length, length), 0)
    col = lax.broadcasted_iota(jnp.int32, (length, length), 1)
    same = (row // BLOCK) == (col // BLOCK)
    loads[0].wait()
    loads[1].wait()
    up_to = jnp.where((row <= col) & ((row // half) == (col // half)), 1.0, 0.0).astype(BF16)
    run = dot_left(ld_ref[...], up_to) * LOG2E
    ends = jnp.concatenate(
        [
            jnp.broadcast_to(run[:, half - 1 : half], (run.shape[0], half)),
            jnp.broadcast_to(run[:, length - 1 : length], (run.shape[0], half)),
        ],
        axis=1,
    )
    steps = dt_ref[...]
    grow = jnp.exp2(run)
    inject = jnp.exp2(ends - run) * steps
    adjusted = run - jnp.log(steps) * LOG2E
    for j in range(chunks):
        part = slice(j * per, (j + 1) * per)
        rows_run[j, 0:per, :] = run[part]
        rows_run[j, per : 2 * per, :] = grow[part]
        rows_run[j, 2 * per : 3 * per, :] = inject[part]
        rows_run[j, 3 * per : 4 * per, :] = inject[part]
        rows_adj[j] = adjusted[part]
    for j in range(chunks):
        cols_run[j] = jnp.transpose(rows_run[j])
    loads[2].wait()
    loads[3].wait()
    bt[...] = jnp.transpose(b_ref[...].astype(F32)).astype(BF16)
    for s in range(2):
        part = slice(s * half, (s + 1) * half)
        gram[s] = jnp.where(
            row[:half, :half] >= col[:half, :half],
            lax.dot_general(c_ref[part, :], b_ref[part, :], NT, preferred_element_type=F32),
            0.0,
        )
    first = lax.broadcasted_iota(jnp.int32, (1, 128), 1) < HEAD_P
    loads[4].wait()
    loads[5].wait()
    second = (me == 1) & has_right
    later = (me >= 2) & has_right
    stride = chunks // groups

    @pl.when(~has_left)
    def _():
        pl.semaphore_wait(barrier, peers)
        start_weights()

    def spread(table, at):
        return jnp.concatenate(
            [
                jnp.where(first, table[:, at + 2 * p : at + 2 * p + 1], table[:, at + 2 * p + 1 : at + 2 * p + 2])
                for p in range(pairs)
            ],
            axis=1,
        )

    def own_part(j, s):
        return own[2 * j + s]

    def send_state(j, entering):
        keep = spread(cols_run[j, length - 1 : length, :], per)
        high, packed, unit = encode(keep * entering + own_part(j, 1))
        code[j, 0:STATE, :] = high
        code[j, STATE : STATE + STATE // 4, :] = packed
        scale[j] = unit
        for copy in state_copies(j):
            copy.start()

    @pl.loop(0, chunks)
    def _(j):
        weighted = x_ref[:, lanes_of(j)].astype(F32) * spread(cols_run[j], 2 * per)

        def keep_part(s):
            own[2 * j + s] = dot_right(bt[:, s * half : (s + 1) * half], weighted[s * half : (s + 1) * half])

        keep_part(0)

        @pl.when(has_right)
        def _():
            keep_part(1)

        @pl.when(~has_left & has_right)
        def _():
            send_state(j, own_part(j, 0))

        for g in range(groups):

            @pl.when(later & (j == g * stride))
            def _(g=g):
                forward(0, 1, g)

    @pl.when(~has_left & has_right)
    def _():
        for g in range(groups):
            pass_own(0, g).start()
            pass_own(1, g).start()

    def inside(j):
        runs = cols_run[j]
        adj = rows_adj[j]
        for p in range(pairs):
            lanes = pl.ds(pl.multiple_of(j * CHUNK + p * 128, 128), 128)
            for s in range(2):
                part = slice(s * half, (s + 1) * half)
                x_own = x_ref[part, lanes]
                x_wide = x_own.astype(F32)
                pieces = []
                for m in range(2):
                    a = 2 * p + m
                    weight = gram[s] * jnp.exp2(jnp.minimum(runs[part, a : a + 1] - adj[a : a + 1, part], 0.0))
                    pieces.append(split(weight))
                both = jnp.concatenate(
                    [
                        jnp.where(first, x_wide, 0.0).astype(BF16),
                        jnp.where(first, 0.0, x_wide).astype(BF16),
                    ],
                    axis=0,
                )
                high, mid, low = (jnp.concatenate([pieces[0][i], pieces[1][i]], axis=1) for i in range(3))
                gain = jnp.where(first, skip_ref[j * per + 2 * p], skip_ref[j * per + 2 * p + 1])
                acc[2 * j + s, :, p * 128 : (p + 1) * 128] = (dot(high, both) + (dot(mid, both) + dot(low, both))) + gain * x_wide

    def table(owner, slot, at):
        for i in range(blocks):
            for m in range(blocks):
                seen = mask_ref[owner * blocks + i, (owner - slot) * blocks + m] == 1
                rows_bias[at, m, :, i * BLOCK : (i + 1) * BLOCK] = jnp.full(
                    (8, BLOCK), jnp.where(seen, 0.0, NEGATIVE), F32
                )

    def diagonal(at, which):
        rows = [jnp.broadcast_to(rows_bias[at, m, 0:1, :], (BLOCK, length)) for m in range(blocks)]
        bias[which] = jnp.where(row <= col, jnp.where(same, 0.0, jnp.concatenate(rows, axis=0)), NEGATIVE)

    for slot in range(n):

        @pl.when(slot <= me)
        def _(slot=slot):
            table(me, slot, slot)

    diagonal(0, 0)

    @pl.when(helper)
    def _():
        for slot in range(n):
            table(me + 1, slot, n + slot)
        diagonal(n, 1)

    q_acc[...] = jnp.zeros_like(q_acc)
    total[...] = jnp.zeros_like(total)
    top[...] = jnp.full_like(top, NEGATIVE)

    @pl.when(later)
    def _():
        pass_own(1, 0).start()

    ahead = jnp.where(me >= 2, chunks, 0)

    @pl.loop(0, ahead)
    def _(j):
        inside(j)

    def add_query(j):
        for t in range(0, q_cols, 512):
            q_acc[:, t : t + 512] += dot(mixer_ref[:, lanes_of(j)], w_own[j, :, t : t + 512])

    def add_other(j):
        mixed_copy(j).wait_recv()
        weight_out(j).wait_recv()
        for t in range(0, q_cols, 512):
            q_acc[:, t : t + 512] += dot(mixed_other[j], w_other[j, :, t : t + 512])

    @pl.when(~has_left)
    def _():
        code_in[...] = jnp.zeros_like(code_in)
        scale_in[...] = jnp.zeros_like(scale_in)

    lag = jnp.where(second, chunks, 0)

    def states_at(j):
        arrived = decode(code_in[j, 0:STATE, :], code_in[j, STATE : STATE + STATE // 4, :], scale_in[j])
        return arrived, spread(cols_run[j, half - 1 : half, :], per) * arrived + own_part(j, 0)

    def relay(j):
        @pl.when(has_left)
        def _():
            for copy in state_copies(j):
                copy.wait_recv()

        @pl.when(middle)
        def _():
            send_state(j, states_at(j)[1])

        for g in range(1, groups):

            @pl.when(later & (j == (chunks // 2 - 1 if g == 1 else chunks - 1)) & passes(g))
            def _(g=g):
                pass_own(1, g).start()

        @pl.when(later & (j == chunks - 1))
        def _():
            forward(0, 2, 0)

        @pl.when(j >= ahead)
        def _():
            inside(j)

    def mix(j):
        for g in range(groups):

            @pl.when(second & (j == g * stride))
            def _(g=g):
                forward(0, 1, g)
                pass_own(1, g).start()
                forward(1, 1, g)

        arrived, entering = states_at(j)
        runs = cols_run[j]
        for s in range(2):
            part = slice(s * half, (s + 1) * half)
            carried = dot_right(c_ref[part, :], arrived if s == 0 else entering)
            grown = spread(runs[part], per)
            for p in range(pairs):
                lanes = slice(p * 128, (p + 1) * 128)
                out_lanes = pl.ds(pl.multiple_of(j * CHUNK + p * 128, 128), 128)
                y = acc[2 * j + s, :, lanes] + carried[:, lanes] * grown[:, lanes]
                squares = y * y
                left = jnp.sum(jnp.where(first, squares, 0.0), axis=1, keepdims=True)
                right = jnp.sum(jnp.where(first, 0.0, squares), axis=1, keepdims=True)
                mean = jnp.where(first, left, right) * (1.0 / HEAD_P)
                mixer_ref[part, out_lanes] = (y * lax.rsqrt(mean + 1e-05) * gain_ref[:, out_lanes]).astype(BF16)
        mixed_copy(j).start()
        mixed_out(j).start()
        weight_in(j).wait()
        add_query(j)

        @pl.when(j >= 1)
        def _():
            add_other(j - 1)

    @pl.loop(0, chunks + lag)
    def _(t):
        @pl.when(t < chunks)
        def _():
            relay(t)

        @pl.when(t >= lag)
        def _():
            mix(t - lag)

    add_other(chunks - 1)
    for h in range(heads):
        q_all[h] = q_acc[:, h * HEAD_DIM : (h + 1) * HEAD_DIM].astype(BF16)

    @pl.when(last)
    def _():
        for member in range(members):
            lend_query(member).start()

    for which in range(2):
        for g in range(groups):
            own_load(which, g).wait()
    unit_scale = HEAD_DIM ** (-0.5) * LOG2E

    def head_lanes(h):
        return pl.ds(pl.multiple_of(h * HEAD_DIM, HEAD_DIM), HEAD_DIM)

    span = BLOCK // 8

    def by_eight(table):
        return table.reshape(length // 8, 8, length)

    def arrive_values(slot, g):
        @pl.when(last & (slot >= 1))
        def _():
            arrive(1, slot, g)

    @pl.loop(0, jnp.where(helper, groups + 1, jnp.where(last, groups - 1, groups)))
    def _(unit):
        lending = helper & (unit == lent)
        g = jnp.minimum(unit, groups - 1)
        base = jnp.where(lending, heads, g * members)
        end = jnp.where(lending, me + 1, me)

        def held(slot):
            return jnp.where(lending, jnp.where(slot == 0, n, slot - 1), slot)

        def scores_of(slot, member):
            keys = kv[0, held(slot), g]
            return by_eight(lax.dot_general(keys, q_all[base + member], NT, preferred_element_type=F32))

        def row_of(slot, m):
            return rows_bias[jnp.where(lending, n + slot, slot), m]

        def best_first():
            for member in range(members):
                h = base + member
                scores = scores_of(0, member) + by_eight(bias[lending.astype(jnp.int32)])
                top[h] = jnp.maximum(top[h], jnp.max(scores, axis=0))

        def weigh_first():
            for member in range(members):
                h = base + member
                scores = scores_of(0, member) + by_eight(bias[lending.astype(jnp.int32)])
                part = jnp.exp2((scores - top[h]) * unit_scale)
                total[h] += jnp.sum(part, axis=0)
                weights[0, member] = part.reshape(length, length).astype(BF16)

        def weigh(slot):
            for member in range(members):
                h = base + member
                scores = scores_of(slot, member)
                summed = total[h]
                for m in range(blocks):
                    shift = top[h] - row_of(slot, m)
                    part = jnp.exp2((scores[m * span : (m + 1) * span] - shift) * unit_scale)
                    summed = summed + jnp.sum(part, axis=0)
                    weights[slot % 2, member, m * BLOCK : (m + 1) * BLOCK, :] = part.reshape(BLOCK, length).astype(BF16)
                total[h] = summed

        def attend(slot):
            values = jnp.transpose(kv[1, held(slot), g].astype(F32)).astype(BF16)
            for member in range(members):
                h = base + member
                acc[h] = jnp.where(slot == 0, 0.0, acc[h]) + dot(values, weights[slot % 2, member])

        @pl.when(later & (unit < groups))
        def _():
            @pl.loop(jnp.where(unit == 0, 3, 2), me + 1)
            def _(slot):
                forward(0, slot, g)

            @pl.loop(1, me + 1)
            def _(slot):
                forward(1, slot, g)

        @pl.when(lending)
        def _():
            for which in range(2):
                lend(which).wait_recv()
            for member in range(members):
                lend_query(member).wait_recv()

        best_first()

        @pl.loop(1, end + 1)
        def _(slot):
            @pl.when(last)
            def _():
                arrive(0, slot, g)

            for member in range(members):
                h = base + member
                scores = scores_of(slot, member)
                best = top[h]
                for m in range(blocks):
                    best = jnp.maximum(best, jnp.max(scores[m * span : (m + 1) * span], axis=0) + row_of(slot, m))
                top[h] = best

        for member in range(members):
            h = base + member
            top[h] = jnp.broadcast_to(jnp.max(top[h], axis=0, keepdims=True), top.shape[1:])
        weigh_first()

        @pl.loop(1, end + 1)
        def _(slot):
            arrive_values(slot - 1, g)
            weigh(slot)
            attend(slot - 1)

        arrive_values(end, g)
        attend(end)
        for member in range(members):
            h = base + member
            out = jnp.transpose(acc[h] / jnp.sum(total[h], axis=0, keepdims=True)).astype(BF16)

            @pl.when(lending)
            def _(member=member, out=out):
                answer[member] = out
                give_back(member).start()

            @pl.when(~lending)
            def _(h=h, out=out):
                attended_ref[:, head_lanes(h)] = out

        @pl.when(~lending)
        def _():
            attended_out(g).start()

    @pl.when(last)
    def _():
        for member in range(members):
            give_back(member).wait_recv()
        attended_out(lent).start()
        for which in range(2):
            lend(which).wait_send()
        for member in range(members):
            lend_query(member).wait_send()

    @pl.when(helper)
    def _():
        for member in range(members):
            give_back(member).wait_send()

    @pl.loop(0, groups)
    def _(g):
        attended_out(g).wait()

    @pl.loop(0, chunks)
    def _(j):
        mixed_copy(j).wait_send()
        mixed_out(j).wait()
        weight_out(j).wait_send()

        @pl.when(has_right)
        def _():
            for copy in state_copies(j):
                copy.wait_send()

    @pl.loop(0, n)
    def _(slot):
        @pl.when((slot <= me) & has_right)
        def _():
            for which in range(2):
                for g in range(groups):

                    @pl.when(passes(g))
                    def _(which=which, g=g):
                        pass_on(which, slot, g).wait_send()


def hand_on(mixer_ref, attended_ref, mixer_out, attended_out, held, loads, stores):
    parts = held.shape[1]
    rows = held.shape[2]
    refs = ((mixer_ref, mixer_out), (attended_ref, attended_out))

    def load(k, i):
        return pltpu.make_async_copy(refs[k][0].at[pl.ds(i * rows, rows)], held.at[k, i], loads.at[k, i])

    def store(k, i):
        return pltpu.make_async_copy(held.at[k, i], refs[k][1].at[pl.ds(i * rows, rows)], stores.at[k, i])

    every = [(k, i) for k in range(2) for i in range(parts)]
    for at in every:
        load(*at).start()
    for at in every:
        load(*at).wait()
        store(*at).start()
    for at in every:
        store(*at).wait()


def on_device(
    ssm_input,
    input_map,
    output_map,
    step_size,
    log_decay,
    skip_gain,
    norm_gain,
    query_weight,
    key_states,
    value_states,
    block_mask,
):
    n = lax.axis_size("context")
    length, channels = ssm_input.shape
    q_cols = query_weight.shape[1] // lax.axis_size("tensor")
    chunks = channels // CHUNK
    heads = q_cols // HEAD_DIM
    per = CHUNK // HEAD_P
    groups = key_states.shape[1] // HEAD_DIM
    smem = pl.BlockSpec(memory_space=pltpu.SMEM)
    hbm = pl.BlockSpec(memory_space=pltpu.HBM)
    far = pl.BlockSpec(memory_space=pl.ANY)
    dma = pltpu.SemaphoreType.DMA
    outs = (
        jax.ShapeDtypeStruct((length, channels), BF16),
        jax.ShapeDtypeStruct((length, q_cols), BF16),
    )
    coded = STATE + STATE // 4
    results = pl.pallas_call(
        functools.partial(kernel, n),
        out_shape=outs,
        in_specs=[smem, smem] + [hbm] * 9,
        out_specs=(hbm, hbm),
        scratch_shapes=[
            pltpu.VMEM((length, channels), BF16),
            pltpu.VMEM((length, q_cols), BF16),
            pltpu.VMEM((length, channels), BF16),
            pltpu.VMEM((length, STATE), BF16),
            pltpu.VMEM((length, STATE), BF16),
            pltpu.VMEM(step_size.shape, F32),
            pltpu.VMEM(log_decay.shape, F32),
            pltpu.VMEM((1, channels), F32),
            pltpu.VMEM((2, n + 1, groups, length, HEAD_DIM), BF16),
            pltpu.VMEM((chunks, CHUNK, q_cols), BF16),
            pltpu.VMEM((chunks, CHUNK, q_cols), BF16),
            pltpu.VMEM((STATE, length), BF16),
            pltpu.VMEM((2, length // 2, length // 2), F32),
            pltpu.VMEM((chunks, 4 * per, length), F32),
            pltpu.VMEM((chunks, length, 4 * per), F32),
            pltpu.VMEM((chunks, per, length), F32),
            pltpu.VMEM((chunks, coded, CHUNK), jnp.int16),
            pltpu.VMEM((chunks, coded, CHUNK), jnp.int16),
            pltpu.VMEM((chunks, 1, CHUNK), F32),
            pltpu.VMEM((chunks, 1, CHUNK), F32),
            pltpu.VMEM((chunks, length, CHUNK), BF16),
            pltpu.VMEM((length, q_cols), F32),
            pltpu.VMEM((heads + heads // groups, length, HEAD_DIM), BF16),
            pltpu.VMEM((2, length, length), F32),
            pltpu.VMEM((2 * n, length // BLOCK, 8, length), F32),
            pltpu.VMEM((2, heads // groups, length, length), BF16),
            pltpu.VMEM((heads + heads // groups, 8, length), F32),
            pltpu.VMEM((heads + heads // groups, 8, length), F32),
            pltpu.VMEM((max(heads + heads // groups, 2 * chunks), HEAD_DIM, length), F32),
            pltpu.VMEM((2 * chunks, STATE, CHUNK), F32),
            dma((6,)),
            dma((2, groups)),
            dma((2, n, groups)),
            dma((2, n + 1, groups)),
        ]
        + [dma((chunks,))] * 10
        + [dma((groups,)), pltpu.VMEM((heads // groups, length, HEAD_DIM), BF16), dma((2,)), dma((2,))]
        + [dma((heads // groups,))] * 4,
        compiler_params=pltpu.CompilerParams(
            collective_id=0, has_side_effects=True, vmem_limit_bytes=56 * 1024 * 1024
        ),
        name="mixer_attention",
    )(
        block_mask,
        skip_gain,
        ssm_input,
        input_map,
        output_map,
        step_size,
        log_decay,
        norm_gain.reshape(1, channels),
        query_weight,
        key_states,
        value_states,
    )
    return pl.pallas_call(
        hand_on,
        out_shape=outs,
        in_specs=[far, far],
        out_specs=[far, far],
        scratch_shapes=[pltpu.VMEM((2, 4, length // 4, channels), BF16), dma((2, 4)), dma((2, 4))],
        name="hand_on",
    )(*results)


def solution(mesh):
    return jax.shard_map(
        on_device,
        mesh=mesh,
        in_specs=(
            P(("dp", "context"), "tensor"),
            P(("dp", "context"), None),
            P(("dp", "context"), None),
            P("tensor", ("dp", "context")),
            P("tensor", ("dp", "context")),
            P("tensor"),
            P("tensor"),
            P("tensor", None),
            P(("dp", "context"), "tensor"),
            P(("dp", "context"), "tensor"),
            P("dp", None),
        ),
        out_specs=(P(("dp", "context"), "tensor"), P(("dp", "context"), "tensor")),
        check_vma=False,
    )
```

```python
import functools

import jax
import jax.numpy as jnp
from jax import lax
from jax.experimental import pallas as pl
from jax.experimental.pallas import tpu as pltpu
from jax.sharding import PartitionSpec as P

HEAD_P = 64
STATE = 128
HEAD_DIM = 128
BLOCK = 128
CHUNK = 256
NEGATIVE = -1e30
LOG2E = 1.4426950408889634
LEVELS = 524287.0
MESH = pl.DeviceIdType.MESH
F32 = jnp.float32
BF16 = jnp.bfloat16
NT = (((1,), (1,)), ((), ()))


def split(wide):
    high = wide.astype(BF16)
    rest = wide - high.astype(F32)
    middle = rest.astype(BF16)
    return high, middle, (rest - middle.astype(F32)).astype(BF16)


def dot(a, b):
    return jnp.dot(a, b, preferred_element_type=F32)


def dot_left(wide, narrow):
    high, middle, low = split(wide)
    return dot(high, narrow) + (dot(middle, narrow) + dot(low, narrow))


def dot_right(narrow, wide):
    high, middle, low = split(wide)
    return dot(narrow, high) + (dot(narrow, middle) + dot(narrow, low))


def encode(wide):
    largest = jnp.maximum(jnp.max(jnp.abs(wide), axis=0, keepdims=True), 1e-30)
    whole = jnp.round(wide * (LEVELS / largest)).astype(jnp.int32)
    quarter = wide.shape[0] // 4
    low = whole & 15
    packed = low[:quarter]
    for i in range(1, 4):
        packed = packed | (low[i * quarter : (i + 1) * quarter] << (4 * i))
    return (whole >> 4).astype(jnp.int16), (packed - 32768).astype(jnp.int16), largest * (1.0 / LEVELS)


def decode(high, packed, scale):
    packed = packed.astype(jnp.int32) + 32768
    low = jnp.concatenate([(packed >> (4 * i)) & 15 for i in range(4)], axis=0)
    return (high.astype(jnp.int32) * 16 + low).astype(F32) * scale


def kernel(
    n,
    mask_ref,
    skip_ref,
    x_hbm,
    b_hbm,
    c_hbm,
    dt_hbm,
    ld_hbm,
    gain_hbm,
    w_ref,
    k_hbm,
    v_hbm,
    mixer_hbm,
    attended_hbm,
    mixer_ref,
    attended_ref,
    x_ref,
    b_ref,
    c_ref,
    dt_ref,
    ld_ref,
    gain_ref,
    kv,
    w_own,
    w_other,
    bt,
    gram,
    rows_run,
    cols_run,
    rows_adj,
    code,
    code_in,
    scale,
    scale_in,
    mixed_other,
    q_acc,
    q_all,
    bias,
    rows_bias,
    weights,
    top,
    total,
    acc,
    own,
    ld_sem,
    own_sem,
    kv_send,
    kv_recv,
    st_send,
    st_recv,
    sc_send,
    sc_recv,
    mx_send,
    mx_recv,
    wt_send,
    wt_recv,
    wt_own,
    mx_out,
    at_out,
    answer,
    lk_send,
    lk_recv,
    lq_send,
    lq_recv,
    an_send,
    an_recv,
):
    me = lax.axis_index("context")
    core = lax.axis_index("tensor")
    other = 1 - core
    length = x_ref.shape[0]
    half = length // 2
    chunks = x_ref.shape[1] // CHUNK
    per = CHUNK // HEAD_P
    pairs = CHUNK // 128
    q_cols = w_own.shape[2]
    has_left = me > 0
    has_right = me < n - 1
    helper = me == n - 2
    last = me == n - 1
    middle = has_left & has_right
    heads = q_cols // HEAD_DIM
    groups = kv.shape[2]
    members = heads // groups
    blocks = length // BLOCK

    barrier = pltpu.get_barrier_semaphore()
    pl.semaphore_signal(barrier, inc=1, device_id={"tensor": other}, device_id_type=MESH)

    @pl.when(has_left)
    def _():
        pl.semaphore_signal(barrier, inc=1, device_id={"context": me - 1}, device_id_type=MESH)

    @pl.when(has_right)
    def _():
        pl.semaphore_signal(barrier, inc=1, device_id={"context": me + 1}, device_id_type=MESH)

    loads = [
        pltpu.make_async_copy(src, dst, ld_sem.at[i])
        for i, (src, dst) in enumerate(
            (
                (ld_hbm, ld_ref),
                (dt_hbm, dt_ref),
                (b_hbm, b_ref),
                (c_hbm, c_ref),
                (x_hbm, x_ref),
                (gain_hbm, gain_ref),
            )
        )
    ]
    for load in loads:
        load.start()

    hbm = (k_hbm, v_hbm)

    def fixed_lanes(g):
        return pl.ds(g * HEAD_DIM, HEAD_DIM)

    def own_load(which, g):
        return pltpu.make_async_copy(hbm[which].at[:, fixed_lanes(g)], kv.at[which, 0, g], own_sem.at[which, g])

    for which in range(2):
        for g in range(groups):
            own_load(which, g).start()

    peers = 1 + has_left.astype(jnp.int32) + has_right.astype(jnp.int32)

    @pl.when(has_left)
    def _():
        pl.semaphore_wait(barrier, peers)

    def pass_own(which, g):
        return pltpu.make_async_remote_copy(
            src_ref=hbm[which].at[:, fixed_lanes(g)],
            dst_ref=kv.at[which, 1, g],
            send_sem=kv_send.at[which, 0, g],
            recv_sem=kv_recv.at[which, 1, g],
            device_id={"context": me + 1},
            device_id_type=MESH,
        )

    def pass_on(which, slot, g):
        return pltpu.make_async_remote_copy(
            src_ref=kv.at[which, slot, g],
            dst_ref=kv.at[which, slot + 1, g],
            send_sem=kv_send.at[which, slot, g],
            recv_sem=kv_recv.at[which, slot + 1, g],
            device_id={"context": me + 1},
            device_id_type=MESH,
        )

    def arrive(which, slot, g):
        pltpu.make_async_remote_copy(
            src_ref=kv.at[which, slot - 1, g],
            dst_ref=kv.at[which, slot, g],
            send_sem=kv_send.at[which, slot - 1, g],
            recv_sem=kv_recv.at[which, slot, g],
            device_id={"context": me - 1},
            device_id_type=MESH,
        ).wait_recv()

    lent = groups - 1

    def passes(g):
        return ~helper | (g != lent)

    def forward(which, slot, g):
        arrive(which, slot, g)

        @pl.when(passes(g))
        def _():
            pass_on(which, slot, g).start()

    def lend(which):
        return pltpu.make_async_remote_copy(
            src_ref=hbm[which].at[:, fixed_lanes(lent)],
            dst_ref=kv.at[which, n, lent],
            send_sem=lk_send.at[which],
            recv_sem=lk_recv.at[which],
            device_id={"context": me - 1},
            device_id_type=MESH,
        )

    def lend_query(member):
        return pltpu.make_async_remote_copy(
            src_ref=q_all.at[lent * members + member],
            dst_ref=q_all.at[heads + member],
            send_sem=lq_send.at[member],
            recv_sem=lq_recv.at[member],
            device_id={"context": me - 1},
            device_id_type=MESH,
        )

    def give_back(member):
        return pltpu.make_async_remote_copy(
            src_ref=answer.at[member],
            dst_ref=attended_ref.at[:, fixed_lanes(lent * members + member)],
            send_sem=an_send.at[member],
            recv_sem=an_recv.at[member],
            device_id={"context": me + 1},
            device_id_type=MESH,
        )

    def state_copies(j):
        return [
            pltpu.make_async_remote_copy(
                src_ref=src.at[j],
                dst_ref=dst.at[j],
                send_sem=send.at[j],
                recv_sem=recv.at[j],
                device_id={"context": me + 1},
                device_id_type=MESH,
            )
            for src, dst, send, recv in ((scale, scale_in, sc_send, sc_recv), (code, code_in, st_send, st_recv))
        ]

    def lanes_of(j):
        return pl.ds(pl.multiple_of(j * CHUNK, CHUNK), CHUNK)

    def mixed_copy(j):
        return pltpu.make_async_remote_copy(
            src_ref=mixer_ref.at[:, lanes_of(j)],
            dst_ref=mixed_other.at[j],
            send_sem=mx_send.at[j],
            recv_sem=mx_recv.at[j],
            device_id={"tensor": other},
            device_id_type=MESH,
        )

    def mixed_out(j):
        return pltpu.make_async_copy(mixer_ref.at[:, lanes_of(j)], mixer_hbm.at[:, lanes_of(j)], mx_out.at[j])

    def attended_out(g):
        lanes = pl.ds(pl.multiple_of(g * members * HEAD_DIM, HEAD_DIM), members * HEAD_DIM)
        return pltpu.make_async_copy(attended_ref.at[:, lanes], attended_hbm.at[:, lanes], at_out.at[g])

    def weight_out(j):
        return pltpu.make_async_remote_copy(
            src_ref=w_ref.at[lanes_of(j), pl.ds(pl.multiple_of(other * q_cols, CHUNK), q_cols)],
            dst_ref=w_other.at[j],
            send_sem=wt_send.at[j],
            recv_sem=wt_recv.at[j],
            device_id={"tensor": other},
            device_id_type=MESH,
        )

    def weight_in(j):
        return pltpu.make_async_copy(
            w_ref.at[lanes_of(j), pl.ds(pl.multiple_of(core * q_cols, CHUNK), q_cols)],
            w_own.at[j],
            wt_own.at[j],
        )

    def start_weights():
        @pl.loop(0, chunks)
        def _(j):
            weight_in(j).start()
            weight_out(j).start()

    @pl.when(has_left)
    def _():
        @pl.when(has_right)
        def _():
            for g in range(groups):

                @pl.when(passes(g))
                def _(g=g):
                    pass_own(0, g).start()

        @pl.when(last)
        def _():
            for which in range(2):
                lend(which).start()

        start_weights()

    row = lax.broadcasted_iota(jnp.int32, (length, length), 0)
    col = lax.broadcasted_iota(jnp.int32, (length, length), 1)
    same = (row // BLOCK) == (col // BLOCK)
    loads[0].wait()
    loads[1].wait()
    up_to = jnp.where((row <= col) & ((row // half) == (col // half)), 1.0, 0.0).astype(BF16)
    run = dot_left(ld_ref[...], up_to) * LOG2E
    ends = jnp.concatenate(
        [
            jnp.broadcast_to(run[:, half - 1 : half], (run.shape[0], half)),
            jnp.broadcast_to(run[:, length - 1 : length], (run.shape[0], half)),
        ],
        axis=1,
    )
    steps = dt_ref[...]
    grow = jnp.exp2(run)
    inject = jnp.exp2(ends - run) * steps
    adjusted = run - jnp.log(steps) * LOG2E
    for j in range(chunks):
        part = slice(j * per, (j + 1) * per)
        rows_run[j, 0:per, :] = run[part]
        rows_run[j, per : 2 * per, :] = grow[part]
        rows_run[j, 2 * per : 3 * per, :] = inject[part]
        rows_run[j, 3 * per : 4 * per, :] = inject[part]
        rows_adj[j] = adjusted[part]
    for j in range(chunks):
        cols_run[j] = jnp.transpose(rows_run[j])
    loads[2].wait()
    loads[3].wait()
    bt[...] = jnp.transpose(b_ref[...].astype(F32)).astype(BF16)
    for s in range(2):
        part = slice(s * half, (s + 1) * half)
        gram[s] = jnp.where(
            row[:half, :half] >= col[:half, :half],
            lax.dot_general(c_ref[part, :], b_ref[part, :], NT, preferred_element_type=F32),
            0.0,
        )
    first = lax.broadcasted_iota(jnp.int32, (1, 128), 1) < HEAD_P
    loads[4].wait()
    loads[5].wait()
    second = (me == 1) & has_right
    later = (me >= 2) & has_right
    stride = chunks // groups

    @pl.when(~has_left)
    def _():
        pl.semaphore_wait(barrier, peers)
        start_weights()

    def spread(table, at):
        return jnp.concatenate(
            [
                jnp.where(first, table[:, at + 2 * p : at + 2 * p + 1], table[:, at + 2 * p + 1 : at + 2 * p + 2])
                for p in range(pairs)
            ],
            axis=1,
        )

    def own_part(j, s):
        return own[2 * j + s]

    def send_state(j, entering):
        keep = spread(cols_run[j, length - 1 : length, :], per)
        high, packed, unit = encode(keep * entering + own_part(j, 1))
        code[j, 0:STATE, :] = high
        code[j, STATE : STATE + STATE // 4, :] = packed
        scale[j] = unit
        for copy in state_copies(j):
            copy.start()

    @pl.loop(0, chunks)
    def _(j):
        weighted = x_ref[:, lanes_of(j)].astype(F32) * spread(cols_run[j], 2 * per)

        def keep_part(s):
            own[2 * j + s] = dot_right(bt[:, s * half : (s + 1) * half], weighted[s * half : (s + 1) * half])

        keep_part(0)

        @pl.when(has_right)
        def _():
            keep_part(1)

        @pl.when(~has_left & has_right)
        def _():
            send_state(j, own_part(j, 0))

        for g in range(groups):

            @pl.when(later & (j == g * stride))
            def _(g=g):
                forward(0, 1, g)

    @pl.when(~has_left & has_right)
    def _():
        for g in range(groups):
            pass_own(0, g).start()
            pass_own(1, g).start()

    def inside(j):
        runs = cols_run[j]
        adj = rows_adj[j]
        for p in range(pairs):
            lanes = pl.ds(pl.multiple_of(j * CHUNK + p * 128, 128), 128)
            for s in range(2):
                part = slice(s * half, (s + 1) * half)
                x_own = x_ref[part, lanes]
                x_wide = x_own.astype(F32)
                pieces = []
                for m in range(2):
                    a = 2 * p + m
                    weight = gram[s] * jnp.exp2(jnp.minimum(runs[part, a : a + 1] - adj[a : a + 1, part], 0.0))
                    pieces.append(split(weight))
                both = jnp.concatenate(
                    [
                        jnp.where(first, x_wide, 0.0).astype(BF16),
                        jnp.where(first, 0.0, x_wide).astype(BF16),
                    ],
                    axis=0,
                )
                high, mid, low = (jnp.concatenate([pieces[0][i], pieces[1][i]], axis=1) for i in range(3))
                gain = jnp.where(first, skip_ref[j * per + 2 * p], skip_ref[j * per + 2 * p + 1])
                acc[2 * j + s, :, p * 128 : (p + 1) * 128] = (dot(high, both) + (dot(mid, both) + dot(low, both))) + gain * x_wide

    def table(owner, slot, at):
        for i in range(blocks):
            for m in range(blocks):
                seen = mask_ref[owner * blocks + i, (owner - slot) * blocks + m] == 1
                rows_bias[at, m, :, i * BLOCK : (i + 1) * BLOCK] = jnp.full(
                    (8, BLOCK), jnp.where(seen, 0.0, NEGATIVE), F32
                )

    def diagonal(at, which):
        rows = [jnp.broadcast_to(rows_bias[at, m, 0:1, :], (BLOCK, length)) for m in range(blocks)]
        bias[which] = jnp.where(row <= col, jnp.where(same, 0.0, jnp.concatenate(rows, axis=0)), NEGATIVE)

    for slot in range(n):

        @pl.when(slot <= me)
        def _(slot=slot):
            table(me, slot, slot)

    diagonal(0, 0)

    @pl.when(helper)
    def _():
        for slot in range(n):
            table(me + 1, slot, n + slot)
        diagonal(n, 1)

    total[...] = jnp.zeros_like(total)
    top[...] = jnp.full_like(top, NEGATIVE)

    @pl.when(later)
    def _():
        pass_own(1, 0).start()

    ahead = jnp.where(me >= 2, chunks, 0)

    @pl.loop(0, ahead)
    def _(j):
        inside(j)

    def add_query(j):
        for t in range(0, q_cols, 512):
            q_acc[:, t : t + 512] = dot(mixer_ref[:, lanes_of(j)], w_own[j, :, t : t + 512])

    def add_other(j):
        mixed_copy(j).wait_recv()
        weight_out(j).wait_recv()
        for t in range(0, q_cols, 512):
            q_acc[:, t : t + 512] += dot(mixed_other[j], w_other[j, :, t : t + 512])

    @pl.when(~has_left)
    def _():
        code_in[...] = jnp.zeros_like(code_in)
        scale_in[...] = jnp.zeros_like(scale_in)

    lag = jnp.where(second, chunks, 0)

    def states_at(j):
        arrived = decode(code_in[j, 0:STATE, :], code_in[j, STATE : STATE + STATE // 4, :], scale_in[j])
        return arrived, spread(cols_run[j, half - 1 : half, :], per) * arrived + own_part(j, 0)

    def relay(j):
        @pl.when(has_left)
        def _():
            for copy in state_copies(j):
                copy.wait_recv()

        @pl.when(middle)
        def _():
            send_state(j, states_at(j)[1])

        for g in range(1, groups):

            @pl.when(later & (j == (0 if g == 1 else chunks - 1)) & passes(g))
            def _(g=g):
                pass_own(1, g).start()

        @pl.when(later & (j == chunks - 1))
        def _():
            forward(0, 2, 0)

        @pl.when(j >= ahead)
        def _():
            inside(j)

    def mix(j):
        for g in range(groups):

            @pl.when(second & (j == g * stride))
            def _(g=g):
                forward(0, 1, g)
                pass_own(1, g).start()
                forward(1, 1, g)

        arrived, entering = states_at(j)
        runs = cols_run[j]
        for s in range(2):
            part = slice(s * half, (s + 1) * half)
            carried = dot_right(c_ref[part, :], arrived if s == 0 else entering)
            grown = spread(runs[part], per)
            for p in range(pairs):
                lanes = slice(p * 128, (p + 1) * 128)
                out_lanes = pl.ds(pl.multiple_of(j * CHUNK + p * 128, 128), 128)
                y = acc[2 * j + s, :, lanes] + carried[:, lanes] * grown[:, lanes]
                squares = y * y
                left = jnp.sum(jnp.where(first, squares, 0.0), axis=1, keepdims=True)
                right = jnp.sum(jnp.where(first, 0.0, squares), axis=1, keepdims=True)
                mean = jnp.where(first, left, right) * (1.0 / HEAD_P)
                mixer_ref[part, out_lanes] = (y * lax.rsqrt(mean + 1e-05) * gain_ref[:, out_lanes]).astype(BF16)
        mixed_copy(j).start()
        mixed_out(j).start()
        weight_in(j).wait()

        @pl.when(j == 0)
        def _():
            add_query(j)

        @pl.when(j >= 1)
        def _():
            mixed_copy(j - 1).wait_recv()
            weight_out(j - 1).wait_recv()
            for t in range(0, q_cols, 512):
                q_acc[:, t : t + 512] += dot(mixer_ref[:, lanes_of(j)], w_own[j, :, t : t + 512]) + dot(
                    mixed_other[j - 1], w_other[j - 1, :, t : t + 512]
                )

    @pl.loop(0, chunks + lag)
    def _(t):
        @pl.when(t < chunks)
        def _():
            relay(t)

        @pl.when(t >= lag)
        def _():
            mix(t - lag)

    add_other(chunks - 1)
    for h in range(heads):
        q_all[h] = q_acc[:, h * HEAD_DIM : (h + 1) * HEAD_DIM].astype(BF16)

    @pl.when(last)
    def _():
        for member in range(members):
            lend_query(member).start()

    for which in range(2):
        for g in range(groups):
            own_load(which, g).wait()
    unit_scale = HEAD_DIM ** (-0.5) * LOG2E

    def head_lanes(h):
        return pl.ds(pl.multiple_of(h * HEAD_DIM, HEAD_DIM), HEAD_DIM)

    span = BLOCK // 8

    def by_eight(table):
        return table.reshape(length // 8, 8, length)

    def arrive_values(slot, g):
        @pl.when(last & (slot >= 1))
        def _():
            arrive(1, slot, g)

    @pl.loop(0, jnp.where(helper, groups + 1, jnp.where(last, groups - 1, groups)))
    def _(unit):
        lending = helper & (unit == lent)
        g = jnp.minimum(unit, groups - 1)
        base = jnp.where(lending, heads, g * members)
        end = jnp.where(lending, me + 1, me)

        def held(slot):
            return jnp.where(lending, jnp.where(slot == 0, n, slot - 1), slot)

        def scores_of(slot, member):
            keys = kv[0, held(slot), g]
            return by_eight(lax.dot_general(keys, q_all[base + member], NT, preferred_element_type=F32))

        def row_of(slot, m):
            return rows_bias[jnp.where(lending, n + slot, slot), m]

        def best_first():
            for member in range(members):
                h = base + member
                scores = scores_of(0, member) + by_eight(bias[lending.astype(jnp.int32)])
                top[h] = jnp.maximum(top[h], jnp.max(scores, axis=0))

        def weigh_first():
            for member in range(members):
                h = base + member
                scores = scores_of(0, member) + by_eight(bias[lending.astype(jnp.int32)])
                part = jnp.exp2((scores - top[h]) * unit_scale)
                total[h] += jnp.sum(part, axis=0)
                weights[0, member] = part.reshape(length, length).astype(BF16)

        def weigh(slot):
            for member in range(members):
                h = base + member
                scores = scores_of(slot, member)
                summed = total[h]
                for m in range(blocks):
                    shift = top[h] - row_of(slot, m)
                    part = jnp.exp2((scores[m * span : (m + 1) * span] - shift) * unit_scale)
                    summed = summed + jnp.sum(part, axis=0)
                    weights[slot % 2, member, m * BLOCK : (m + 1) * BLOCK, :] = part.reshape(BLOCK, length).astype(BF16)
                total[h] = summed

        def attend(slot):
            values = jnp.transpose(kv[1, held(slot), g].astype(F32)).astype(BF16)
            for member in range(members):
                h = base + member
                acc[h] = jnp.where(slot == 0, 0.0, acc[h]) + dot(values, weights[slot % 2, member])

        @pl.when(later & (unit < groups))
        def _():
            @pl.loop(jnp.where(unit == 0, 3, 2), me + 1)
            def _(slot):
                forward(0, slot, g)

            @pl.loop(1, me + 1)
            def _(slot):
                forward(1, slot, g)

        @pl.when(lending)
        def _():
            for which in range(2):
                lend(which).wait_recv()
            for member in range(members):
                lend_query(member).wait_recv()

        best_first()

        @pl.loop(1, end + 1)
        def _(slot):
            @pl.when(last)
            def _():
                arrive(0, slot, g)

            for member in range(members):
                h = base + member
                scores = scores_of(slot, member)
                best = top[h]
                for m in range(blocks):
                    best = jnp.maximum(best, jnp.max(scores[m * span : (m + 1) * span], axis=0) + row_of(slot, m))
                top[h] = best

        for member in range(members):
            h = base + member
            top[h] = jnp.broadcast_to(jnp.max(top[h], axis=0, keepdims=True), top.shape[1:])
        weigh_first()

        @pl.loop(1, end + 1)
        def _(slot):
            arrive_values(slot - 1, g)
            weigh(slot)
            attend(slot - 1)

        arrive_values(end, g)
        attend(end)
        for member in range(members):
            h = base + member
            out = jnp.transpose(acc[h] / jnp.sum(total[h], axis=0, keepdims=True)).astype(BF16)

            @pl.when(lending)
            def _(member=member, out=out):
                answer[member] = out
                give_back(member).start()

            @pl.when(~lending)
            def _(h=h, out=out):
                attended_ref[:, head_lanes(h)] = out

        @pl.when(~lending)
        def _():
            attended_out(g).start()

    @pl.when(last)
    def _():
        for member in range(members):
            give_back(member).wait_recv()
        attended_out(lent).start()
        for which in range(2):
            lend(which).wait_send()
        for member in range(members):
            lend_query(member).wait_send()

    @pl.when(helper)
    def _():
        for member in range(members):
            give_back(member).wait_send()

    @pl.loop(0, groups)
    def _(g):
        attended_out(g).wait()

    @pl.loop(0, chunks)
    def _(j):
        mixed_copy(j).wait_send()
        mixed_out(j).wait()
        weight_out(j).wait_send()

        @pl.when(has_right)
        def _():
            for copy in state_copies(j):
                copy.wait_send()

    @pl.loop(0, n)
    def _(slot):
        @pl.when((slot <= me) & has_right)
        def _():
            for which in range(2):
                for g in range(groups):

                    @pl.when(passes(g))
                    def _(which=which, g=g):
                        pass_on(which, slot, g).wait_send()


def hand_on(mixer_ref, attended_ref, mixer_out, attended_out, held, loads, stores):
    parts = held.shape[1]
    rows = held.shape[2]
    refs = ((mixer_ref, mixer_out), (attended_ref, attended_out))

    def load(k, i):
        return pltpu.make_async_copy(refs[k][0].at[pl.ds(i * rows, rows)], held.at[k, i], loads.at[k, i])

    def store(k, i):
        return pltpu.make_async_copy(held.at[k, i], refs[k][1].at[pl.ds(i * rows, rows)], stores.at[k, i])

    every = [(k, i) for k in range(2) for i in range(parts)]
    for at in every:
        load(*at).start()
    for at in every:
        load(*at).wait()
        store(*at).start()
    for at in every:
        store(*at).wait()


def on_device(
    ssm_input,
    input_map,
    output_map,
    step_size,
    log_decay,
    skip_gain,
    norm_gain,
    query_weight,
    key_states,
    value_states,
    block_mask,
):
    n = lax.axis_size("context")
    length, channels = ssm_input.shape
    q_cols = query_weight.shape[1] // lax.axis_size("tensor")
    chunks = channels // CHUNK
    heads = q_cols // HEAD_DIM
    per = CHUNK // HEAD_P
    groups = key_states.shape[1] // HEAD_DIM
    smem = pl.BlockSpec(memory_space=pltpu.SMEM)
    hbm = pl.BlockSpec(memory_space=pltpu.HBM)
    far = pl.BlockSpec(memory_space=pl.ANY)
    dma = pltpu.SemaphoreType.DMA
    outs = (
        jax.ShapeDtypeStruct((length, channels), BF16),
        jax.ShapeDtypeStruct((length, q_cols), BF16),
    )
    coded = STATE + STATE // 4
    results = pl.pallas_call(
        functools.partial(kernel, n),
        out_shape=outs,
        in_specs=[smem, smem] + [hbm] * 9,
        out_specs=(hbm, hbm),
        scratch_shapes=[
            pltpu.VMEM((length, channels), BF16),
            pltpu.VMEM((length, q_cols), BF16),
            pltpu.VMEM((length, channels), BF16),
            pltpu.VMEM((length, STATE), BF16),
            pltpu.VMEM((length, STATE), BF16),
            pltpu.VMEM(step_size.shape, F32),
            pltpu.VMEM(log_decay.shape, F32),
            pltpu.VMEM((1, channels), F32),
            pltpu.VMEM((2, n + 1, groups, length, HEAD_DIM), BF16),
            pltpu.VMEM((chunks, CHUNK, q_cols), BF16),
            pltpu.VMEM((chunks, CHUNK, q_cols), BF16),
            pltpu.VMEM((STATE, length), BF16),
            pltpu.VMEM((2, length // 2, length // 2), F32),
            pltpu.VMEM((chunks, 4 * per, length), F32),
            pltpu.VMEM((chunks, length, 4 * per), F32),
            pltpu.VMEM((chunks, per, length), F32),
            pltpu.VMEM((chunks, coded, CHUNK), jnp.int16),
            pltpu.VMEM((chunks, coded, CHUNK), jnp.int16),
            pltpu.VMEM((chunks, 1, CHUNK), F32),
            pltpu.VMEM((chunks, 1, CHUNK), F32),
            pltpu.VMEM((chunks, length, CHUNK), BF16),
            pltpu.VMEM((length, q_cols), F32),
            pltpu.VMEM((heads + heads // groups, length, HEAD_DIM), BF16),
            pltpu.VMEM((2, length, length), F32),
            pltpu.VMEM((2 * n, length // BLOCK, 8, length), F32),
            pltpu.VMEM((2, heads // groups, length, length), BF16),
            pltpu.VMEM((heads + heads // groups, 8, length), F32),
            pltpu.VMEM((heads + heads // groups, 8, length), F32),
            pltpu.VMEM((max(heads + heads // groups, 2 * chunks), HEAD_DIM, length), F32),
            pltpu.VMEM((2 * chunks, STATE, CHUNK), F32),
            dma((6,)),
            dma((2, groups)),
            dma((2, n, groups)),
            dma((2, n + 1, groups)),
        ]
        + [dma((chunks,))] * 10
        + [dma((groups,)), pltpu.VMEM((heads // groups, length, HEAD_DIM), BF16), dma((2,)), dma((2,))]
        + [dma((heads // groups,))] * 4,
        compiler_params=pltpu.CompilerParams(
            collective_id=0, has_side_effects=True, vmem_limit_bytes=56 * 1024 * 1024
        ),
        name="mixer_attention",
    )(
        block_mask,
        skip_gain,
        ssm_input,
        input_map,
        output_map,
        step_size,
        log_decay,
        norm_gain.reshape(1, channels),
        query_weight,
        key_states,
        value_states,
    )
    return pl.pallas_call(
        hand_on,
        out_shape=outs,
        in_specs=[far, far],
        out_specs=[far, far],
        scratch_shapes=[pltpu.VMEM((2, 4, length // 4, channels), BF16), dma((2, 4)), dma((2, 4))],
        name="hand_on",
    )(*results)


def solution(mesh):
    return jax.shard_map(
        on_device,
        mesh=mesh,
        in_specs=(
            P(("dp", "context"), "tensor"),
            P(("dp", "context"), None),
            P(("dp", "context"), None),
            P("tensor", ("dp", "context")),
            P("tensor", ("dp", "context")),
            P("tensor"),
            P("tensor"),
            P("tensor", None),
            P(("dp", "context"), "tensor"),
            P(("dp", "context"), "tensor"),
            P("dp", None),
        ),
        out_specs=(P(("dp", "context"), "tensor"), P(("dp", "context"), "tensor")),
        check_vma=False,
    )
```

```python
import functools

import jax
import jax.numpy as jnp
from jax import lax
from jax.experimental import pallas as pl
from jax.experimental.pallas import tpu as pltpu
from jax.sharding import PartitionSpec as P

HEAD_P = 64
STATE = 128
HEAD_DIM = 128
BLOCK = 128
CHUNK = 256
NEGATIVE = -1e30
LOG2E = 1.4426950408889634
LEVELS = 524287.0
MESH = pl.DeviceIdType.MESH
F32 = jnp.float32
BF16 = jnp.bfloat16
NT = (((1,), (1,)), ((), ()))


def split(wide):
    high = wide.astype(BF16)
    rest = wide - high.astype(F32)
    middle = rest.astype(BF16)
    return high, middle, (rest - middle.astype(F32)).astype(BF16)


def dot(a, b):
    return jnp.dot(a, b, preferred_element_type=F32)


def dot_left(wide, narrow):
    high, middle, low = split(wide)
    return dot(high, narrow) + (dot(middle, narrow) + dot(low, narrow))


def dot_right(narrow, wide):
    high, middle, low = split(wide)
    return dot(narrow, high) + (dot(narrow, middle) + dot(narrow, low))


def encode(wide):
    largest = jnp.maximum(jnp.max(jnp.abs(wide), axis=0, keepdims=True), 1e-30)
    whole = jnp.round(wide * (LEVELS / largest)).astype(jnp.int32)
    quarter = wide.shape[0] // 4
    low = whole & 15
    packed = low[:quarter]
    for i in range(1, 4):
        packed = packed | (low[i * quarter : (i + 1) * quarter] << (4 * i))
    return (whole >> 4).astype(jnp.int16), (packed - 32768).astype(jnp.int16), largest * (1.0 / LEVELS)


def decode(high, packed, scale):
    packed = packed.astype(jnp.int32) + 32768
    low = jnp.concatenate([(packed >> (4 * i)) & 15 for i in range(4)], axis=0)
    return (high.astype(jnp.int32) * 16 + low).astype(F32) * scale


def kernel(
    n,
    mask_ref,
    skip_ref,
    x_hbm,
    b_hbm,
    c_hbm,
    dt_hbm,
    ld_hbm,
    gain_hbm,
    w_ref,
    k_hbm,
    v_hbm,
    mixer_hbm,
    attended_hbm,
    mixer_ref,
    attended_ref,
    x_ref,
    b_ref,
    c_ref,
    dt_ref,
    ld_ref,
    gain_ref,
    kv,
    w_own,
    w_other,
    bt,
    gram,
    rows_run,
    cols_run,
    rows_adj,
    code,
    code_in,
    scale,
    scale_in,
    mixed_other,
    q_acc,
    q_all,
    bias,
    rows_bias,
    weights,
    top,
    total,
    acc,
    own,
    ld_sem,
    own_sem,
    kv_send,
    kv_recv,
    st_send,
    st_recv,
    sc_send,
    sc_recv,
    mx_send,
    mx_recv,
    wt_send,
    wt_recv,
    wt_own,
    mx_out,
    at_out,
    answer,
    lk_send,
    lk_recv,
    lq_send,
    lq_recv,
    an_send,
    an_recv,
):
    me = lax.axis_index("context")
    core = lax.axis_index("tensor")
    other = 1 - core
    length = x_ref.shape[0]
    half = length // 2
    chunks = x_ref.shape[1] // CHUNK
    per = CHUNK // HEAD_P
    pairs = CHUNK // 128
    q_cols = w_own.shape[2]
    has_left = me > 0
    has_right = me < n - 1
    helper = me == n - 2
    last = me == n - 1
    middle = has_left & has_right
    heads = q_cols // HEAD_DIM
    groups = kv.shape[2]
    members = heads // groups
    blocks = length // BLOCK

    barrier = pltpu.get_barrier_semaphore()
    pl.semaphore_signal(barrier, inc=1, device_id={"tensor": other}, device_id_type=MESH)

    @pl.when(has_left)
    def _():
        pl.semaphore_signal(barrier, inc=1, device_id={"context": me - 1}, device_id_type=MESH)

    @pl.when(has_right)
    def _():
        pl.semaphore_signal(barrier, inc=1, device_id={"context": me + 1}, device_id_type=MESH)

    loads = [
        pltpu.make_async_copy(src, dst, ld_sem.at[i])
        for i, (src, dst) in enumerate(
            (
                (ld_hbm, ld_ref),
                (dt_hbm, dt_ref),
                (b_hbm, b_ref),
                (c_hbm, c_ref),
                (x_hbm, x_ref),
                (gain_hbm, gain_ref),
            )
        )
    ]
    for load in loads:
        load.start()

    hbm = (k_hbm, v_hbm)

    def fixed_lanes(g):
        return pl.ds(g * HEAD_DIM, HEAD_DIM)

    def own_load(which, g):
        return pltpu.make_async_copy(hbm[which].at[:, fixed_lanes(g)], kv.at[which, 0, g], own_sem.at[which, g])

    for which in range(2):
        for g in range(groups):
            own_load(which, g).start()

    peers = 1 + has_left.astype(jnp.int32) + has_right.astype(jnp.int32)

    @pl.when(has_left)
    def _():
        pl.semaphore_wait(barrier, peers)

    def pass_own(which, g):
        return pltpu.make_async_remote_copy(
            src_ref=hbm[which].at[:, fixed_lanes(g)],
            dst_ref=kv.at[which, 1, g],
            send_sem=kv_send.at[which, 0, g],
            recv_sem=kv_recv.at[which, 1, g],
            device_id={"context": me + 1},
            device_id_type=MESH,
        )

    def pass_on(which, slot, g):
        return pltpu.make_async_remote_copy(
            src_ref=kv.at[which, slot, g],
            dst_ref=kv.at[which, slot + 1, g],
            send_sem=kv_send.at[which, slot, g],
            recv_sem=kv_recv.at[which, slot + 1, g],
            device_id={"context": me + 1},
            device_id_type=MESH,
        )

    def arrive(which, slot, g):
        pltpu.make_async_remote_copy(
            src_ref=kv.at[which, slot - 1, g],
            dst_ref=kv.at[which, slot, g],
            send_sem=kv_send.at[which, slot - 1, g],
            recv_sem=kv_recv.at[which, slot, g],
            device_id={"context": me - 1},
            device_id_type=MESH,
        ).wait_recv()

    lent = groups - 1

    def passes(g):
        return ~helper | (g != lent)

    def forward(which, slot, g):
        arrive(which, slot, g)

        @pl.when(passes(g))
        def _():
            pass_on(which, slot, g).start()

    def lend(which):
        return pltpu.make_async_remote_copy(
            src_ref=hbm[which].at[:, fixed_lanes(lent)],
            dst_ref=kv.at[which, n, lent],
            send_sem=lk_send.at[which],
            recv_sem=lk_recv.at[which],
            device_id={"context": me - 1},
            device_id_type=MESH,
        )

    def lend_query(member):
        return pltpu.make_async_remote_copy(
            src_ref=q_all.at[lent * members + member],
            dst_ref=q_all.at[heads + member],
            send_sem=lq_send.at[member],
            recv_sem=lq_recv.at[member],
            device_id={"context": me - 1},
            device_id_type=MESH,
        )

    def give_back(member):
        return pltpu.make_async_remote_copy(
            src_ref=answer.at[member],
            dst_ref=attended_ref.at[:, fixed_lanes(lent * members + member)],
            send_sem=an_send.at[member],
            recv_sem=an_recv.at[member],
            device_id={"context": me + 1},
            device_id_type=MESH,
        )

    def state_copies(j):
        return [
            pltpu.make_async_remote_copy(
                src_ref=src.at[j],
                dst_ref=dst.at[j],
                send_sem=send.at[j],
                recv_sem=recv.at[j],
                device_id={"context": me + 1},
                device_id_type=MESH,
            )
            for src, dst, send, recv in ((scale, scale_in, sc_send, sc_recv), (code, code_in, st_send, st_recv))
        ]

    def lanes_of(j):
        return pl.ds(pl.multiple_of(j * CHUNK, CHUNK), CHUNK)

    def mixed_copy(j):
        return pltpu.make_async_remote_copy(
            src_ref=mixer_ref.at[:, lanes_of(j)],
            dst_ref=mixed_other.at[j],
            send_sem=mx_send.at[j],
            recv_sem=mx_recv.at[j],
            device_id={"tensor": other},
            device_id_type=MESH,
        )

    def mixed_out(j):
        return pltpu.make_async_copy(mixer_ref.at[:, lanes_of(j)], mixer_hbm.at[:, lanes_of(j)], mx_out.at[j])

    def attended_out(g):
        lanes = pl.ds(pl.multiple_of(g * members * HEAD_DIM, HEAD_DIM), members * HEAD_DIM)
        return pltpu.make_async_copy(attended_ref.at[:, lanes], attended_hbm.at[:, lanes], at_out.at[g])

    def weight_out(j):
        return pltpu.make_async_remote_copy(
            src_ref=w_ref.at[lanes_of(j), pl.ds(pl.multiple_of(other * q_cols, CHUNK), q_cols)],
            dst_ref=w_other.at[j],
            send_sem=wt_send.at[j],
            recv_sem=wt_recv.at[j],
            device_id={"tensor": other},
            device_id_type=MESH,
        )

    def weight_in(j):
        return pltpu.make_async_copy(
            w_ref.at[lanes_of(j), pl.ds(pl.multiple_of(core * q_cols, CHUNK), q_cols)],
            w_own.at[j],
            wt_own.at[j],
        )

    def start_weights():
        @pl.loop(0, chunks)
        def _(j):
            weight_in(j).start()
            weight_out(j).start()

    @pl.when(has_left)
    def _():
        @pl.when(has_right)
        def _():
            for g in range(groups):

                @pl.when(passes(g))
                def _(g=g):
                    pass_own(0, g).start()

        @pl.when(last)
        def _():
            for which in range(2):
                lend(which).start()

        start_weights()

    row = lax.broadcasted_iota(jnp.int32, (length, length), 0)
    col = lax.broadcasted_iota(jnp.int32, (length, length), 1)
    same = (row // BLOCK) == (col // BLOCK)
    loads[0].wait()
    loads[1].wait()
    up_to = jnp.where((row <= col) & ((row // half) == (col // half)), 1.0, 0.0).astype(BF16)
    run = dot_left(ld_ref[...], up_to) * LOG2E
    ends = jnp.concatenate(
        [
            jnp.broadcast_to(run[:, half - 1 : half], (run.shape[0], half)),
            jnp.broadcast_to(run[:, length - 1 : length], (run.shape[0], half)),
        ],
        axis=1,
    )
    steps = dt_ref[...]
    grow = jnp.exp2(run)
    inject = jnp.exp2(ends - run) * steps
    adjusted = run - jnp.log(steps) * LOG2E
    for j in range(chunks):
        part = slice(j * per, (j + 1) * per)
        rows_run[j, 0:per, :] = run[part]
        rows_run[j, per : 2 * per, :] = grow[part]
        rows_run[j, 2 * per : 3 * per, :] = inject[part]
        rows_run[j, 3 * per : 4 * per, :] = inject[part]
        rows_adj[j] = adjusted[part]
    for j in range(chunks):
        cols_run[j] = jnp.transpose(rows_run[j])
    loads[2].wait()
    loads[3].wait()
    bt[...] = jnp.transpose(b_ref[...].astype(F32)).astype(BF16)
    for s in range(2):
        part = slice(s * half, (s + 1) * half)
        gram[s] = jnp.where(
            row[:half, :half] >= col[:half, :half],
            lax.dot_general(c_ref[part, :], b_ref[part, :], NT, preferred_element_type=F32),
            0.0,
        )
    first = lax.broadcasted_iota(jnp.int32, (1, 128), 1) < HEAD_P
    loads[4].wait()
    loads[5].wait()
    second = (me == 1) & has_right
    later = (me >= 2) & has_right
    stride = chunks // groups

    @pl.when(~has_left)
    def _():
        pl.semaphore_wait(barrier, peers)
        start_weights()

    def spread(table, at):
        return jnp.concatenate(
            [
                jnp.where(first, table[:, at + 2 * p : at + 2 * p + 1], table[:, at + 2 * p + 1 : at + 2 * p + 2])
                for p in range(pairs)
            ],
            axis=1,
        )

    def own_part(j, s):
        return own[2 * j + s]

    def send_state(j, entering):
        keep = spread(cols_run[j, length - 1 : length, :], per)
        high, packed, unit = encode(keep * entering + own_part(j, 1))
        code[j, 0:STATE, :] = high
        code[j, STATE : STATE + STATE // 4, :] = packed
        scale[j] = unit
        for copy in state_copies(j):
            copy.start()

    @pl.loop(0, chunks)
    def _(j):
        weighted = x_ref[:, lanes_of(j)].astype(F32) * spread(cols_run[j], 2 * per)

        def keep_part(s):
            own[2 * j + s] = dot_right(bt[:, s * half : (s + 1) * half], weighted[s * half : (s + 1) * half])

        keep_part(0)

        @pl.when(has_right)
        def _():
            keep_part(1)

        @pl.when(~has_left & has_right)
        def _():
            send_state(j, own_part(j, 0))

        for g in range(groups):

            @pl.when(later & (j == g * stride))
            def _(g=g):
                forward(0, 1, g)

    @pl.when(~has_left & has_right)
    def _():
        for g in range(groups):
            pass_own(0, g).start()
            pass_own(1, g).start()

    def inside(j):
        runs = cols_run[j]
        adj = rows_adj[j]
        for p in range(pairs):
            lanes = pl.ds(pl.multiple_of(j * CHUNK + p * 128, 128), 128)
            for s in range(2):
                part = slice(s * half, (s + 1) * half)
                x_own = x_ref[part, lanes]
                x_wide = x_own.astype(F32)
                pieces = []
                for m in range(2):
                    a = 2 * p + m
                    weight = gram[s] * jnp.exp2(jnp.minimum(runs[part, a : a + 1] - adj[a : a + 1, part], 0.0))
                    pieces.append(split(weight))
                both = jnp.concatenate(
                    [
                        jnp.where(first, x_wide, 0.0).astype(BF16),
                        jnp.where(first, 0.0, x_wide).astype(BF16),
                    ],
                    axis=0,
                )
                high, mid, low = (jnp.concatenate([pieces[0][i], pieces[1][i]], axis=1) for i in range(3))
                gain = jnp.where(first, skip_ref[j * per + 2 * p], skip_ref[j * per + 2 * p + 1])
                acc[2 * j + s, :, p * 128 : (p + 1) * 128] = (dot(high, both) + (dot(mid, both) + dot(low, both))) + gain * x_wide

    def table(owner, slot, at):
        for i in range(blocks):
            for m in range(blocks):
                seen = mask_ref[owner * blocks + i, (owner - slot) * blocks + m] == 1
                rows_bias[at, m, :, i * BLOCK : (i + 1) * BLOCK] = jnp.full(
                    (8, BLOCK), jnp.where(seen, 0.0, NEGATIVE), F32
                )

    def diagonal(at, which):
        rows = [jnp.broadcast_to(rows_bias[at, m, 0:1, :], (BLOCK, length)) for m in range(blocks)]
        bias[which] = jnp.where(row <= col, jnp.where(same, 0.0, jnp.concatenate(rows, axis=0)), NEGATIVE)

    for slot in range(n):

        @pl.when(slot <= me)
        def _(slot=slot):
            table(me, slot, slot)

    diagonal(0, 0)

    @pl.when(helper)
    def _():
        for slot in range(n):
            table(me + 1, slot, n + slot)
        diagonal(n, 1)

    total[...] = jnp.zeros_like(total)
    top[...] = jnp.full_like(top, NEGATIVE)

    @pl.when(later)
    def _():
        pass_own(1, 0).start()
        pass_own(1, 1).start()

    ahead = jnp.where(me >= 2, chunks, 0)

    @pl.loop(0, ahead)
    def _(j):
        inside(j)

    def add_query(j):
        for t in range(0, q_cols, 512):
            q_acc[:, t : t + 512] = dot(mixer_ref[:, lanes_of(j)], w_own[j, :, t : t + 512])

    def add_other(j):
        mixed_copy(j).wait_recv()
        weight_out(j).wait_recv()
        for t in range(0, q_cols, 512):
            q_acc[:, t : t + 512] += dot(mixed_other[j], w_other[j, :, t : t + 512])

    @pl.when(~has_left)
    def _():
        code_in[...] = jnp.zeros_like(code_in)
        scale_in[...] = jnp.zeros_like(scale_in)

    lag = jnp.where(second, chunks, 0)

    def states_at(j):
        arrived = decode(code_in[j, 0:STATE, :], code_in[j, STATE : STATE + STATE // 4, :], scale_in[j])
        return arrived, spread(cols_run[j, half - 1 : half, :], per) * arrived + own_part(j, 0)

    def relay(j):
        @pl.when(has_left)
        def _():
            for copy in state_copies(j):
                copy.wait_recv()

        @pl.when(middle)
        def _():
            send_state(j, states_at(j)[1])

        for g in range(2, groups):

            @pl.when(later & (j == chunks - 1) & passes(g))
            def _(g=g):
                pass_own(1, g).start()

        @pl.when(later & (j == chunks - 1))
        def _():
            forward(0, 2, 0)

        @pl.when(j >= ahead)
        def _():
            inside(j)

    def mix(j):
        for g in range(groups):

            @pl.when(second & (j == g * stride))
            def _(g=g):
                forward(0, 1, g)
                pass_own(1, g).start()
                forward(1, 1, g)

        arrived, entering = states_at(j)
        runs = cols_run[j]
        for s in range(2):
            part = slice(s * half, (s + 1) * half)
            carried = dot_right(c_ref[part, :], arrived if s == 0 else entering)
            grown = spread(runs[part], per)
            for p in range(pairs):
                lanes = slice(p * 128, (p + 1) * 128)
                out_lanes = pl.ds(pl.multiple_of(j * CHUNK + p * 128, 128), 128)
                y = acc[2 * j + s, :, lanes] + carried[:, lanes] * grown[:, lanes]
                squares = y * y
                left = jnp.sum(jnp.where(first, squares, 0.0), axis=1, keepdims=True)
                right = jnp.sum(jnp.where(first, 0.0, squares), axis=1, keepdims=True)
                mean = jnp.where(first, left, right) * (1.0 / HEAD_P)
                mixer_ref[part, out_lanes] = (y * lax.rsqrt(mean + 1e-05) * gain_ref[:, out_lanes]).astype(BF16)
        mixed_copy(j).start()
        mixed_out(j).start()
        weight_in(j).wait()

        @pl.when(j == 0)
        def _():
            add_query(j)

        @pl.when(j >= 1)
        def _():
            mixed_copy(j - 1).wait_recv()
            weight_out(j - 1).wait_recv()
            for t in range(0, q_cols, 512):
                q_acc[:, t : t + 512] += dot(mixer_ref[:, lanes_of(j)], w_own[j, :, t : t + 512]) + dot(
                    mixed_other[j - 1], w_other[j - 1, :, t : t + 512]
                )

    @pl.loop(0, chunks + lag)
    def _(t):
        @pl.when(t < chunks)
        def _():
            relay(t)

        @pl.when(t >= lag)
        def _():
            mix(t - lag)

    add_other(chunks - 1)
    for h in range(heads):
        q_all[h] = q_acc[:, h * HEAD_DIM : (h + 1) * HEAD_DIM].astype(BF16)

    @pl.when(last)
    def _():
        for member in range(members):
            lend_query(member).start()

    for which in range(2):
        for g in range(groups):
            own_load(which, g).wait()
    unit_scale = HEAD_DIM ** (-0.5) * LOG2E

    def head_lanes(h):
        return pl.ds(pl.multiple_of(h * HEAD_DIM, HEAD_DIM), HEAD_DIM)

    span = BLOCK // 8

    def by_eight(table):
        return table.reshape(length // 8, 8, length)

    def arrive_values(slot, g):
        @pl.when(last & (slot >= 1))
        def _():
            arrive(1, slot, g)

    @pl.loop(0, jnp.where(helper, groups + 1, jnp.where(last, groups - 1, groups)))
    def _(unit):
        lending = helper & (unit == lent)
        g = jnp.minimum(unit, groups - 1)
        base = jnp.where(lending, heads, g * members)
        end = jnp.where(lending, me + 1, me)

        def held(slot):
            return jnp.where(lending, jnp.where(slot == 0, n, slot - 1), slot)

        def scores_of(slot, member):
            keys = kv[0, held(slot), g]
            return by_eight(lax.dot_general(keys, q_all[base + member], NT, preferred_element_type=F32))

        def row_of(slot, m):
            return rows_bias[jnp.where(lending, n + slot, slot), m]

        def best_first():
            for member in range(members):
                h = base + member
                scores = scores_of(0, member) + by_eight(bias[lending.astype(jnp.int32)])
                top[h] = jnp.maximum(top[h], jnp.max(scores, axis=0))

        def weigh_first():
            for member in range(members):
                h = base + member
                scores = scores_of(0, member) + by_eight(bias[lending.astype(jnp.int32)])
                part = jnp.exp2((scores - top[h]) * unit_scale)
                total[h] += jnp.sum(part, axis=0)
                weights[0, member] = part.reshape(length, length).astype(BF16)

        def weigh(slot):
            for member in range(members):
                h = base + member
                scores = scores_of(slot, member)
                summed = total[h]
                for m in range(blocks):
                    shift = top[h] - row_of(slot, m)
                    part = jnp.exp2((scores[m * span : (m + 1) * span] - shift) * unit_scale)
                    summed = summed + jnp.sum(part, axis=0)
                    weights[slot % 2, member, m * BLOCK : (m + 1) * BLOCK, :] = part.reshape(BLOCK, length).astype(BF16)
                total[h] = summed

        def attend(slot):
            values = jnp.transpose(kv[1, held(slot), g].astype(F32)).astype(BF16)
            for member in range(members):
                h = base + member
                acc[h] = jnp.where(slot == 0, 0.0, acc[h]) + dot(values, weights[slot % 2, member])

        @pl.when(later & (unit < groups))
        def _():
            @pl.loop(jnp.where(unit == 0, 3, 2), me + 1)
            def _(slot):
                forward(0, slot, g)

            @pl.loop(1, me + 1)
            def _(slot):
                forward(1, slot, g)

        @pl.when(lending)
        def _():
            for which in range(2):
                lend(which).wait_recv()
            for member in range(members):
                lend_query(member).wait_recv()

        best_first()

        @pl.loop(1, end + 1)
        def _(slot):
            @pl.when(last)
            def _():
                arrive(0, slot, g)

            for member in range(members):
                h = base + member
                scores = scores_of(slot, member)
                best = top[h]
                for m in range(blocks):
                    best = jnp.maximum(best, jnp.max(scores[m * span : (m + 1) * span], axis=0) + row_of(slot, m))
                top[h] = best

        for member in range(members):
            h = base + member
            top[h] = jnp.broadcast_to(jnp.max(top[h], axis=0, keepdims=True), top.shape[1:])
        weigh_first()

        @pl.loop(1, end + 1)
        def _(slot):
            arrive_values(slot - 1, g)
            weigh(slot)
            attend(slot - 1)

        arrive_values(end, g)
        attend(end)
        for member in range(members):
            h = base + member
            out = jnp.transpose(acc[h] / jnp.sum(total[h], axis=0, keepdims=True)).astype(BF16)

            @pl.when(lending)
            def _(member=member, out=out):
                answer[member] = out
                give_back(member).start()

            @pl.when(~lending)
            def _(h=h, out=out):
                attended_ref[:, head_lanes(h)] = out

        @pl.when(~lending)
        def _():
            attended_out(g).start()

    @pl.when(last)
    def _():
        for member in range(members):
            give_back(member).wait_recv()
        attended_out(lent).start()
        for which in range(2):
            lend(which).wait_send()
        for member in range(members):
            lend_query(member).wait_send()

    @pl.when(helper)
    def _():
        for member in range(members):
            give_back(member).wait_send()

    @pl.loop(0, groups)
    def _(g):
        attended_out(g).wait()

    @pl.loop(0, chunks)
    def _(j):
        mixed_copy(j).wait_send()
        mixed_out(j).wait()
        weight_out(j).wait_send()

        @pl.when(has_right)
        def _():
            for copy in state_copies(j):
                copy.wait_send()

    @pl.loop(0, n)
    def _(slot):
        @pl.when((slot <= me) & has_right)
        def _():
            for which in range(2):
                for g in range(groups):

                    @pl.when(passes(g))
                    def _(which=which, g=g):
                        pass_on(which, slot, g).wait_send()


def hand_on(mixer_ref, attended_ref, mixer_out, attended_out, held, loads, stores):
    parts = held.shape[1]
    rows = held.shape[2]
    refs = ((mixer_ref, mixer_out), (attended_ref, attended_out))

    def load(k, i):
        return pltpu.make_async_copy(refs[k][0].at[pl.ds(i * rows, rows)], held.at[k, i], loads.at[k, i])

    def store(k, i):
        return pltpu.make_async_copy(held.at[k, i], refs[k][1].at[pl.ds(i * rows, rows)], stores.at[k, i])

    every = [(k, i) for k in range(2) for i in range(parts)]
    for at in every:
        load(*at).start()
    for at in every:
        load(*at).wait()
        store(*at).start()
    for at in every:
        store(*at).wait()


def on_device(
    ssm_input,
    input_map,
    output_map,
    step_size,
    log_decay,
    skip_gain,
    norm_gain,
    query_weight,
    key_states,
    value_states,
    block_mask,
):
    n = lax.axis_size("context")
    length, channels = ssm_input.shape
    q_cols = query_weight.shape[1] // lax.axis_size("tensor")
    chunks = channels // CHUNK
    heads = q_cols // HEAD_DIM
    per = CHUNK // HEAD_P
    groups = key_states.shape[1] // HEAD_DIM
    smem = pl.BlockSpec(memory_space=pltpu.SMEM)
    hbm = pl.BlockSpec(memory_space=pltpu.HBM)
    far = pl.BlockSpec(memory_space=pl.ANY)
    dma = pltpu.SemaphoreType.DMA
    outs = (
        jax.ShapeDtypeStruct((length, channels), BF16),
        jax.ShapeDtypeStruct((length, q_cols), BF16),
    )
    coded = STATE + STATE // 4
    results = pl.pallas_call(
        functools.partial(kernel, n),
        out_shape=outs,
        in_specs=[smem, smem] + [hbm] * 9,
        out_specs=(hbm, hbm),
        scratch_shapes=[
            pltpu.VMEM((length, channels), BF16),
            pltpu.VMEM((length, q_cols), BF16),
            pltpu.VMEM((length, channels), BF16),
            pltpu.VMEM((length, STATE), BF16),
            pltpu.VMEM((length, STATE), BF16),
            pltpu.VMEM(step_size.shape, F32),
            pltpu.VMEM(log_decay.shape, F32),
            pltpu.VMEM((1, channels), F32),
            pltpu.VMEM((2, n + 1, groups, length, HEAD_DIM), BF16),
            pltpu.VMEM((chunks, CHUNK, q_cols), BF16),
            pltpu.VMEM((chunks, CHUNK, q_cols), BF16),
            pltpu.VMEM((STATE, length), BF16),
            pltpu.VMEM((2, length // 2, length // 2), F32),
            pltpu.VMEM((chunks, 4 * per, length), F32),
            pltpu.VMEM((chunks, length, 4 * per), F32),
            pltpu.VMEM((chunks, per, length), F32),
            pltpu.VMEM((chunks, coded, CHUNK), jnp.int16),
            pltpu.VMEM((chunks, coded, CHUNK), jnp.int16),
            pltpu.VMEM((chunks, 1, CHUNK), F32),
            pltpu.VMEM((chunks, 1, CHUNK), F32),
            pltpu.VMEM((chunks, length, CHUNK), BF16),
            pltpu.VMEM((length, q_cols), F32),
            pltpu.VMEM((heads + heads // groups, length, HEAD_DIM), BF16),
            pltpu.VMEM((2, length, length), F32),
            pltpu.VMEM((2 * n, length // BLOCK, 8, length), F32),
            pltpu.VMEM((2, heads // groups, length, length), BF16),
            pltpu.VMEM((heads + heads // groups, 8, length), F32),
            pltpu.VMEM((heads + heads // groups, 8, length), F32),
            pltpu.VMEM((max(heads + heads // groups, 2 * chunks), HEAD_DIM, length), F32),
            pltpu.VMEM((2 * chunks, STATE, CHUNK), F32),
            dma((6,)),
            dma((2, groups)),
            dma((2, n, groups)),
            dma((2, n + 1, groups)),
        ]
        + [dma((chunks,))] * 10
        + [dma((groups,)), pltpu.VMEM((heads // groups, length, HEAD_DIM), BF16), dma((2,)), dma((2,))]
        + [dma((heads // groups,))] * 4,
        compiler_params=pltpu.CompilerParams(
            collective_id=0, has_side_effects=True, vmem_limit_bytes=56 * 1024 * 1024
        ),
        name="mixer_attention",
    )(
        block_mask,
        skip_gain,
        ssm_input,
        input_map,
        output_map,
        step_size,
        log_decay,
        norm_gain.reshape(1, channels),
        query_weight,
        key_states,
        value_states,
    )
    return pl.pallas_call(
        hand_on,
        out_shape=outs,
        in_specs=[far, far],
        out_specs=[far, far],
        scratch_shapes=[pltpu.VMEM((2, 4, length // 4, channels), BF16), dma((2, 4)), dma((2, 4))],
        name="hand_on",
    )(*results)


def solution(mesh):
    return jax.shard_map(
        on_device,
        mesh=mesh,
        in_specs=(
            P(("dp", "context"), "tensor"),
            P(("dp", "context"), None),
            P(("dp", "context"), None),
            P("tensor", ("dp", "context")),
            P("tensor", ("dp", "context")),
            P("tensor"),
            P("tensor"),
            P("tensor", None),
            P(("dp", "context"), "tensor"),
            P(("dp", "context"), "tensor"),
            P("dp", None),
        ),
        out_specs=(P(("dp", "context"), "tensor"), P(("dp", "context"), "tensor")),
        check_vma=False,
    )
```

```python
import functools

import jax
import jax.numpy as jnp
from jax import lax
from jax.experimental import pallas as pl
from jax.experimental.pallas import tpu as pltpu
from jax.sharding import PartitionSpec as P

HEAD_P = 64
STATE = 128
HEAD_DIM = 128
BLOCK = 128
CHUNK = 256
NEGATIVE = -1e30
LOG2E = 1.4426950408889634
LEVELS = 524287.0
MESH = pl.DeviceIdType.MESH
F32 = jnp.float32
BF16 = jnp.bfloat16
NT = (((1,), (1,)), ((), ()))


def split(wide):
    high = wide.astype(BF16)
    rest = wide - high.astype(F32)
    middle = rest.astype(BF16)
    return high, middle, (rest - middle.astype(F32)).astype(BF16)


def dot(a, b):
    return jnp.dot(a, b, preferred_element_type=F32)


def dot_left(wide, narrow):
    high, middle, low = split(wide)
    return dot(high, narrow) + (dot(middle, narrow) + dot(low, narrow))


def dot_right(narrow, wide):
    high, middle, low = split(wide)
    return dot(narrow, high) + (dot(narrow, middle) + dot(narrow, low))


def encode(wide):
    largest = jnp.maximum(jnp.max(jnp.abs(wide), axis=0, keepdims=True), 1e-30)
    whole = jnp.round(wide * (LEVELS / largest)).astype(jnp.int32)
    quarter = wide.shape[0] // 4
    low = whole & 15
    packed = low[:quarter]
    for i in range(1, 4):
        packed = packed | (low[i * quarter : (i + 1) * quarter] << (4 * i))
    return (whole >> 4).astype(jnp.int16), (packed - 32768).astype(jnp.int16), largest * (1.0 / LEVELS)


def decode(high, packed, scale):
    packed = packed.astype(jnp.int32) + 32768
    low = jnp.concatenate([(packed >> (4 * i)) & 15 for i in range(4)], axis=0)
    return (high.astype(jnp.int32) * 16 + low).astype(F32) * scale


def kernel(
    n,
    mask_ref,
    skip_ref,
    x_hbm,
    b_hbm,
    c_hbm,
    dt_hbm,
    ld_hbm,
    gain_hbm,
    w_ref,
    k_hbm,
    v_hbm,
    mixer_hbm,
    attended_hbm,
    mixer_ref,
    attended_ref,
    x_ref,
    b_ref,
    c_ref,
    dt_ref,
    ld_ref,
    gain_ref,
    kv,
    w_own,
    w_other,
    bt,
    gram,
    rows_run,
    cols_run,
    rows_adj,
    code,
    code_in,
    scale,
    scale_in,
    mixed_other,
    q_acc,
    q_all,
    bias,
    rows_bias,
    weights,
    top,
    total,
    acc,
    own,
    ld_sem,
    own_sem,
    kv_send,
    kv_recv,
    st_send,
    st_recv,
    sc_send,
    sc_recv,
    mx_send,
    mx_recv,
    wt_send,
    wt_recv,
    wt_own,
    mx_out,
    at_out,
    answer,
    lk_send,
    lk_recv,
    lq_send,
    lq_recv,
    an_send,
    an_recv,
):
    me = lax.axis_index("context")
    core = lax.axis_index("tensor")
    other = 1 - core
    length = x_ref.shape[0]
    half = length // 2
    chunks = x_ref.shape[1] // CHUNK
    per = CHUNK // HEAD_P
    pairs = CHUNK // 128
    q_cols = w_own.shape[2]
    has_left = me > 0
    has_right = me < n - 1
    helper = me == n - 2
    last = me == n - 1
    middle = has_left & has_right
    heads = q_cols // HEAD_DIM
    groups = kv.shape[2]
    members = heads // groups
    blocks = length // BLOCK

    barrier = pltpu.get_barrier_semaphore()
    pl.semaphore_signal(barrier, inc=1, device_id={"tensor": other}, device_id_type=MESH)

    @pl.when(has_left)
    def _():
        pl.semaphore_signal(barrier, inc=1, device_id={"context": me - 1}, device_id_type=MESH)

    @pl.when(has_right)
    def _():
        pl.semaphore_signal(barrier, inc=1, device_id={"context": me + 1}, device_id_type=MESH)

    loads = [
        pltpu.make_async_copy(src, dst, ld_sem.at[i])
        for i, (src, dst) in enumerate(
            (
                (ld_hbm, ld_ref),
                (dt_hbm, dt_ref),
                (b_hbm, b_ref),
                (c_hbm, c_ref),
                (x_hbm, x_ref),
                (gain_hbm, gain_ref),
            )
        )
    ]
    for load in loads:
        load.start()

    hbm = (k_hbm, v_hbm)

    def fixed_lanes(g):
        return pl.ds(g * HEAD_DIM, HEAD_DIM)

    def own_load(which, g):
        return pltpu.make_async_copy(hbm[which].at[:, fixed_lanes(g)], kv.at[which, 0, g], own_sem.at[which, g])

    for which in range(2):
        for g in range(groups):
            own_load(which, g).start()

    peers = 1 + has_left.astype(jnp.int32) + has_right.astype(jnp.int32)

    @pl.when(has_left)
    def _():
        pl.semaphore_wait(barrier, peers)

    def pass_own(which, g):
        return pltpu.make_async_remote_copy(
            src_ref=hbm[which].at[:, fixed_lanes(g)],
            dst_ref=kv.at[which, 1, g],
            send_sem=kv_send.at[which, 0, g],
            recv_sem=kv_recv.at[which, 1, g],
            device_id={"context": me + 1},
            device_id_type=MESH,
        )

    def pass_on(which, slot, g):
        return pltpu.make_async_remote_copy(
            src_ref=kv.at[which, slot, g],
            dst_ref=kv.at[which, slot + 1, g],
            send_sem=kv_send.at[which, slot, g],
            recv_sem=kv_recv.at[which, slot + 1, g],
            device_id={"context": me + 1},
            device_id_type=MESH,
        )

    def arrive(which, slot, g):
        pltpu.make_async_remote_copy(
            src_ref=kv.at[which, slot - 1, g],
            dst_ref=kv.at[which, slot, g],
            send_sem=kv_send.at[which, slot - 1, g],
            recv_sem=kv_recv.at[which, slot, g],
            device_id={"context": me - 1},
            device_id_type=MESH,
        ).wait_recv()

    lent = groups - 1

    def passes(g):
        return ~helper | (g != lent)

    def forward(which, slot, g):
        arrive(which, slot, g)

        @pl.when(passes(g))
        def _():
            pass_on(which, slot, g).start()

    def lend(which):
        return pltpu.make_async_remote_copy(
            src_ref=hbm[which].at[:, fixed_lanes(lent)],
            dst_ref=kv.at[which, n, lent],
            send_sem=lk_send.at[which],
            recv_sem=lk_recv.at[which],
            device_id={"context": me - 1},
            device_id_type=MESH,
        )

    def lend_query(member):
        return pltpu.make_async_remote_copy(
            src_ref=q_all.at[lent * members + member],
            dst_ref=q_all.at[heads + member],
            send_sem=lq_send.at[member],
            recv_sem=lq_recv.at[member],
            device_id={"context": me - 1},
            device_id_type=MESH,
        )

    def give_back(member):
        return pltpu.make_async_remote_copy(
            src_ref=answer.at[member],
            dst_ref=attended_ref.at[:, fixed_lanes(lent * members + member)],
            send_sem=an_send.at[member],
            recv_sem=an_recv.at[member],
            device_id={"context": me + 1},
            device_id_type=MESH,
        )

    def state_copies(j):
        return [
            pltpu.make_async_remote_copy(
                src_ref=src.at[j],
                dst_ref=dst.at[j],
                send_sem=send.at[j],
                recv_sem=recv.at[j],
                device_id={"context": me + 1},
                device_id_type=MESH,
            )
            for src, dst, send, recv in ((scale, scale_in, sc_send, sc_recv), (code, code_in, st_send, st_recv))
        ]

    def lanes_of(j):
        return pl.ds(pl.multiple_of(j * CHUNK, CHUNK), CHUNK)

    def mixed_copy(j):
        return pltpu.make_async_remote_copy(
            src_ref=mixer_ref.at[:, lanes_of(j)],
            dst_ref=mixed_other.at[j],
            send_sem=mx_send.at[j],
            recv_sem=mx_recv.at[j],
            device_id={"tensor": other},
            device_id_type=MESH,
        )

    def mixed_out(j):
        return pltpu.make_async_copy(mixer_ref.at[:, lanes_of(j)], mixer_hbm.at[:, lanes_of(j)], mx_out.at[j])

    def attended_out(g):
        lanes = pl.ds(pl.multiple_of(g * members * HEAD_DIM, HEAD_DIM), members * HEAD_DIM)
        return pltpu.make_async_copy(attended_ref.at[:, lanes], attended_hbm.at[:, lanes], at_out.at[g])

    def weight_out(j):
        return pltpu.make_async_remote_copy(
            src_ref=w_ref.at[lanes_of(j), pl.ds(pl.multiple_of(other * q_cols, CHUNK), q_cols)],
            dst_ref=w_other.at[j],
            send_sem=wt_send.at[j],
            recv_sem=wt_recv.at[j],
            device_id={"tensor": other},
            device_id_type=MESH,
        )

    def weight_in(j):
        return pltpu.make_async_copy(
            w_ref.at[lanes_of(j), pl.ds(pl.multiple_of(core * q_cols, CHUNK), q_cols)],
            w_own.at[j],
            wt_own.at[j],
        )

    def start_weights():
        @pl.loop(0, chunks)
        def _(j):
            weight_in(j).start()
            weight_out(j).start()

    @pl.when(has_left)
    def _():
        @pl.when(has_right)
        def _():
            for g in range(groups):

                @pl.when(passes(g))
                def _(g=g):
                    pass_own(0, g).start()

        @pl.when(last)
        def _():
            for which in range(2):
                lend(which).start()

        start_weights()

    row = lax.broadcasted_iota(jnp.int32, (length, length), 0)
    col = lax.broadcasted_iota(jnp.int32, (length, length), 1)
    same = (row // BLOCK) == (col // BLOCK)
    loads[0].wait()
    loads[1].wait()
    up_to = jnp.where((row <= col) & ((row // half) == (col // half)), 1.0, 0.0).astype(BF16)
    run = dot_left(ld_ref[...], up_to) * LOG2E
    ends = jnp.concatenate(
        [
            jnp.broadcast_to(run[:, half - 1 : half], (run.shape[0], half)),
            jnp.broadcast_to(run[:, length - 1 : length], (run.shape[0], half)),
        ],
        axis=1,
    )
    steps = dt_ref[...]
    grow = jnp.exp2(run)
    inject = jnp.exp2(ends - run) * steps
    adjusted = run - jnp.log(steps) * LOG2E
    for j in range(chunks):
        part = slice(j * per, (j + 1) * per)
        rows_run[j, 0:per, :] = run[part]
        rows_run[j, per : 2 * per, :] = grow[part]
        rows_run[j, 2 * per : 3 * per, :] = inject[part]
        rows_run[j, 3 * per : 4 * per, :] = inject[part]
        rows_adj[j] = adjusted[part]
    for j in range(chunks):
        cols_run[j] = jnp.transpose(rows_run[j])
    loads[2].wait()
    loads[3].wait()
    bt[...] = jnp.transpose(b_ref[...].astype(F32)).astype(BF16)
    for s in range(2):
        part = slice(s * half, (s + 1) * half)
        gram[s] = jnp.where(
            row[:half, :half] >= col[:half, :half],
            lax.dot_general(c_ref[part, :], b_ref[part, :], NT, preferred_element_type=F32),
            0.0,
        )
    first = lax.broadcasted_iota(jnp.int32, (1, 128), 1) < HEAD_P
    loads[4].wait()
    loads[5].wait()
    second = (me == 1) & has_right
    later = (me >= 2) & has_right
    stride = chunks // groups

    @pl.when(~has_left)
    def _():
        pl.semaphore_wait(barrier, peers)
        start_weights()

    def spread(table, at):
        return jnp.concatenate(
            [
                jnp.where(first, table[:, at + 2 * p : at + 2 * p + 1], table[:, at + 2 * p + 1 : at + 2 * p + 2])
                for p in range(pairs)
            ],
            axis=1,
        )

    def own_part(j, s):
        return own[2 * j + s]

    def send_state(j, entering):
        keep = spread(cols_run[j, length - 1 : length, :], per)
        high, packed, unit = encode(keep * entering + own_part(j, 1))
        code[j, 0:STATE, :] = high
        code[j, STATE : STATE + STATE // 4, :] = packed
        scale[j] = unit
        for copy in state_copies(j):
            copy.start()

    @pl.loop(0, chunks)
    def _(j):
        weighted = x_ref[:, lanes_of(j)].astype(F32) * spread(cols_run[j], 2 * per)

        def keep_part(s):
            own[2 * j + s] = dot_right(bt[:, s * half : (s + 1) * half], weighted[s * half : (s + 1) * half])

        keep_part(0)

        @pl.when(has_right)
        def _():
            keep_part(1)

        @pl.when(~has_left & has_right)
        def _():
            send_state(j, own_part(j, 0))

        for g in range(groups):

            @pl.when(later & (j == g * stride))
            def _(g=g):
                forward(0, 1, g)

    @pl.when(~has_left & has_right)
    def _():
        for g in range(groups):
            pass_own(0, g).start()
            pass_own(1, g).start()

    def inside(j):
        runs = cols_run[j]
        adj = rows_adj[j]
        for p in range(pairs):
            lanes = pl.ds(pl.multiple_of(j * CHUNK + p * 128, 128), 128)
            for s in range(2):
                part = slice(s * half, (s + 1) * half)
                x_own = x_ref[part, lanes]
                x_wide = x_own.astype(F32)
                pieces = []
                for m in range(2):
                    a = 2 * p + m
                    weight = gram[s] * jnp.exp2(jnp.minimum(runs[part, a : a + 1] - adj[a : a + 1, part], 0.0))
                    pieces.append(split(weight))
                both = jnp.concatenate(
                    [
                        jnp.where(first, x_wide, 0.0).astype(BF16),
                        jnp.where(first, 0.0, x_wide).astype(BF16),
                    ],
                    axis=0,
                )
                high, mid, low = (jnp.concatenate([pieces[0][i], pieces[1][i]], axis=1) for i in range(3))
                gain = jnp.where(first, skip_ref[j * per + 2 * p], skip_ref[j * per + 2 * p + 1])
                acc[2 * j + s, :, p * 128 : (p + 1) * 128] = (dot(high, both) + (dot(mid, both) + dot(low, both))) + gain * x_wide

    def table(owner, slot, at):
        for i in range(blocks):
            for m in range(blocks):
                seen = mask_ref[owner * blocks + i, (owner - slot) * blocks + m] == 1
                rows_bias[at, m, :, i * BLOCK : (i + 1) * BLOCK] = jnp.full(
                    (8, BLOCK), jnp.where(seen, 0.0, NEGATIVE), F32
                )

    def diagonal(at, which):
        rows = [jnp.broadcast_to(rows_bias[at, m, 0:1, :], (BLOCK, length)) for m in range(blocks)]
        bias[which] = jnp.where(row <= col, jnp.where(same, 0.0, jnp.concatenate(rows, axis=0)), NEGATIVE)

    for slot in range(n):

        @pl.when(slot <= me)
        def _(slot=slot):
            table(me, slot, slot)

    diagonal(0, 0)

    @pl.when(helper)
    def _():
        for slot in range(n):
            table(me + 1, slot, n + slot)
        diagonal(n, 1)

    total[...] = jnp.zeros_like(total)
    top[...] = jnp.full_like(top, NEGATIVE)

    @pl.when(later)
    def _():
        pass_own(1, 0).start()
        pass_own(1, 1).start()

    ahead = jnp.where(me >= 2, jnp.where(has_right, chunks - 3, chunks), 0)

    @pl.loop(0, ahead)
    def _(j):
        inside(j)

    def add_query(j):
        for t in range(0, q_cols, 512):
            q_acc[:, t : t + 512] = dot(mixer_ref[:, lanes_of(j)], w_own[j, :, t : t + 512])

    def add_other(j):
        mixed_copy(j).wait_recv()
        weight_out(j).wait_recv()
        for t in range(0, q_cols, 512):
            q_acc[:, t : t + 512] += dot(mixed_other[j], w_other[j, :, t : t + 512])

    @pl.when(~has_left)
    def _():
        code_in[...] = jnp.zeros_like(code_in)
        scale_in[...] = jnp.zeros_like(scale_in)

    lag = jnp.where(second, chunks, 0)

    def states_at(j):
        arrived = decode(code_in[j, 0:STATE, :], code_in[j, STATE : STATE + STATE // 4, :], scale_in[j])
        return arrived, spread(cols_run[j, half - 1 : half, :], per) * arrived + own_part(j, 0)

    def relay(j):
        @pl.when(has_left)
        def _():
            for copy in state_copies(j):
                copy.wait_recv()

        @pl.when(middle)
        def _():
            send_state(j, states_at(j)[1])

        for g in range(2, groups):

            @pl.when(later & (j == chunks - 1) & passes(g))
            def _(g=g):
                pass_own(1, g).start()

        @pl.when(later & (j == chunks - 1))
        def _():
            forward(0, 2, 0)

        @pl.when(j >= ahead)
        def _():
            inside(j)

    def mix(j):
        for g in range(groups):

            @pl.when(second & (j == g * stride))
            def _(g=g):
                forward(0, 1, g)
                pass_own(1, g).start()
                forward(1, 1, g)

        arrived, entering = states_at(j)
        runs = cols_run[j]
        for s in range(2):
            part = slice(s * half, (s + 1) * half)
            carried = dot_right(c_ref[part, :], arrived if s == 0 else entering)
            grown = spread(runs[part], per)
            for p in range(pairs):
                lanes = slice(p * 128, (p + 1) * 128)
                out_lanes = pl.ds(pl.multiple_of(j * CHUNK + p * 128, 128), 128)
                y = acc[2 * j + s, :, lanes] + carried[:, lanes] * grown[:, lanes]
                squares = y * y
                left = jnp.sum(jnp.where(first, squares, 0.0), axis=1, keepdims=True)
                right = jnp.sum(jnp.where(first, 0.0, squares), axis=1, keepdims=True)
                mean = jnp.where(first, left, right) * (1.0 / HEAD_P)
                mixer_ref[part, out_lanes] = (y * lax.rsqrt(mean + 1e-05) * gain_ref[:, out_lanes]).astype(BF16)
        mixed_copy(j).start()
        mixed_out(j).start()
        weight_in(j).wait()

        @pl.when(j == 0)
        def _():
            add_query(j)

        @pl.when(j >= 1)
        def _():
            mixed_copy(j - 1).wait_recv()
            weight_out(j - 1).wait_recv()
            for t in range(0, q_cols, 512):
                q_acc[:, t : t + 512] += dot(mixer_ref[:, lanes_of(j)], w_own[j, :, t : t + 512]) + dot(
                    mixed_other[j - 1], w_other[j - 1, :, t : t + 512]
                )

    @pl.loop(0, chunks + lag)
    def _(t):
        @pl.when(t < chunks)
        def _():
            relay(t)

        @pl.when(t >= lag)
        def _():
            mix(t - lag)

    add_other(chunks - 1)
    for h in range(heads):
        q_all[h] = q_acc[:, h * HEAD_DIM : (h + 1) * HEAD_DIM].astype(BF16)

    @pl.when(last)
    def _():
        for member in range(members):
            lend_query(member).start()

    for which in range(2):
        for g in range(groups):
            own_load(which, g).wait()
    unit_scale = HEAD_DIM ** (-0.5) * LOG2E

    def head_lanes(h):
        return pl.ds(pl.multiple_of(h * HEAD_DIM, HEAD_DIM), HEAD_DIM)

    span = BLOCK // 8

    def by_eight(table):
        return table.reshape(length // 8, 8, length)

    turn = 3

    @pl.loop(0, jnp.where(helper, groups + 1, jnp.where(last, groups - 1, groups)))
    def _(unit):
        lending = helper & (unit == turn)
        g = jnp.where(lending, lent, unit - (helper & (unit > turn)).astype(jnp.int32))
        base = jnp.where(lending, heads, g * members)
        end = jnp.where(lending, me + 1, me)

        def held(slot):
            return jnp.where(lending, jnp.where(slot == 0, n, slot - 1), slot)

        def scores_of(slot, member):
            keys = kv[0, held(slot), g]
            return by_eight(lax.dot_general(keys, q_all[base + member], NT, preferred_element_type=F32))

        def row_of(slot, m):
            return rows_bias[jnp.where(lending, n + slot, slot), m]

        def best_first():
            for member in range(members):
                h = base + member
                scores = scores_of(0, member) + by_eight(bias[lending.astype(jnp.int32)])
                top[h] = jnp.maximum(top[h], jnp.max(scores, axis=0))

        def weigh_first():
            for member in range(members):
                h = base + member
                scores = scores_of(0, member) + by_eight(bias[lending.astype(jnp.int32)])
                part = jnp.exp2((scores - top[h]) * unit_scale)
                total[h] += jnp.sum(part, axis=0)
                weights[0, member] = part.reshape(length, length).astype(BF16)

        def arrive_values(slot):
            @pl.when((last & (slot >= 1)) | (lending & (slot >= 2)))
            def _():
                arrive(1, held(slot), g)

        def weigh(slot):
            for member in range(members):
                h = base + member
                scores = scores_of(slot, member)
                summed = total[h]
                for m in range(blocks):
                    shift = top[h] - row_of(slot, m)
                    part = jnp.exp2((scores[m * span : (m + 1) * span] - shift) * unit_scale)
                    summed = summed + jnp.sum(part, axis=0)
                    weights[slot % 2, member, m * BLOCK : (m + 1) * BLOCK, :] = part.reshape(BLOCK, length).astype(BF16)
                total[h] = summed

        def attend(slot):
            values = jnp.transpose(kv[1, held(slot), g].astype(F32)).astype(BF16)
            for member in range(members):
                h = base + member
                acc[h] = jnp.where(slot == 0, 0.0, acc[h]) + dot(values, weights[slot % 2, member])

        @pl.when(later & (unit < jnp.where(helper, lent, groups)))
        def _():
            @pl.loop(jnp.where(unit == 0, 3, 2), me + 1)
            def _(slot):
                forward(0, slot, unit)

            @pl.loop(1, me + 1)
            def _(slot):
                forward(1, slot, unit)

        @pl.when(lending)
        def _():
            for which in range(2):
                lend(which).wait_recv()
            for member in range(members):
                lend_query(member).wait_recv()

        best_first()

        @pl.loop(1, end + 1)
        def _(slot):
            @pl.when(last | (lending & (slot >= 3)))
            def _():
                arrive(0, held(slot), g)

            for member in range(members):
                h = base + member
                scores = scores_of(slot, member)
                best = top[h]
                for m in range(blocks):
                    best = jnp.maximum(best, jnp.max(scores[m * span : (m + 1) * span], axis=0) + row_of(slot, m))
                top[h] = best

        for member in range(members):
            h = base + member
            top[h] = jnp.broadcast_to(jnp.max(top[h], axis=0, keepdims=True), top.shape[1:])
        weigh_first()

        @pl.loop(1, end + 1)
        def _(slot):
            arrive_values(slot - 1)
            weigh(slot)
            attend(slot - 1)

        arrive_values(end)
        attend(end)
        for member in range(members):
            h = base + member
            out = jnp.transpose(acc[h] / jnp.sum(total[h], axis=0, keepdims=True)).astype(BF16)

            @pl.when(lending)
            def _(member=member, out=out):
                answer[member] = out
                give_back(member).start()

            @pl.when(~lending)
            def _(h=h, out=out):
                attended_ref[:, head_lanes(h)] = out

        @pl.when(~lending)
        def _():
            attended_out(g).start()

    @pl.when(last)
    def _():
        for member in range(members):
            give_back(member).wait_recv()
        attended_out(lent).start()
        for which in range(2):
            lend(which).wait_send()
        for member in range(members):
            lend_query(member).wait_send()

    @pl.when(helper)
    def _():
        for member in range(members):
            give_back(member).wait_send()

    @pl.loop(0, groups)
    def _(g):
        attended_out(g).wait()

    @pl.loop(0, chunks)
    def _(j):
        mixed_copy(j).wait_send()
        mixed_out(j).wait()
        weight_out(j).wait_send()

        @pl.when(has_right)
        def _():
            for copy in state_copies(j):
                copy.wait_send()

    @pl.loop(0, n)
    def _(slot):
        @pl.when((slot <= me) & has_right)
        def _():
            for which in range(2):
                for g in range(groups):

                    @pl.when(passes(g))
                    def _(which=which, g=g):
                        pass_on(which, slot, g).wait_send()


def hand_on(mixer_ref, attended_ref, mixer_out, attended_out, held, loads, stores):
    parts = held.shape[1]
    rows = held.shape[2]
    refs = ((mixer_ref, mixer_out), (attended_ref, attended_out))

    def load(k, i):
        return pltpu.make_async_copy(refs[k][0].at[pl.ds(i * rows, rows)], held.at[k, i], loads.at[k, i])

    def store(k, i):
        return pltpu.make_async_copy(held.at[k, i], refs[k][1].at[pl.ds(i * rows, rows)], stores.at[k, i])

    every = [(k, i) for k in range(2) for i in range(parts)]
    for at in every:
        load(*at).start()
    for at in every:
        load(*at).wait()
        store(*at).start()
    for at in every:
        store(*at).wait()


def on_device(
    ssm_input,
    input_map,
    output_map,
    step_size,
    log_decay,
    skip_gain,
    norm_gain,
    query_weight,
    key_states,
    value_states,
    block_mask,
):
    n = lax.axis_size("context")
    length, channels = ssm_input.shape
    q_cols = query_weight.shape[1] // lax.axis_size("tensor")
    chunks = channels // CHUNK
    heads = q_cols // HEAD_DIM
    per = CHUNK // HEAD_P
    groups = key_states.shape[1] // HEAD_DIM
    smem = pl.BlockSpec(memory_space=pltpu.SMEM)
    hbm = pl.BlockSpec(memory_space=pltpu.HBM)
    far = pl.BlockSpec(memory_space=pl.ANY)
    dma = pltpu.SemaphoreType.DMA
    outs = (
        jax.ShapeDtypeStruct((length, channels), BF16),
        jax.ShapeDtypeStruct((length, q_cols), BF16),
    )
    coded = STATE + STATE // 4
    results = pl.pallas_call(
        functools.partial(kernel, n),
        out_shape=outs,
        in_specs=[smem, smem] + [hbm] * 9,
        out_specs=(hbm, hbm),
        scratch_shapes=[
            pltpu.VMEM((length, channels), BF16),
            pltpu.VMEM((length, q_cols), BF16),
            pltpu.VMEM((length, channels), BF16),
            pltpu.VMEM((length, STATE), BF16),
            pltpu.VMEM((length, STATE), BF16),
            pltpu.VMEM(step_size.shape, F32),
            pltpu.VMEM(log_decay.shape, F32),
            pltpu.VMEM((1, channels), F32),
            pltpu.VMEM((2, n + 1, groups, length, HEAD_DIM), BF16),
            pltpu.VMEM((chunks, CHUNK, q_cols), BF16),
            pltpu.VMEM((chunks, CHUNK, q_cols), BF16),
            pltpu.VMEM((STATE, length), BF16),
            pltpu.VMEM((2, length // 2, length // 2), F32),
            pltpu.VMEM((chunks, 4 * per, length), F32),
            pltpu.VMEM((chunks, length, 4 * per), F32),
            pltpu.VMEM((chunks, per, length), F32),
            pltpu.VMEM((chunks, coded, CHUNK), jnp.int16),
            pltpu.VMEM((chunks, coded, CHUNK), jnp.int16),
            pltpu.VMEM((chunks, 1, CHUNK), F32),
            pltpu.VMEM((chunks, 1, CHUNK), F32),
            pltpu.VMEM((chunks, length, CHUNK), BF16),
            pltpu.VMEM((length, q_cols), F32),
            pltpu.VMEM((heads + heads // groups, length, HEAD_DIM), BF16),
            pltpu.VMEM((2, length, length), F32),
            pltpu.VMEM((2 * n, length // BLOCK, 8, length), F32),
            pltpu.VMEM((2, heads // groups, length, length), BF16),
            pltpu.VMEM((heads + heads // groups, 8, length), F32),
            pltpu.VMEM((heads + heads // groups, 8, length), F32),
            pltpu.VMEM((max(heads + heads // groups, 2 * chunks), HEAD_DIM, length), F32),
            pltpu.VMEM((2 * chunks, STATE, CHUNK), F32),
            dma((6,)),
            dma((2, groups)),
            dma((2, n, groups)),
            dma((2, n + 1, groups)),
        ]
        + [dma((chunks,))] * 10
        + [dma((groups,)), pltpu.VMEM((heads // groups, length, HEAD_DIM), BF16), dma((2,)), dma((2,))]
        + [dma((heads // groups,))] * 4,
        compiler_params=pltpu.CompilerParams(
            collective_id=0, has_side_effects=True, vmem_limit_bytes=56 * 1024 * 1024
        ),
        name="mixer_attention",
    )(
        block_mask,
        skip_gain,
        ssm_input,
        input_map,
        output_map,
        step_size,
        log_decay,
        norm_gain.reshape(1, channels),
        query_weight,
        key_states,
        value_states,
    )
    return pl.pallas_call(
        hand_on,
        out_shape=outs,
        in_specs=[far, far],
        out_specs=[far, far],
        scratch_shapes=[pltpu.VMEM((2, 4, length // 4, channels), BF16), dma((2, 4)), dma((2, 4))],
        name="hand_on",
    )(*results)


def solution(mesh):
    return jax.shard_map(
        on_device,
        mesh=mesh,
        in_specs=(
            P(("dp", "context"), "tensor"),
            P(("dp", "context"), None),
            P(("dp", "context"), None),
            P("tensor", ("dp", "context")),
            P("tensor", ("dp", "context")),
            P("tensor"),
            P("tensor"),
            P("tensor", None),
            P(("dp", "context"), "tensor"),
            P(("dp", "context"), "tensor"),
            P("dp", None),
        ),
        out_specs=(P(("dp", "context"), "tensor"), P(("dp", "context"), "tensor")),
        check_vma=False,
    )
```
